32 devices in a mesh: dp: 8 (over y, x, core), tensor: 4 (over z).
Axes of the slice: x: 2, y: 2, z: 4, core: 2. Of those that a mesh axis runs over, the one named last changes fastest.
Arguments:
- tokens: bfloat16 [8192, 1536], P(('dp', 'tensor')), may hold values from -6 to 6
- segments: int32 [8, 1024], P('dp'), may hold values from -1 to 17, as said below
- granularity: int32 [8], P('dp'), may hold values from 1 to 4
- norm1_gain: float32 [1536], replicated, may hold values from 0.5 to 1.5
- norm2_gain: float32 [1536], replicated, may hold values from 0.5 to 1.5
- w_query: bfloat16 [1536, 1536], P(None, 'tensor'), may hold values from -0.15625 to 0.15625
- w_key: bfloat16 [1536, 1536], P(None, 'tensor'), may hold values from -0.15625 to 0.15625
- w_value: bfloat16 [1536, 1536], P(None, 'tensor'), may hold values from -0.15625 to 0.15625
- w_out: bfloat16 [1536, 1536], P('tensor'), may hold values from -0.625 to 0.625
- w_gate: bfloat16 [1536, 6144], P(None, 'tensor'), may hold values from -0.15625 to 0.15625
- w_up: bfloat16 [1536, 6144], P(None, 'tensor'), may hold values from -0.15625 to 0.15625
- w_down: bfloat16 [6144, 1536], P('tensor'), may hold values from -0.15625 to 0.15625
- cotangent: bfloat16 [8192, 1536], P(('dp', 'tensor')), may hold values from -6 to 6
Outputs:
- output: bfloat16 [8192, 1536], P(('dp', 'tensor'))
- grad_tokens: bfloat16 [8192, 1536], P(('dp', 'tensor'))
- grad_norm1: float32 [1536], replicated
- grad_norm2: float32 [1536], replicated
- grad_query: float32 [1536, 1536], P('dp', 'tensor')
- grad_key: float32 [1536, 1536], P('dp', 'tensor')
- grad_value: float32 [1536, 1536], P('dp', 'tensor')
- grad_out: float32 [1536, 1536], P('tensor', 'dp')
- grad_gate: float32 [1536, 6144], P('dp', 'tensor')
- grad_up: float32 [1536, 6144], P('dp', 'tensor')
- grad_down: float32 [6144, 1536], P('tensor', 'dp')
The draws below stay inside these ranges and needn't reach their ends.
Inputs may be any that keep to these rules, and one draw needn't show every extreme that they name: `segments`: in each packed sequence ids start at 0 and never fall, a document is a run of equal ids, every sequence holds exactly 18 documents, and the sequence ends in 1 to 128 padding tokens of id -1.
All inputs are finite; a program needn't handle non-finite values.
Results may differ from the reference program's by a relative error of at most 0.017.
Values may be sent and summed in bfloat16 or wider, within the bound.
A program may use at most 192 MiB of HBM per device.

```python
import jax
import jax.numpy as jnp
from jax import lax

D = 1536
HEADS = 12
HD = 128
FF = 6144
LEN = 1024
HQ = 1536
NSEQ = 8
TOKENS = 8192


def pick_bounds(key):
    usable = LEN - LEN // 8
    order = jax.random.permutation(key, usable - 1).astype(jnp.int32) + 1
    return order[:LEN // 64 + 1]


def draw_segments(key, part):
    key_bounds, key_pads = jax.random.split(key)
    bounds = jax.vmap(pick_bounds)(jax.random.split(key_bounds, NSEQ))
    positions = jnp.arange(LEN, dtype=jnp.int32)[None, :]
    marks = jnp.any(positions[:, :, None] == bounds[:, None, :], axis=-1)
    doc_ids = jnp.cumsum(marks.astype(jnp.int32), axis=1)
    pad_count = jax.random.randint(key_pads, (NSEQ, 1), 1, LEN // 8 + 1)
    return jnp.where(positions >= LEN - pad_count, -1, doc_ids).astype(jnp.int32)


def place_ends(array, stream_key, smallest, top_value):
    longest = array.shape.index(max(array.shape))
    spots = []
    for shift in (0, 1):
        where = [jax.random.randint(jax.random.fold_in(stream_key, axis), (), 0, length) for axis, length in enumerate(array.shape)]
        where[longest] = (where[longest] + shift) % array.shape[longest]
        spots.append(tuple(where))
    return array.at[spots[0]].set(smallest).at[spots[1]].set(top_value)


def steps_of(stream_key, dims, cuts, low, top_value):
    factor_of = 1.0
    for axis_at, shards_of in cuts:
        heights = jax.random.uniform(jax.random.fold_in(jax.random.fold_in(stream_key, 6), axis_at), (shards_of,), jnp.float32, low / len(cuts), top_value / len(cuts))
        factor_of = factor_of * jnp.repeat(jnp.exp(heights), dims[axis_at] // shards_of).reshape((-1,) + (1,) * (len(dims) - 1 - axis_at))
    return factor_of


def centred(rng, extent, width, reach, cuts=(), held_as=jnp.bfloat16):
    entries = jax.random.normal(rng, extent, jnp.float32) * width
    if len(cuts) > 0:
        entries = steps_of(rng, extent, cuts, -0.22, 0.18) * entries
    return jnp.clip(entries, min=-reach, max=reach).astype(held_as)


def setup_inputs(seed: int = 0) -> dict:
    seeds = jax.random.split(jax.random.key(seed), 14)
    tokens = centred(seeds[0], (TOKENS, D), 1.0, 6.0, ((0, 32),))
    segments = draw_segments(jax.random.fold_in(seeds[13], 71), 0)
    granularity = place_ends(jax.random.randint(seeds[2], (NSEQ,), 1, 5), jax.random.fold_in(seeds[2], 1), 1, 4).astype(jnp.int32)
    norm1_gain = jnp.clip(1.0 + 0.1 * jax.random.normal(seeds[3], (D,), jnp.float32), 0.5, 1.5)
    norm2_gain = jnp.clip(1.0 + 0.1 * jax.random.normal(seeds[4], (D,), jnp.float32), 0.5, 1.5)
    w_query = centred(seeds[5], (D, HQ), D ** -0.5, 0.15625, ((1, 4),))
    w_key = centred(seeds[6], (D, HQ), D ** -0.5, 0.15625, ((1, 4),))
    w_value = centred(seeds[7], (D, HQ), D ** -0.5, 0.15625, ((1, 4),))
    w_out = centred(seeds[8], (HQ, D), (HQ // 16) ** -0.5, 0.625, ((0, 4),))
    w_gate = centred(seeds[9], (D, FF), D ** -0.5, 0.15625, ((1, 4),))
    w_up = centred(seeds[10], (D, FF), D ** -0.5, 0.15625, ((1, 4),))
    w_down = centred(seeds[11], (FF, D), (FF // 4) ** -0.5, 0.15625, ((0, 4),))
    cotangent = centred(seeds[12], (TOKENS, D), 1.0, 6.0, ((0, 32),))
    return {"tokens": tokens, "segments": segments, "granularity": granularity, "norm1_gain": norm1_gain, "norm2_gain": norm2_gain, "w_query": w_query, "w_key": w_key, "w_value": w_value, "w_out": w_out, "w_gate": w_gate, "w_up": w_up, "w_down": w_down, "cotangent": cotangent}


EPS = 1e-06
NEG = -1e+30
HIGH = lax.Precision.HIGHEST

@jax.custom_vjp
def low(v):
    return lax.optimization_barrier(v.astype(jnp.bfloat16)).astype(jnp.float32)

@jax.custom_vjp
def low_back(v):
    return v

def low_keep(v):
    return (low(v), None)

def low_pass(kept, grad):
    return (grad,)

def back_keep(v):
    return (v, None)

def back_low(kept, grad):
    return (low(grad),)
low.defvjp(low_keep, low_pass)
low_back.defvjp(back_keep, back_low)

def matmul(left, right):
    return jnp.dot(left, right, precision=HIGH, preferred_element_type=jnp.float32)

def norm_rows(values, row_gain):
    factor = lax.rsqrt(lax.optimization_barrier(jnp.mean(values * values, axis=-1, keepdims=True)) + EPS)
    return values * factor * row_gain

def rope_tables(length, head_size):
    half_size = head_size // 2
    frequency = 10000.0 ** (-jnp.arange(half_size, dtype=jnp.float32) / half_size)
    angles = jnp.arange(length, dtype=jnp.float32)[:, None] * frequency[None, :]
    return (jnp.cos(angles)[:, None, :], jnp.sin(angles)[:, None, :])

def rotate(values, cosine, sine_table):
    half_size = values.shape[-1] // 2
    lower_half = values[..., :half_size]
    upper_half = values[..., half_size:]
    return jnp.concatenate([lower_half * cosine - upper_half * sine_table, upper_half * cosine + lower_half * sine_table], axis=-1)

def attend_sequence(inputs):
    queries, keys_all, values_all, seg_ids = inputs
    cosine, sine_table = rope_tables(LEN, HD)
    query_rot = low(rotate(queries, cosine, sine_table))
    key_rot = low(rotate(keys_all, cosine, sine_table))
    raw_scores = low_back(jnp.einsum('qhd,khd->hqk', query_rot, key_rot, precision=HIGH))
    query_pos = jnp.arange(LEN)[:, None]
    key_pos = jnp.arange(LEN)[None, :]
    allowed = (key_pos <= query_pos) & (seg_ids[:, None] == seg_ids[None, :])
    logits = jnp.where(allowed[None], raw_scores * HD ** (-0.5), NEG)
    row_max = lax.optimization_barrier(jnp.max(logits, axis=-1, keepdims=True))
    expo = jnp.exp(logits - row_max)
    probs = expo / lax.optimization_barrier(jnp.sum(expo, axis=-1, keepdims=True))
    return jnp.einsum('hqk,khd->qhd', low(probs), values_all, precision=HIGH)

def reference(tokens, segments, granularity, norm1_gain, norm2_gain, w_query, w_key, w_value, w_out, w_gate, w_up, w_down, cotangent):
    flat_ids = segments.reshape(TOKENS)
    token_width = jnp.repeat(FF // 8 * 2 ** (granularity - 1), LEN)
    unit_mask = (jnp.arange(FF)[None, :] < token_width[:, None]).astype(jnp.float32)

    def heads_view(matrix):
        return matrix.reshape(NSEQ, LEN, HEADS, HD)

    def forward(inputs_f, gain_one, gain_two, mat_q, mat_k, mat_v, mat_o, mat_g, mat_u, mat_d):
        normed_one = low(norm_rows(inputs_f, gain_one))
        query_f = low_back(matmul(normed_one, mat_q))
        key_f = low_back(matmul(normed_one, mat_k))
        value_f = low(low_back(matmul(normed_one, mat_v)))
        attended = lax.map(jax.checkpoint(attend_sequence), (heads_view(query_f), heads_view(key_f), heads_view(value_f), segments))
        attended_low = low(low_back(attended.reshape(TOKENS, HQ)))
        hidden_f = inputs_f + low_back(matmul(attended_low, mat_o))
        normed_two = low(norm_rows(hidden_f, gain_two))
        gate_f = low_back(matmul(normed_two, mat_g))
        up_f = low_back(matmul(normed_two, mat_u))
        inner_low = low(jax.nn.silu(gate_f) * up_f * unit_mask)
        return hidden_f + low_back(matmul(inner_low, mat_d))
    floats = (tokens.astype(jnp.float32), norm1_gain.astype(jnp.float32), norm2_gain.astype(jnp.float32), w_query.astype(jnp.float32), w_key.astype(jnp.float32), w_value.astype(jnp.float32), w_out.astype(jnp.float32), w_gate.astype(jnp.float32), w_up.astype(jnp.float32), w_down.astype(jnp.float32))
    result, pullback = jax.vjp(forward, *floats)
    cot_rows = cotangent.astype(jnp.float32) * (flat_ids >= 0).astype(jnp.float32)[:, None]
    grads = pullback(cot_rows)
    return (result.astype(jnp.bfloat16), grads[0].astype(jnp.bfloat16), grads[1], grads[2], grads[3], grads[4], grads[5], grads[6], grads[7], grads[8], grads[9])
```

```python
import functools

import jax
import jax.numpy as jnp
from jax import lax
from jax.experimental import pallas as pl
from jax.experimental.pallas import tpu as pltpu
from jax.sharding import PartitionSpec as P

HD = 128
FF = 6144
EPS = 1e-06
NEG = -1e30
BF = jnp.bfloat16
F32 = jnp.float32
QB = 256


def norm_factor(values):
    return lax.rsqrt(jnp.mean(values * values, axis=-1, keepdims=True) + EPS)


def norm_back(values, factor, row_gain, gradient):
    scaled = gradient * row_gain
    inner_mean = jnp.mean(scaled * values, axis=-1, keepdims=True)
    back_rows = factor * scaled - values * (factor * factor * factor) * inner_mean
    return (back_rows, jnp.sum(gradient * values * factor, axis=0))


def rope_tables(length, head_size):
    half_size = head_size // 2
    frequency = 10000.0 ** (-jnp.arange(half_size, dtype=F32) / half_size)
    angles = jnp.arange(length, dtype=F32)[:, None] * frequency[None, :]
    cosine, sine = jnp.cos(angles), jnp.sin(angles)
    return (jnp.concatenate([cosine, cosine], 1), jnp.concatenate([-sine, sine], 1))


def dot(left, right, dims=((1,), (0,))):
    return lax.dot_general(left, right, (dims, ((), ())), preferred_element_type=F32)


def attend_forward_body(q_ref, k_ref, v_ref, cos_ref, sin_ref, seg_col, seg_row, qr_ref, kr_ref, vb_ref, p_ref, o_ref):
    length = q_ref.shape[0]
    half = HD // 2
    cosine, sine = cos_ref[...], sin_ref[...]
    q, k = q_ref[...], k_ref[...]
    qr_ref[...] = (q * cosine + pltpu.roll(q, half, 1) * sine).astype(BF)
    kr_ref[...] = (k * cosine + pltpu.roll(k, half, 1) * sine).astype(BF)
    vb_ref[...] = v_ref[...].astype(BF)
    scale = HD ** (-0.5)
    for start in range(0, length, QB):
        extent = start + QB
        scores = dot(qr_ref[start:extent, :], kr_ref[:extent, :], ((1,), (1,)))
        rows = lax.broadcasted_iota(jnp.int32, (QB, extent), 0) + start
        cols = lax.broadcasted_iota(jnp.int32, (QB, extent), 1)
        allowed = (cols <= rows) & (seg_col[start:extent, :] == seg_row[:, :extent])
        logits = jnp.where(allowed, scores * scale, NEG)
        expo = jnp.exp(logits - jnp.max(logits, axis=-1, keepdims=True))
        weights = (expo / jnp.sum(expo, axis=-1, keepdims=True)).astype(BF)
        p_ref[0, start:extent, :extent] = weights
        o_ref[start:extent, :] = dot(weights, vb_ref[:extent, :]).astype(BF)


def attend_backward_body(q_ref, k_ref, v_ref, do_ref, p_ref, cos_ref, sin_ref, dq_ref, dk_ref, dv_ref, ds_ref):
    length = q_ref.shape[0]
    half = HD // 2
    scale = HD ** (-0.5)

    def unrope(grad, rows):
        return (grad * cos_ref[rows, :] - pltpu.roll(grad, half, 1) * sin_ref[rows, :]).astype(BF)

    for start in range(0, length, QB):
        extent = start + QB
        rows = slice(start, extent)
        grad_p = dot(do_ref[rows, :], v_ref[:extent, :], ((1,), (1,)))
        p = p_ref[0, rows, :extent].astype(F32)
        weighted = p * grad_p
        delta = jnp.sum(weighted, axis=-1, keepdims=True)
        ds_ref[rows, :extent] = ((weighted - p * delta) * scale).astype(BF)
        dq_ref[rows, :] = unrope(dot(ds_ref[rows, :extent], k_ref[:extent, :]), rows)
    for start in range(0, length, QB):
        rows = slice(start, start + QB)
        dk_ref[rows, :] = unrope(dot(ds_ref[start:, rows], q_ref[start:, :], ((0,), (0,))), rows)
        dv_ref[rows, :] = dot(p_ref[0, start:, rows], do_ref[start:, :], ((0,), (0,))).astype(BF)


def head_specs(length, width):
    head = pl.BlockSpec((length, HD), lambda h: (0, h))
    table = pl.BlockSpec((length, HD), lambda h: (0, 0))
    probs = pl.BlockSpec((1, length, length), lambda h: (h, 0, 0))
    array = jax.ShapeDtypeStruct((length, width), BF)
    return head, table, probs, array


def attend_forward(query, key, value, cosine, sine, seg_ids):
    length, width = query.shape
    heads = width // HD
    head, table, probs, array = head_specs(length, width)
    return pl.pallas_call(
        attend_forward_body,
        grid=(heads,),
        in_specs=[head, head, head, table, table,
                  pl.BlockSpec((length, 1), lambda h: (0, 0)), pl.BlockSpec((1, length), lambda h: (0, 0))],
        out_specs=[head, head, head, probs, head],
        out_shape=[array, array, array, jax.ShapeDtypeStruct((heads, length, length), BF), array],
        compiler_params=pltpu.CompilerParams(dimension_semantics=("arbitrary",)),
        cost_estimate=pl.CostEstimate(flops=4 * heads * length * length * HD, bytes_accessed=12 << 20, transcendentals=heads * length * length),
        name="attend_forward",
    )(query, key, value, cosine, sine, seg_ids.reshape(length, 1), seg_ids.reshape(1, length))


def attend_backward(query, key, value, grad, probs_low, cosine, sine):
    length, width = query.shape
    heads = width // HD
    head, table, probs, array = head_specs(length, width)
    return pl.pallas_call(
        attend_backward_body,
        grid=(heads,),
        in_specs=[head, head, head, head, probs, table, table],
        out_specs=[head, head, head],
        out_shape=[array, array, array],
        scratch_shapes=[pltpu.VMEM((length, length), BF)],
        compiler_params=pltpu.CompilerParams(dimension_semantics=("arbitrary",)),
        cost_estimate=pl.CostEstimate(flops=8 * heads * length * length * HD, bytes_accessed=12 << 20, transcendentals=0),
        name="attend_backward",
    )(query, key, value, grad, probs_low, cosine, sine)


def on_device(tokens, segments, granularity, norm1_gain, norm2_gain, w_query, w_key, w_value, w_out, w_gate, w_up, w_down, cotangent):
    own_rows, model = tokens.shape
    length = segments.shape[1]
    heads_width = w_query.shape[1]
    width_here = w_gate.shape[1]
    ranks = length // own_rows
    tensor_rank = lax.axis_index("tensor")
    seg_ids = segments.reshape(length)
    cosine, sine = rope_tables(length, HD)

    def own(array):
        return lax.dynamic_slice_in_dim(array, tensor_rank * own_rows, own_rows, 0)

    def scatter_rows(partial):
        return lax.psum_scatter(partial.astype(BF), "tensor", scatter_dimension=0, tiled=True).astype(F32)

    tokens_all = lax.all_gather(tokens, "tensor", axis=0, tiled=True)
    inputs_f = tokens_all.astype(F32)
    rows_one = (inputs_f * norm_factor(inputs_f) * norm1_gain).astype(BF)
    query, key, value = dot(rows_one, w_query), dot(rows_one, w_key), dot(rows_one, w_value)
    query_rot, key_rot, value_low, probs_low, attended = attend_forward(query, key, value, cosine, sine, seg_ids)
    attended_all = lax.all_gather(attended, "tensor", axis=0)
    w_out_all = lax.all_gather(w_out, "tensor", axis=0)
    hidden_f = inputs_f + lax.dot_general(
        attended_all, w_out_all, (((0, 2), (0, 1)), ((), ())), preferred_element_type=F32
    )
    rows_two = (hidden_f * norm_factor(hidden_f) * norm2_gain).astype(BF)
    gate_f = dot(rows_two, w_gate)
    up_f = dot(rows_two, w_up)
    unit_ids = tensor_rank * width_here + jnp.arange(width_here)
    unit_mask = unit_ids[None, :] < (FF // 8 * 2 ** (granularity - 1))[:, None]
    sigma = jax.nn.sigmoid(gate_f)
    activated = jnp.where(unit_mask, gate_f * sigma, 0.0)
    inner_low = (activated * up_f).astype(BF)
    hidden_own = own(hidden_f)
    output = (hidden_own + scatter_rows(dot(inner_low, w_down))).astype(BF)
    cotangent_all = lax.all_gather(cotangent, "tensor", axis=0, tiled=True)
    grad_rows = jnp.where((seg_ids >= 0)[:, None], cotangent_all, 0)
    grad_inner = dot(grad_rows, w_down, ((1,), (1,)))
    grad_gate_low = jnp.where(unit_mask, grad_inner * up_f * sigma * (1.0 + gate_f * (1.0 - sigma)), 0.0).astype(BF)
    grad_up_low = (grad_inner * activated).astype(BF)
    grad_normed_two = scatter_rows(dot(grad_gate_low, w_gate, ((1,), (1,))) + dot(grad_up_low, w_up, ((1,), (1,))))
    grad_gate = dot(rows_two, grad_gate_low, ((0,), (0,))).astype(BF)
    grad_up = dot(rows_two, grad_up_low, ((0,), (0,))).astype(BF)
    grad_down_t = dot(grad_rows, inner_low, ((0,), (0,))).astype(BF)

    def reduce_dp(partial):
        return lax.psum_scatter(partial, "dp", scatter_dimension=0, tiled=True)

    back_two, gain_two = norm_back(hidden_own, norm_factor(hidden_own), norm2_gain, grad_normed_two)
    grad_hidden = own(grad_rows).astype(F32) + back_two
    grad_hidden_low = grad_hidden.astype(BF)
    grad_attended_own = lax.dot_general(
        w_out_all, grad_hidden_low, (((2,), (1,)), ((), ())), preferred_element_type=F32
    ).astype(BF)
    grad_attended_own = jnp.transpose(grad_attended_own, (0, 2, 1))
    grad_attended = lax.all_to_all(grad_attended_own, "tensor", 0, 0).reshape(length, heads_width)
    attended_own = lax.dynamic_slice_in_dim(attended_all, tensor_rank * own_rows, own_rows, 1)
    grad_out_part = jnp.stack([dot(attended_own[r], grad_hidden_low, ((0,), (0,))) for r in range(ranks)]).astype(BF)
    grad_q, grad_k, grad_v = attend_backward(query_rot, key_rot, value_low, grad_attended, probs_low, cosine, sine)
    grad_normed_one = scatter_rows(
        dot(grad_q, w_query, ((1,), (1,))) + dot(grad_k, w_key, ((1,), (1,))) + dot(grad_v, w_value, ((1,), (1,)))
    )
    grads_qkv = reduce_dp(jnp.concatenate([dot(rows_one, g, ((0,), (0,))).astype(BF) for g in (grad_q, grad_k, grad_v)], axis=1)).astype(F32)
    inputs_own = tokens.astype(F32)
    back_one, gain_one = norm_back(inputs_own, norm_factor(inputs_own), norm1_gain, grad_normed_one)
    grad_tokens = (grad_hidden + back_one).astype(BF)
    gain_one, gain_two = lax.psum((gain_one, gain_two), ("dp", "tensor"))
    grad_out = lax.psum_scatter(grad_out_part, "dp", scatter_dimension=2, tiled=True)
    grad_out = lax.psum_scatter(grad_out, "tensor", scatter_dimension=0, tiled=True)[0].astype(F32)
    return (
        output,
        grad_tokens,
        gain_one,
        gain_two,
        grads_qkv[:, :heads_width],
        grads_qkv[:, heads_width : 2 * heads_width],
        grads_qkv[:, 2 * heads_width :],
        grad_out,
        reduce_dp(grad_gate).astype(F32),
        reduce_dp(grad_up).astype(F32),
        reduce_dp(grad_down_t).astype(F32).T,
    )


def solution(mesh):
    in_specs = (
        P(("dp", "tensor"), None), P("dp", None), P("dp"), P(), P(),
        P(None, "tensor"), P(None, "tensor"), P(None, "tensor"), P("tensor", None),
        P(None, "tensor"), P(None, "tensor"), P("tensor", None), P(("dp", "tensor"), None),
    )
    out_specs = (
        P(("dp", "tensor"), None), P(("dp", "tensor"), None), P(), P(),
        P("dp", "tensor"), P("dp", "tensor"), P("dp", "tensor"), P("tensor", "dp"),
        P("dp", "tensor"), P("dp", "tensor"), P("tensor", "dp"),
    )
    return jax.shard_map(on_device, mesh=mesh, in_specs=in_specs, out_specs=out_specs, check_vma=False)
```

```python
import functools

import jax
import jax.numpy as jnp
import numpy as np
from jax import lax
from jax.experimental import pallas as pl
from jax.experimental.pallas import tpu as pltpu
from jax.sharding import PartitionSpec as P

HD = 128
FF = 6144
EPS = 1e-06
NEG = -1e30
BF = jnp.bfloat16
F32 = jnp.float32
QB = 256


def norm_factor(values):
    return lax.rsqrt(jnp.mean(values * values, axis=-1, keepdims=True) + EPS)


def norm_back(values, factor, row_gain, gradient):
    scaled = gradient * row_gain
    inner_mean = jnp.mean(scaled * values, axis=-1, keepdims=True)
    back_rows = factor * scaled - values * (factor * factor * factor) * inner_mean
    return (back_rows, jnp.sum(gradient * values * factor, axis=0))


def dot(left, right, dims=((1,), (0,))):
    return lax.dot_general(left, right, (dims, ((), ())), preferred_element_type=F32)


MESH = pl.DeviceIdType.MESH
ANY = pl.BlockSpec(memory_space=pl.ANY)
VM = pl.BlockSpec(memory_space=pltpu.VMEM)
DMA = pltpu.SemaphoreType.DMA
RANKS = 4


def across(rank, k):
    if k == 3:
        return 3 - rank
    if k == 1:
        return rank + 1 - 2 * lax.rem(rank, 2)
    if k == 2:
        return rank + 2 - 4 * lax.div(rank, 2)
    return rank


def flip(index, bit):
    step = 2**bit
    return index + step - 2 * step * lax.rem(lax.div(index, step), 2)


def inner_plane(rank):
    return (rank == 1) | (rank == 2)


def greet(peers):
    barrier = pltpu.get_barrier_semaphore()
    for peer in peers:
        pl.semaphore_signal(barrier, inc=1, device_id=peer, device_id_type=MESH)
    pl.semaphore_wait(barrier, len(peers))


def line_peers(rank):
    return [{"tensor": across(rank, k)} for k in (1, 2, 3)]


class LineGather:
    def __init__(self, rank, view, pieces, send_sems, recv_sems):
        self.rank, self.view, self.pieces = rank, view, pieces
        self.send_sems, self.recv_sems = send_sems, recv_sems
        self.inner = inner_plane(rank)

    @staticmethod
    def sems(pieces):
        return [DMA((4, pieces)), DMA((RANKS, pieces))]

    def copy(self, source, piece, k, slot):
        return pltpu.make_async_remote_copy(
            src_ref=self.view(source, piece), dst_ref=self.view(source, piece),
            send_sem=self.send_sems.at[slot, piece], recv_sem=self.recv_sems.at[source, piece],
            device_id={"tensor": across(self.rank, k)}, device_id_type=MESH,
        )

    def start(self, piece):
        self.copy(self.rank, piece, 2, 0).start()
        self.copy(self.rank, piece, 1, 1).start()
        pl.when(self.inner)(lambda: self.copy(self.rank, piece, 3, 2).start())

    def arrive(self, k, piece):
        source = across(self.rank, k)
        self.copy(source, piece, 1, 3).wait_recv()
        if k == 2:
            pl.when(self.inner)(lambda: self.copy(source, piece, 1, 3).start())

    def finish(self):
        for piece in range(self.pieces):
            self.copy(self.rank, piece, 2, 0).wait_send()
            self.copy(self.rank, piece, 1, 1).wait_send()

        @pl.when(self.inner)
        def _():
            for piece in range(self.pieces):
                self.copy(self.rank, piece, 3, 2).wait_send()
                self.copy(across(self.rank, 2), piece, 1, 3).wait_send()


def local(source, target, sem):
    return pltpu.make_async_copy(source, target, sem)


def rope_numpy(length):
    half = HD // 2
    frequency = np.float32(10000.0) ** (-np.arange(half, dtype=np.float32) / np.float32(half))
    angles = np.arange(length, dtype=np.float32)[:, None] * frequency[None, :]
    cosine, sine = np.cos(angles), np.sin(angles)
    return (np.concatenate([cosine, cosine], 1), np.concatenate([-sine, sine], 1))


def input_body(dp, tok, cot, seg, wo, wq, wk, wv, gain, cosine, sine,
               x_out, a1_out, q_out, k_out, v_out, wo_out, cot_out,
               xs, a1s, qkv, ws, wos, cots, x_ss, x_rs, z_ss, z_rs, d_ss, d_rs, c_ss, l_sem):
    rank, group = lax.axis_index("tensor"), lax.axis_index("dp")
    rows = tok.shape[0]
    half_rows = rows // 2
    mates = dp // 2
    partner = flip(group, 0)
    parity = lax.rem(group, 2)
    pair = lax.div(group, 2)

    def mate(step):
        return lax.rem(pair + step, mates) * 2 + parity

    first = [local(wo.at[group], wos.at[rank, group], l_sem.at[0]), local(tok, xs.at[rank], l_sem.at[1]), local(cot, cots, l_sem.at[2])]
    weights = [local(w, ws.at[i], l_sem.at[3 + i]) for i, w in enumerate((wq, wk, wv))]
    for c in first + weights:
        c.start()
    greet(line_peers(rank) + [{"dp": partner}] + [{"dp": mate(s)} for s in range(1, mates)])
    out_gather = LineGather(rank, lambda s, p: wos.at[s, group], 1, z_ss, z_rs)
    first[0].wait()
    out_gather.start(0)
    gather = LineGather(rank, lambda s, p: xs.at[s, pl.ds(p * half_rows, half_rows)], 2, x_ss, x_rs)
    first[1].wait()
    gather.start(0)
    gather.start(1)
    first[2].wait()
    cots[...] = jnp.where(seg[...] >= 0, cots[...], jnp.zeros_like(cots))
    for w in weights:
        w.wait()

    def chunk(source):
        x = xs[source].astype(F32)
        a1s[source] = (x * norm_factor(x) * gain[...]).astype(BF)
        where = pl.ds(pl.multiple_of(source * rows, rows), rows)
        for i in range(3):
            product = dot(a1s[source], ws[i])
            for h in range(product.shape[1] // HD):
                head = product[:, h * HD : (h + 1) * HD]
                if i < 2:
                    head = head * cosine[where, :] + pltpu.roll(head, HD // 2, 1) * sine[where, :]
                qkv[i, where, h * HD : (h + 1) * HD] = head.astype(BF)

    chunk(rank)
    for k in (1, 2, 3):
        out_gather.arrive(k, 0)

    def mate_copy(step):
        return pltpu.make_async_remote_copy(
            src_ref=wos.at[:, group], dst_ref=wos.at[:, group], send_sem=d_ss.at[step], recv_sem=d_rs.at[group],
            device_id={"dp": mate(step)}, device_id_type=MESH)

    def mate_arrival(step):
        piece = mate(step)
        return pltpu.make_async_remote_copy(
            src_ref=wos.at[:, piece], dst_ref=wos.at[:, piece], send_sem=d_ss.at[step], recv_sem=d_rs.at[piece],
            device_id={"dp": piece}, device_id_type=MESH)

    def core_copy(step, owner):
        piece = lax.rem(pair + step, mates) * 2 + owner
        return pltpu.make_async_remote_copy(
            src_ref=wos.at[:, piece], dst_ref=wos.at[:, piece], send_sem=c_ss.at[step], recv_sem=d_rs.at[piece],
            device_id={"dp": partner}, device_id_type=MESH)

    for step in range(1, mates):
        mate_copy(step).start()
    core_copy(0, parity).start()
    for piece in range(2):
        gather.arrive(1, piece)
        gather.arrive(2, piece)
    chunk(across(rank, 1))
    chunk(across(rank, 2))
    for step in range(1, mates):
        mate_arrival(step).wait_recv()
        core_copy(step, parity).start()
    for piece in range(2):
        gather.arrive(3, piece)
    chunk(across(rank, 3))
    for step in range(mates):
        core_copy(step, 1 - parity).wait_recv()
    gather.finish()
    out_gather.finish()
    for step in range(1, mates):
        mate_copy(step).wait_send()
    for step in range(mates):
        core_copy(step, parity).wait_send()
    last = [local(xs, x_out, l_sem.at[0]), local(a1s, a1_out, l_sem.at[1]), local(wos, wo_out, l_sem.at[2]),
            local(qkv.at[0], q_out, l_sem.at[3]), local(qkv.at[1], k_out, l_sem.at[4]), local(qkv.at[2], v_out, l_sem.at[5]),
            local(cots, cot_out, l_sem.at[6])]
    for c in last:
        c.start()
    for c in last:
        c.wait()


def input_kernel(dp, tokens, cotangent, seg_own, w_out, w_query, w_key, w_value, gain, cosine, sine):
    rows, model = tokens.shape
    width = w_query.shape[1]
    length = RANKS * rows
    part = w_out.shape[0] // dp
    mates = dp // 2
    shard = jax.ShapeDtypeStruct((RANKS, rows, model), BF)
    heads = jax.ShapeDtypeStruct((length, width), BF)
    outs = pl.pallas_call(
        functools.partial(input_body, dp),
        in_specs=[ANY, ANY, VM, ANY, ANY, ANY, ANY, VM, VM, VM],
        out_specs=[ANY] * 7,
        out_shape=[shard, shard, heads, heads, heads, jax.ShapeDtypeStruct((RANKS, dp, part, model), BF),
                   jax.ShapeDtypeStruct((rows, model), BF)],
        scratch_shapes=[
            pltpu.VMEM((RANKS, rows, model), BF), pltpu.VMEM((RANKS, rows, model), BF), pltpu.VMEM((3, length, width), BF),
            pltpu.VMEM((3, model, width), BF), pltpu.VMEM((RANKS, dp, part, model), BF), pltpu.VMEM((rows, model), BF),
            *LineGather.sems(2), *LineGather.sems(1),
            DMA((mates,)), DMA((dp,)), DMA((mates,)), DMA((7,)),
        ],
        compiler_params=pltpu.CompilerParams(collective_id=1, has_side_effects=True, vmem_limit_bytes=56 << 20),
        name="input_gather",
    )(tokens, cotangent, seg_own, w_out.reshape(dp, part, model), w_query, w_key, w_value, gain, cosine, sine)
    x_all, a1_all, query, key, value, w_out_all, cot_own = outs
    return x_all, a1_all, query, key, value, w_out_all.reshape(RANKS, dp * part, model), cot_own


def attend_body(q, k, v, cot, x_all, wo_all, seg_col, seg_row, gain,
                p_out, dy_out, a2_out, h_out, ob_out,
                qkv, ps, dys, obs, xs, wos, hs, a2s, y_ss, y_rs, o_ss, o_rs, l_sem):
    rank = lax.axis_index("tensor")
    heads = p_out.shape[0]
    length = q.shape[0]
    rows = cot.shape[0]
    half_rows = rows // 2
    scale = HD ** (-0.5)
    loads = [local(cot, dys.at[rank], l_sem.at[0])]
    loads += [local(t, qkv.at[i], l_sem.at[1 + i]) for i, t in enumerate((q, k, v))]
    late = [local(x_all, xs, l_sem.at[4]), local(wo_all, wos, l_sem.at[5])]
    for c in loads + late:
        c.start()
    greet(line_peers(rank))
    grads = LineGather(rank, lambda s, p: dys.at[s, pl.ds(p * half_rows, half_rows)], 2, y_ss, y_rs)
    attended = LineGather(rank, lambda s, p: obs.at[s, :, pl.ds(pl.multiple_of(p * HD, HD), HD)], heads, o_ss, o_rs)
    loads[0].wait()
    grads.start(0)
    grads.start(1)
    for c in loads[1:]:
        c.wait()

    def head(h, carry):
        cols = pl.ds(pl.multiple_of(h * HD, HD), HD)
        for start in range(0, length, QB):
            extent = start + QB
            scores = dot(qkv[0, start:extent, cols], qkv[1, :extent, cols], ((1,), (1,)))
            row_ids = lax.broadcasted_iota(jnp.int32, (QB, extent), 0) + start
            col_ids = lax.broadcasted_iota(jnp.int32, (QB, extent), 1)
            allowed = (col_ids <= row_ids) & (seg_col[start:extent, :] == seg_row[:, :extent])
            logits = jnp.where(allowed, scores * scale, NEG)
            expo = jnp.exp(logits - jnp.max(logits, axis=-1, keepdims=True))
            probs = (expo * (1.0 / jnp.sum(expo, axis=-1, keepdims=True))).astype(BF)
            ps[h, start:extent, :extent] = probs
            obs[rank, start:extent, cols] = dot(probs, qkv[2, :extent, cols]).astype(BF)
        attended.start(h)
        return carry

    lax.fori_loop(0, heads, head, 0)
    keep = local(ps, p_out, l_sem.at[6])
    keep.start()
    for c in late:
        c.wait()

    def add(source, first=False, last=False):
        def block(b, carry):
            part = dot(obs[source, pl.ds(pl.multiple_of(b * rows, rows), rows), :], wos[source])
            total = part + (xs[b].astype(F32) if first else hs[b])
            hs[b] = total
            if last:
                a2s[b] = (total * norm_factor(total) * gain[...]).astype(BF)
            return carry

        lax.fori_loop(0, RANKS, block, 0)

    add(rank, first=True)
    for piece in range(2):
        grads.arrive(2, piece)
    for piece in range(heads):
        attended.arrive(2, piece)
    for piece in range(heads):
        attended.arrive(1, piece)
    add(across(rank, 2))
    add(across(rank, 1))
    for piece in range(2):
        grads.arrive(1, piece)
        grads.arrive(3, piece)
    dy_done = local(dys, dy_out, l_sem.at[0])
    dy_done.start()
    for piece in range(heads):
        attended.arrive(3, piece)
    add(across(rank, 3), last=True)
    last = [local(a2s, a2_out, l_sem.at[1]), local(hs.at[rank], h_out, l_sem.at[2]),
            local(obs.at[:, pl.ds(pl.multiple_of(rank * rows, rows), rows)], ob_out, l_sem.at[3])]
    for c in last:
        c.start()
    grads.finish()
    attended.finish()
    for c in last + [keep, dy_done]:
        c.wait()


def attend_kernel(query, key, value, cot_own, x_all, w_out_all, seg_ids, gain):
    length, width = query.shape
    heads = width // HD
    rows, model = cot_own.shape
    shard = (RANKS, rows, model)
    return pl.pallas_call(
        attend_body,
        in_specs=[ANY] * 6 + [VM] * 3,
        out_specs=[ANY] * 5,
        out_shape=[jax.ShapeDtypeStruct((heads, length, length), BF), jax.ShapeDtypeStruct(shard, BF), jax.ShapeDtypeStruct(shard, BF),
                   jax.ShapeDtypeStruct((rows, model), F32), jax.ShapeDtypeStruct((RANKS, rows, width), BF)],
        scratch_shapes=[
            pltpu.VMEM((3, length, width), BF), pltpu.VMEM((heads, length, length), BF), pltpu.VMEM(shard, BF),
            pltpu.VMEM((RANKS, length, width), BF), pltpu.VMEM(shard, BF), pltpu.VMEM((RANKS, width, model), BF),
            pltpu.VMEM(shard, F32), pltpu.VMEM(shard, BF),
            *LineGather.sems(2), *LineGather.sems(heads), DMA((7,)),
        ],
        compiler_params=pltpu.CompilerParams(collective_id=2, has_side_effects=True, vmem_limit_bytes=60 << 20),
        name="attend_gather",
    )(query, key, value, cot_own, x_all, w_out_all, seg_ids.reshape(length, 1), seg_ids.reshape(1, length), gain)


def attend_backward_body(q_ref, k_ref, v_ref, do_ref, p_ref, cos_ref, sin_ref, dq_ref, dk_ref, dv_ref, ds_ref):
    length = q_ref.shape[0]
    half = HD // 2
    scale = HD ** (-0.5)

    def unrope(grad, rows):
        return (grad * cos_ref[rows, :] - pltpu.roll(grad, half, 1) * sin_ref[rows, :]).astype(BF)

    for start in range(0, length, QB):
        extent = start + QB
        rows = slice(start, extent)
        grad_p = dot(do_ref[rows, :], v_ref[:extent, :], ((1,), (1,)))
        p = p_ref[0, rows, :extent].astype(F32)
        weighted = p * grad_p
        delta = jnp.sum(weighted, axis=-1, keepdims=True)
        ds_ref[rows, :extent] = ((weighted - p * delta) * scale).astype(BF)
        dq_ref[rows, :] = unrope(dot(ds_ref[rows, :extent], k_ref[:extent, :]), rows)
    for start in range(0, length, QB):
        rows = slice(start, start + QB)
        dk_ref[rows, :] = unrope(dot(ds_ref[start:, rows], q_ref[start:, :], ((0,), (0,))), rows)
        dv_ref[rows, :] = dot(p_ref[0, start:, rows], do_ref[start:, :], ((0,), (0,))).astype(BF)


def head_specs(length, width):
    head = pl.BlockSpec((length, HD), lambda h: (0, h))
    table = pl.BlockSpec((length, HD), lambda h: (0, 0))
    probs = pl.BlockSpec((1, length, length), lambda h: (h, 0, 0))
    array = jax.ShapeDtypeStruct((length, width), BF)
    return head, table, probs, array


def attend_backward(query, key, value, grad, probs_low, cosine, sine):
    length, width = query.shape
    heads = width // HD
    head, table, probs, array = head_specs(length, width)
    return pl.pallas_call(
        attend_backward_body,
        grid=(heads,),
        in_specs=[head, head, head, head, probs, table, table],
        out_specs=[head, head, head],
        out_shape=[array, array, array],
        scratch_shapes=[pltpu.VMEM((length, length), BF)],
        compiler_params=pltpu.CompilerParams(dimension_semantics=("arbitrary",)),
        cost_estimate=pl.CostEstimate(flops=8 * heads * length * length * HD, bytes_accessed=12 << 20, transcendentals=0),
        name="attend_backward",
    )(query, key, value, grad, probs_low, cosine, sine)


def on_device(tokens, segments, granularity, norm1_gain, norm2_gain, w_query, w_key, w_value, w_out, w_gate, w_up, w_down, cotangent):
    own_rows, model = tokens.shape
    length = segments.shape[1]
    heads_width = w_query.shape[1]
    width_here = w_gate.shape[1]
    ranks = length // own_rows
    tensor_rank = lax.axis_index("tensor")
    seg_ids = segments.reshape(length)
    cosine, sine = (jnp.asarray(t) for t in rope_numpy(length))
    dp = lax.axis_size("dp")
    seg_own = lax.dynamic_slice_in_dim(seg_ids, tensor_rank * own_rows, own_rows, 0).reshape(own_rows, 1)

    def scatter_rows(partial):
        return lax.psum_scatter(partial.astype(BF), "tensor", scatter_dimension=0, tiled=True).astype(F32)

    x_all, a1_all, query_rot, key_rot, value_low, w_out_all, cot_own = input_kernel(
        dp, tokens, cotangent, seg_own, w_out, w_query, w_key, w_value, norm1_gain.reshape(1, model), cosine, sine
    )
    probs_low, grad_rows, rows_two, hidden_own, attended_own = attend_kernel(
        query_rot, key_rot, value_low, cot_own, x_all, w_out_all, seg_ids, norm2_gain.reshape(1, model)
    )
    rows_one = a1_all.reshape(length, model)
    rows_two = rows_two.reshape(length, model)
    grad_rows = grad_rows.reshape(length, model)
    gate_f = dot(rows_two, w_gate)
    up_f = dot(rows_two, w_up)
    unit_ids = tensor_rank * width_here + jnp.arange(width_here)
    unit_mask = unit_ids[None, :] < (FF // 8 * 2 ** (granularity - 1))[:, None]
    sigma = jax.nn.sigmoid(gate_f)
    activated = jnp.where(unit_mask, gate_f * sigma, 0.0)
    inner_low = (activated * up_f).astype(BF)
    output = (hidden_own + scatter_rows(dot(inner_low, w_down))).astype(BF)
    grad_inner = dot(grad_rows, w_down, ((1,), (1,)))
    grad_gate_low = jnp.where(unit_mask, grad_inner * up_f * sigma * (1.0 + gate_f * (1.0 - sigma)), 0.0).astype(BF)
    grad_up_low = (grad_inner * activated).astype(BF)
    grad_normed_two = scatter_rows(dot(grad_gate_low, w_gate, ((1,), (1,))) + dot(grad_up_low, w_up, ((1,), (1,))))
    grad_gate = dot(rows_two, grad_gate_low, ((0,), (0,))).astype(BF)
    grad_up = dot(rows_two, grad_up_low, ((0,), (0,))).astype(BF)
    grad_down_t = dot(grad_rows, inner_low, ((0,), (0,))).astype(BF)

    def reduce_dp(partial):
        return lax.psum_scatter(partial, "dp", scatter_dimension=0, tiled=True)

    back_two, gain_two = norm_back(hidden_own, norm_factor(hidden_own), norm2_gain, grad_normed_two)
    grad_hidden = cot_own.astype(F32) + back_two
    grad_hidden_low = grad_hidden.astype(BF)
    grad_attended_own = lax.dot_general(
        w_out_all, grad_hidden_low, (((2,), (1,)), ((), ())), preferred_element_type=F32
    ).astype(BF)
    grad_attended_own = jnp.transpose(grad_attended_own, (0, 2, 1))
    grad_attended = lax.all_to_all(grad_attended_own, "tensor", 0, 0).reshape(length, heads_width)
    grad_out_part = jnp.stack([dot(attended_own[r], grad_hidden_low, ((0,), (0,))) for r in range(ranks)]).astype(BF)
    grad_q, grad_k, grad_v = attend_backward(query_rot, key_rot, value_low, grad_attended, probs_low, cosine, sine)
    grad_normed_one = scatter_rows(
        dot(grad_q, w_query, ((1,), (1,))) + dot(grad_k, w_key, ((1,), (1,))) + dot(grad_v, w_value, ((1,), (1,)))
    )
    grads_qkv = reduce_dp(jnp.concatenate([dot(rows_one, g, ((0,), (0,))).astype(BF) for g in (grad_q, grad_k, grad_v)], axis=1)).astype(F32)
    inputs_own = tokens.astype(F32)
    back_one, gain_one = norm_back(inputs_own, norm_factor(inputs_own), norm1_gain, grad_normed_one)
    grad_tokens = (grad_hidden + back_one).astype(BF)
    gain_one, gain_two = lax.psum((gain_one, gain_two), ("dp", "tensor"))
    grad_out = lax.psum_scatter(grad_out_part, "dp", scatter_dimension=2, tiled=True)
    grad_out = lax.psum_scatter(grad_out, "tensor", scatter_dimension=0, tiled=True)[0].astype(F32)
    return (
        output,
        grad_tokens,
        gain_one,
        gain_two,
        grads_qkv[:, :heads_width],
        grads_qkv[:, heads_width : 2 * heads_width],
        grads_qkv[:, 2 * heads_width :],
        grad_out,
        reduce_dp(grad_gate).astype(F32),
        reduce_dp(grad_up).astype(F32),
        reduce_dp(grad_down_t).astype(F32).T,
    )


def solution(mesh):
    in_specs = (
        P(("dp", "tensor"), None), P("dp", None), P("dp"), P(), P(),
        P(None, "tensor"), P(None, "tensor"), P(None, "tensor"), P("tensor", None),
        P(None, "tensor"), P(None, "tensor"), P("tensor", None), P(("dp", "tensor"), None),
    )
    out_specs = (
        P(("dp", "tensor"), None), P(("dp", "tensor"), None), P(), P(),
        P("dp", "tensor"), P("dp", "tensor"), P("dp", "tensor"), P("tensor", "dp"),
        P("dp", "tensor"), P("dp", "tensor"), P("tensor", "dp"),
    )
    return jax.shard_map(on_device, mesh=mesh, in_specs=in_specs, out_specs=out_specs, check_vma=False)
```

```python
import functools

import jax
import jax.numpy as jnp
import numpy as np
from jax import lax
from jax.experimental import pallas as pl
from jax.experimental.pallas import tpu as pltpu
from jax.sharding import PartitionSpec as P

HD = 128
FF = 6144
EPS = 1e-06
NEG = -1e30
BF = jnp.bfloat16
F32 = jnp.float32
QB = 256


def norm_factor(values):
    return lax.rsqrt(jnp.mean(values * values, axis=-1, keepdims=True) + EPS)


def norm_back(values, factor, row_gain, gradient):
    scaled = gradient * row_gain
    inner_mean = jnp.mean(scaled * values, axis=-1, keepdims=True)
    back_rows = factor * scaled - values * (factor * factor * factor) * inner_mean
    return (back_rows, jnp.sum(gradient * values * factor, axis=0))


def dot(left, right, dims=((1,), (0,))):
    return lax.dot_general(left, right, (dims, ((), ())), preferred_element_type=F32)


MESH = pl.DeviceIdType.MESH
ANY = pl.BlockSpec(memory_space=pl.ANY)
VM = pl.BlockSpec(memory_space=pltpu.VMEM)
DMA = pltpu.SemaphoreType.DMA
RANKS = 4


def across(rank, k):
    if k == 3:
        return 3 - rank
    if k == 1:
        return rank + 1 - 2 * lax.rem(rank, 2)
    if k == 2:
        return rank + 2 - 4 * lax.div(rank, 2)
    return rank


def flip(index, bit):
    step = 2**bit
    return index + step - 2 * step * lax.rem(lax.div(index, step), 2)


def inner_plane(rank):
    return (rank == 1) | (rank == 2)


def greet(peers):
    barrier = pltpu.get_barrier_semaphore()
    for peer in peers:
        pl.semaphore_signal(barrier, inc=1, device_id=peer, device_id_type=MESH)
    pl.semaphore_wait(barrier, len(peers))


def line_peers(rank):
    return [{"tensor": across(rank, k)} for k in (1, 2, 3)]


class LineGather:
    def __init__(self, rank, view, pieces, send_sems, recv_sems):
        self.rank, self.view, self.pieces = rank, view, pieces
        self.send_sems, self.recv_sems = send_sems, recv_sems
        self.inner = inner_plane(rank)

    @staticmethod
    def sems(pieces):
        return [DMA((4, pieces)), DMA((RANKS, pieces))]

    def copy(self, source, piece, k, slot):
        return pltpu.make_async_remote_copy(
            src_ref=self.view(source, piece), dst_ref=self.view(source, piece),
            send_sem=self.send_sems.at[slot, piece], recv_sem=self.recv_sems.at[source, piece],
            device_id={"tensor": across(self.rank, k)}, device_id_type=MESH,
        )

    def start(self, piece):
        self.copy(self.rank, piece, 2, 0).start()
        self.copy(self.rank, piece, 1, 1).start()
        pl.when(self.inner)(lambda: self.copy(self.rank, piece, 3, 2).start())

    def arrive(self, k, piece):
        source = across(self.rank, k)
        self.copy(source, piece, 1, 3).wait_recv()
        if k == 2:
            pl.when(self.inner)(lambda: self.copy(source, piece, 1, 3).start())

    def finish(self):
        for piece in range(self.pieces):
            self.copy(self.rank, piece, 2, 0).wait_send()
            self.copy(self.rank, piece, 1, 1).wait_send()

        @pl.when(self.inner)
        def _():
            for piece in range(self.pieces):
                self.copy(self.rank, piece, 3, 2).wait_send()
                self.copy(across(self.rank, 2), piece, 1, 3).wait_send()


def local(source, target, sem):
    return pltpu.make_async_copy(source, target, sem)


class LineScatter:
    def __init__(self, rank, parts, inbox, send_sems, recv_sems, pieces):
        self.rank, self.parts, self.inbox, self.pieces = rank, parts, inbox, pieces
        self.send_sems, self.recv_sems = send_sems, recv_sems
        self.inner = inner_plane(rank)
        self.end = (rank == 0) | (rank == 3)
        self.rows = parts.shape[1] // pieces

    @staticmethod
    def sems(pieces):
        return [DMA((4, pieces)), DMA((4, pieces))]

    def where(self, piece):
        return pl.ds(piece * self.rows, self.rows)

    def copy(self, part, slot, k, piece):
        return pltpu.make_async_remote_copy(
            src_ref=self.parts.at[part, self.where(piece)], dst_ref=self.inbox.at[slot, self.where(piece)],
            send_sem=self.send_sems.at[part, piece], recv_sem=self.recv_sems.at[slot, piece],
            device_id={"tensor": across(self.rank, k)}, device_id_type=MESH,
        )

    def send_far(self):
        for piece in range(self.pieces):
            pl.when(self.inner)(lambda: self.copy(3, 3, 3, piece).start())
            pl.when(self.end)(lambda: self.copy(3, 0, 1, piece).start())

    def send_two_end(self):
        @pl.when(self.end)
        def _():
            for piece in range(self.pieces):
                self.copy(2, 2, 2, piece).start()

    def send_two_inner(self):
        @pl.when(self.inner)
        def _():
            for piece in range(self.pieces):
                where = self.where(piece)
                self.copy(3, 0, 1, piece).wait_recv()
                self.parts[2, where] = (self.parts[2, where].astype(F32) + self.inbox[0, where].astype(F32)).astype(BF)
                self.copy(2, 2, 2, piece).start()

    def send_near(self):
        for piece in range(self.pieces):
            self.copy(1, 1, 1, piece).start()

    def total(self, target):
        for piece in range(self.pieces):
            where = self.where(piece)
            self.copy(1, 1, 1, piece).wait_recv()
            self.copy(2, 2, 2, piece).wait_recv()
            target[where] = (self.parts[0, where].astype(F32) + self.inbox[1, where].astype(F32)) + self.inbox[2, where].astype(F32)

        @pl.when(self.inner)
        def _():
            for piece in range(self.pieces):
                where = self.where(piece)
                self.copy(3, 3, 3, piece).wait_recv()
                target[where] += self.inbox[3, where].astype(F32)

    def finish(self):
        for piece in range(self.pieces):
            for part in (1, 2, 3):
                self.copy(part, part, part, piece).wait_send()


class GroupReduce:
    def __init__(self, group, dp, send, keep, first, boxes, split, sems):
        self.group, self.dp, self.send, self.keep, self.first, self.boxes = group, dp, send, keep, first, boxes
        self.bits = dp.bit_length() - 1
        self.mates = dp // 2
        columns = first.shape[3]
        self.cols = (pl.ds(0, split), pl.ds(split, columns - split))
        self.sems = sems

    @staticmethod
    def sem_shapes(dp, count):
        mates, bits = dp // 2, dp.bit_length() - 1
        shapes = [DMA((count, mates)), DMA((count, mates))]
        for t in range(1, bits):
            shapes += [DMA((2, count, mates >> t)), DMA((2, count, mates >> t))]
        return shapes

    @staticmethod
    def box_shapes(dp, count, share, columns, split):
        mates, bits = dp // 2, dp.bit_length() - 1
        shapes = [pltpu.VMEM((count, mates, share, columns), BF)]
        for t in range(1, bits):
            shapes += [pltpu.VMEM((count, mates >> t, share, split), BF), pltpu.VMEM((count, mates >> t, share, columns - split), BF)]
        return shapes

    def peers(self):
        return [{"dp": flip(self.group, b)} for b in range(self.bits)]

    def bit(self, b):
        return lax.rem(lax.div(self.group, 2**b), 2)

    def copy0(self, w, j):
        return pltpu.make_async_remote_copy(
            src_ref=self.send(w, 2 * j + 1 - self.bit(0)), dst_ref=self.first.at[w, j],
            send_sem=self.sems[0].at[w, j], recv_sem=self.sems[1].at[w, j],
            device_id={"dp": flip(self.group, 0)}, device_id_type=MESH)

    def place(self, t, half, j, mine):
        n = self.bits
        if half == 0:
            low = sum((self.bit(i) * 2 ** (i - 1) for i in range(1, t)), 0)
            bit = self.bit(t)
            return (2 * j + (bit if mine else 1 - bit)) * 2 ** (t - 1) + low
        high = sum((self.bit(n - i) * 2 ** (n - 1 - i) for i in range(1, t)), 0)
        bit = self.bit(n - t)
        return high + (bit if mine else 1 - bit) * 2 ** (n - 1 - t) + j

    def copy(self, t, half, w, j):
        return pltpu.make_async_remote_copy(
            src_ref=self.keep(w, self.place(t, half, j, False)).at[:, self.cols[half]], dst_ref=self.boxes[2 * (t - 1) + half].at[w, j],
            send_sem=self.sems[2 * t].at[half, w, j], recv_sem=self.sems[2 * t + 1].at[half, w, j],
            device_id={"dp": flip(self.group, t if half == 0 else self.bits - t)}, device_id_type=MESH)

    def start0(self, w):
        for j in range(self.mates):
            self.copy0(w, j).start()

    def start(self, t, w):
        for j in range(self.mates >> t):
            for half in range(2):
                self.copy(t, half, w, j).start()

    def add0(self, w):
        def body(j, carry):
            self.copy0(w, j).wait_recv()
            mine = self.keep(w, j)
            mine[...] = (mine[...].astype(F32) + self.first[w, j].astype(F32)).astype(BF)
            return carry

        lax.fori_loop(0, self.mates, body, 0)
        self.start(1, w)

    def add(self, t, w, target=None):
        for half in range(2):
            def body(j, carry):
                self.copy(t, half, w, j).wait_recv()
                mine = self.keep(w, self.place(t, half, j, True)).at[:, self.cols[half]]
                value = mine[...].astype(F32) + self.boxes[2 * (t - 1) + half][w, j].astype(F32)
                if target is None:
                    mine[...] = value.astype(BF)
                else:
                    target[:, self.cols[half]] = value
                return carry

            lax.fori_loop(0, self.mates >> t, body, 0)
        if target is None:
            self.start(t + 1, w)

    def finish(self, count):
        def body(w, carry):
            for j in range(self.mates):
                self.copy0(w, j).wait_send()
            for t in range(1, self.bits):
                for j in range(self.mates >> t):
                    for half in range(2):
                        self.copy(t, half, w, j).wait_send()
            return carry

        lax.fori_loop(0, count, body, 0)


def rope_numpy(length):
    half = HD // 2
    frequency = np.float32(10000.0) ** (-np.arange(half, dtype=np.float32) / np.float32(half))
    angles = np.arange(length, dtype=np.float32)[:, None] * frequency[None, :]
    cosine, sine = np.cos(angles), np.sin(angles)
    return (np.concatenate([cosine, cosine], 1), np.concatenate([-sine, sine], 1))


def input_body(dp, tok, cot, seg, wo, wq, wk, wv, gain, cosine, sine,
               x_out, a1_out, q_out, k_out, v_out, wo_out, cot_out,
               xs, a1s, qkv, ws, wos, cots, x_ss, x_rs, z_ss, z_rs, d_ss, d_rs, c_ss, l_sem):
    rank, group = lax.axis_index("tensor"), lax.axis_index("dp")
    rows = tok.shape[0]
    half_rows = rows // 2
    mates = dp // 2
    partner = flip(group, 0)
    parity = lax.rem(group, 2)
    pair = lax.div(group, 2)

    def mate(step):
        return lax.rem(pair + step, mates) * 2 + parity

    first = [local(wo.at[group], wos.at[rank, group], l_sem.at[0]), local(tok, xs.at[rank], l_sem.at[1]), local(cot, cots, l_sem.at[2])]
    weights = [local(w, ws.at[i], l_sem.at[3 + i]) for i, w in enumerate((wq, wk, wv))]
    for c in first + weights:
        c.start()
    greet(line_peers(rank) + [{"dp": partner}] + [{"dp": mate(s)} for s in range(1, mates)])
    out_gather = LineGather(rank, lambda s, p: wos.at[s, group], 1, z_ss, z_rs)
    first[0].wait()
    out_gather.start(0)
    gather = LineGather(rank, lambda s, p: xs.at[s, pl.ds(p * half_rows, half_rows)], 2, x_ss, x_rs)
    first[1].wait()
    gather.start(0)
    gather.start(1)
    first[2].wait()
    cots[...] = jnp.where(seg[...] >= 0, cots[...], jnp.zeros_like(cots))
    for w in weights:
        w.wait()

    def chunk(source):
        x = xs[source].astype(F32)
        a1s[source] = (x * norm_factor(x) * gain[...]).astype(BF)
        where = pl.ds(pl.multiple_of(source * rows, rows), rows)
        for i in range(3):
            product = dot(a1s[source], ws[i])
            for h in range(product.shape[1] // HD):
                head = product[:, h * HD : (h + 1) * HD]
                if i < 2:
                    head = head * cosine[where, :] + pltpu.roll(head, HD // 2, 1) * sine[where, :]
                qkv[i, where, h * HD : (h + 1) * HD] = head.astype(BF)

    chunk(rank)
    for k in (1, 2, 3):
        out_gather.arrive(k, 0)

    def mate_copy(step):
        return pltpu.make_async_remote_copy(
            src_ref=wos.at[:, group], dst_ref=wos.at[:, group], send_sem=d_ss.at[step], recv_sem=d_rs.at[group],
            device_id={"dp": mate(step)}, device_id_type=MESH)

    def mate_arrival(step):
        piece = mate(step)
        return pltpu.make_async_remote_copy(
            src_ref=wos.at[:, piece], dst_ref=wos.at[:, piece], send_sem=d_ss.at[step], recv_sem=d_rs.at[piece],
            device_id={"dp": piece}, device_id_type=MESH)

    def core_copy(step, owner):
        piece = lax.rem(pair + step, mates) * 2 + owner
        return pltpu.make_async_remote_copy(
            src_ref=wos.at[:, piece], dst_ref=wos.at[:, piece], send_sem=c_ss.at[step], recv_sem=d_rs.at[piece],
            device_id={"dp": partner}, device_id_type=MESH)

    for step in range(1, mates):
        mate_copy(step).start()
    core_copy(0, parity).start()
    for piece in range(2):
        gather.arrive(1, piece)
        gather.arrive(2, piece)
    chunk(across(rank, 1))
    chunk(across(rank, 2))
    for step in range(1, mates):
        mate_arrival(step).wait_recv()
        core_copy(step, parity).start()
    for piece in range(2):
        gather.arrive(3, piece)
    chunk(across(rank, 3))
    for step in range(mates):
        core_copy(step, 1 - parity).wait_recv()
    gather.finish()
    out_gather.finish()
    for step in range(1, mates):
        mate_copy(step).wait_send()
    for step in range(mates):
        core_copy(step, parity).wait_send()
    last = [local(xs, x_out, l_sem.at[0]), local(a1s, a1_out, l_sem.at[1]), local(wos, wo_out, l_sem.at[2]),
            local(qkv.at[0], q_out, l_sem.at[3]), local(qkv.at[1], k_out, l_sem.at[4]), local(qkv.at[2], v_out, l_sem.at[5]),
            local(cots, cot_out, l_sem.at[6])]
    for c in last:
        c.start()
    for c in last:
        c.wait()


def input_kernel(dp, tokens, cotangent, seg_own, w_out, w_query, w_key, w_value, gain, cosine, sine):
    rows, model = tokens.shape
    width = w_query.shape[1]
    length = RANKS * rows
    part = w_out.shape[0] // dp
    mates = dp // 2
    shard = jax.ShapeDtypeStruct((RANKS, rows, model), BF)
    heads = jax.ShapeDtypeStruct((length, width), BF)
    outs = pl.pallas_call(
        functools.partial(input_body, dp),
        in_specs=[ANY, ANY, VM, ANY, ANY, ANY, ANY, VM, VM, VM],
        out_specs=[ANY] * 7,
        out_shape=[shard, shard, heads, heads, heads, jax.ShapeDtypeStruct((RANKS, dp, part, model), BF),
                   jax.ShapeDtypeStruct((rows, model), BF)],
        scratch_shapes=[
            pltpu.VMEM((RANKS, rows, model), BF), pltpu.VMEM((RANKS, rows, model), BF), pltpu.VMEM((3, length, width), BF),
            pltpu.VMEM((3, model, width), BF), pltpu.VMEM((RANKS, dp, part, model), BF), pltpu.VMEM((rows, model), BF),
            *LineGather.sems(2), *LineGather.sems(1),
            DMA((mates,)), DMA((dp,)), DMA((mates,)), DMA((7,)),
        ],
        compiler_params=pltpu.CompilerParams(collective_id=1, has_side_effects=True, vmem_limit_bytes=56 << 20),
        name="input_gather",
    )(tokens, cotangent, seg_own, w_out.reshape(dp, part, model), w_query, w_key, w_value, gain, cosine, sine)
    x_all, a1_all, query, key, value, w_out_all, cot_own = outs
    return x_all, a1_all, query, key, value, w_out_all.reshape(RANKS, dp * part, model), cot_own


def attend_body(q, k, v, cot, x_all, wo_all, seg_col, seg_row, gain,
                p_out, dy_out, a2_out, h_out, ob_out,
                qkv, ps, dys, obs, xs, wos, hs, a2s, y_ss, y_rs, o_ss, o_rs, l_sem):
    rank = lax.axis_index("tensor")
    heads = p_out.shape[0]
    length = q.shape[0]
    rows = cot.shape[0]
    half_rows = rows // 2
    scale = HD ** (-0.5)
    loads = [local(cot, dys.at[rank], l_sem.at[0])]
    loads += [local(t, qkv.at[i], l_sem.at[1 + i]) for i, t in enumerate((q, k, v))]
    late = [local(x_all, xs, l_sem.at[4]), local(wo_all, wos, l_sem.at[5])]
    for c in loads + late:
        c.start()
    greet(line_peers(rank))
    grads = LineGather(rank, lambda s, p: dys.at[s, pl.ds(p * half_rows, half_rows)], 2, y_ss, y_rs)
    attended = LineGather(rank, lambda s, p: obs.at[s, :, pl.ds(pl.multiple_of(p * HD, HD), HD)], heads, o_ss, o_rs)
    loads[0].wait()
    grads.start(0)
    grads.start(1)
    for c in loads[1:]:
        c.wait()

    def head(h, carry):
        cols = pl.ds(pl.multiple_of(h * HD, HD), HD)
        for start in range(0, length, QB):
            extent = start + QB
            scores = dot(qkv[0, start:extent, cols], qkv[1, :extent, cols], ((1,), (1,)))
            row_ids = lax.broadcasted_iota(jnp.int32, (QB, extent), 0) + start
            col_ids = lax.broadcasted_iota(jnp.int32, (QB, extent), 1)
            allowed = (col_ids <= row_ids) & (seg_col[start:extent, :] == seg_row[:, :extent])
            logits = jnp.where(allowed, scores * scale, NEG)
            expo = jnp.exp(logits - jnp.max(logits, axis=-1, keepdims=True))
            probs = (expo * (1.0 / jnp.sum(expo, axis=-1, keepdims=True))).astype(BF)
            ps[h, start:extent, :extent] = probs
            obs[rank, start:extent, cols] = dot(probs, qkv[2, :extent, cols]).astype(BF)
        attended.start(h)
        return carry

    lax.fori_loop(0, heads, head, 0)
    keep = local(ps, p_out, l_sem.at[6])
    keep.start()
    for c in late:
        c.wait()

    def add(source, first=False, last=False):
        def block(b, carry):
            part = dot(obs[source, pl.ds(pl.multiple_of(b * rows, rows), rows), :], wos[source])
            total = part + (xs[b].astype(F32) if first else hs[b])
            hs[b] = total
            if last:
                a2s[b] = (total * norm_factor(total) * gain[...]).astype(BF)
            return carry

        lax.fori_loop(0, RANKS, block, 0)

    add(rank, first=True)
    for piece in range(2):
        grads.arrive(2, piece)
    for piece in range(heads):
        attended.arrive(2, piece)
    for piece in range(heads):
        attended.arrive(1, piece)
    add(across(rank, 2))
    add(across(rank, 1))
    for piece in range(2):
        grads.arrive(1, piece)
        grads.arrive(3, piece)
    dy_done = local(dys, dy_out, l_sem.at[0])
    dy_done.start()
    for piece in range(heads):
        attended.arrive(3, piece)
    add(across(rank, 3), last=True)
    last = [local(a2s, a2_out, l_sem.at[1]), local(hs.at[rank], h_out, l_sem.at[2]),
            local(obs.at[:, pl.ds(pl.multiple_of(rank * rows, rows), rows)], ob_out, l_sem.at[3])]
    for c in last:
        c.start()
    grads.finish()
    attended.finish()
    for c in last + [keep, dy_done]:
        c.wait()


def attend_kernel(query, key, value, cot_own, x_all, w_out_all, seg_ids, gain):
    length, width = query.shape
    heads = width // HD
    rows, model = cot_own.shape
    shard = (RANKS, rows, model)
    return pl.pallas_call(
        attend_body,
        in_specs=[ANY] * 6 + [VM] * 3,
        out_specs=[ANY] * 5,
        out_shape=[jax.ShapeDtypeStruct((heads, length, length), BF), jax.ShapeDtypeStruct(shard, BF), jax.ShapeDtypeStruct(shard, BF),
                   jax.ShapeDtypeStruct((rows, model), F32), jax.ShapeDtypeStruct((RANKS, rows, width), BF)],
        scratch_shapes=[
            pltpu.VMEM((3, length, width), BF), pltpu.VMEM((heads, length, length), BF), pltpu.VMEM(shard, BF),
            pltpu.VMEM((RANKS, length, width), BF), pltpu.VMEM(shard, BF), pltpu.VMEM((RANKS, width, model), BF),
            pltpu.VMEM(shard, F32), pltpu.VMEM(shard, BF),
            *LineGather.sems(2), *LineGather.sems(heads), DMA((7,)),
        ],
        compiler_params=pltpu.CompilerParams(collective_id=2, has_side_effects=True, vmem_limit_bytes=60 << 20),
        name="attend_gather",
    )(query, key, value, cot_own, x_all, w_out_all, seg_ids.reshape(length, 1), seg_ids.reshape(1, length), gain)


def pick(step, choices):
    value = choices[-1]
    for i in range(len(choices) - 1):
        value = jnp.where(step == i, choices[i], value)
    return value


FT = 768
WB = 384


def mlp_body(a2, dy, wg, wu, wd, hid, cot, gran, gain,
             g_out, down_out, dh_out, gain_out,
             lefts, acts, ws, parts, inbox, stage, downs, hs, cots, total, gains, r_ss, r_rs, l_sem, s_sem):
    rank = lax.axis_index("tensor")
    rows, model = cot.shape
    width = wg.shape[1]
    per, share = stage.shape[1], stage.shape[2]
    loads = [local(wg, ws.at[0], l_sem.at[0]), local(a2, lefts.at[0], l_sem.at[1]), local(wu, ws.at[1], l_sem.at[2]),
             local(dy, lefts.at[1], l_sem.at[3]), local(wd, ws.at[2], l_sem.at[4])]
    late = [local(hid, hs, l_sem.at[5]), local(cot, cots, l_sem.at[6])]
    for c in loads + late:
        c.start()
    greet(line_peers(rank))
    scatter = LineScatter(rank, parts, inbox, r_ss, r_rs, 2)
    order = [across(rank, k) for k in (3, 2, 1, 0)]
    limit = FF // 8 * lax.shift_left(1, gran[0] - 1) - rank * width

    def step(i, carry):
        j = pick(i, order)

        def tile(t, inner_carry):
            cols = pl.ds(pl.multiple_of(t * FT, FT), FT)

            @pl.when((i == 0) & (t == 0))
            def _():
                loads[0].wait()
                loads[1].wait()

            gate = dot(lefts[0, j], ws[0, :, cols])

            @pl.when((i == 0) & (t == 0))
            def _():
                loads[2].wait()

            up = dot(lefts[0, j], ws[1, :, cols])

            @pl.when((i == 0) & (t == 0))
            def _():
                loads[3].wait()
                loads[4].wait()

            dz = dot(lefts[1, j], ws[2, cols, :], ((1,), (1,)))
            unit = lax.broadcasted_iota(jnp.int32, gate.shape, 1) + t * FT
            mask = unit < limit
            sigma = jax.nn.sigmoid(gate)
            active = jnp.where(mask, gate * sigma, 0.0)
            acts[2, j, :, cols] = (active * up).astype(BF)
            acts[0, j, :, cols] = jnp.where(mask, dz * up * sigma * (1.0 + gate * (1.0 - sigma)), 0.0).astype(BF)
            acts[1, j, :, cols] = (dz * active).astype(BF)
            return inner_carry

        lax.fori_loop(0, width // FT, tile, 0)

        def back(t, inner_carry):
            cols = pl.ds(pl.multiple_of(t * FT, FT), FT)
            parts[3 - i, :, cols] = (
                dot(acts[0, j], ws[0, cols, :], ((1,), (1,))) + dot(acts[1, j], ws[1, cols, :], ((1,), (1,)))
            ).astype(BF)
            return inner_carry

        lax.fori_loop(0, model // FT, back, 0)
        pl.when(i == 0)(scatter.send_far)
        pl.when(i == 1)(scatter.send_two_end)

        @pl.when(i == 2)
        def _():
            scatter.send_near()
            scatter.send_two_inner()

        return carry

    lax.fori_loop(0, 4, step, 0)
    blocks = model // WB

    def put(i, slot):
        w, b = lax.div(i, blocks), lax.rem(i, blocks)
        return local(stage.at[slot], g_out.at[w, pl.ds(b * per, per)], s_sem.at[slot])

    def grads(i, carry):
        slot = lax.rem(i, 2)
        w, b = lax.div(i, blocks), lax.rem(i, blocks)
        left = lax.div(w, 2)
        cols = pl.ds(pl.multiple_of(b * WB, WB), WB)
        value = dot(lefts[left, 0, :, cols], acts[w, 0], ((0,), (0,)))
        for s in range(1, RANKS):
            value += dot(lefts[left, s, :, cols], acts[w, s], ((0,), (0,)))
        pl.when(i >= 2)(lambda: put(i - 2, slot).wait())
        low = value.astype(BF)
        for p in range(per):
            stage[slot, p] = low[p * share : (p + 1) * share]
        put(i, slot).start()
        return carry

    lax.fori_loop(0, 3 * blocks, grads, 0)

    def down(i, carry):
        downs[3 - i] = dot(acts[2, pick(i, order)], ws[2]).astype(BF)
        return carry

    lax.fori_loop(0, 4, down, 0)
    keep = local(downs, down_out, l_sem.at[0])
    keep.start()
    for c in late:
        c.wait()
    scatter.total(total)
    values, gradient = hs[...], total[...]
    factor = norm_factor(values)
    back_rows, gain_rows = norm_back(values, factor, gain[...], gradient)
    total[...] = cots[...].astype(F32) + back_rows
    gains[...] = gain_rows.reshape(1, model)
    last = [local(total, dh_out, l_sem.at[1]), local(gains, gain_out, l_sem.at[2])]
    for c in last:
        c.start()
    scatter.finish()
    put(3 * blocks - 2, 0).wait()
    put(3 * blocks - 1, 1).wait()
    for c in last + [keep]:
        c.wait()


def mlp_kernel(dp, a2, dy, w_gate, w_up, w_down, hidden_own, cot_own, granularity, gain):
    rows, model = cot_own.shape
    width = w_gate.shape[1]
    share = model // dp
    shard = (RANKS, rows, model)
    return pl.pallas_call(
        mlp_body,
        in_specs=[ANY] * 7 + [pl.BlockSpec(memory_space=pltpu.SMEM), VM],
        out_specs=[ANY] * 4,
        out_shape=[jax.ShapeDtypeStruct((3, dp, share, width), BF), jax.ShapeDtypeStruct(shard, BF),
                   jax.ShapeDtypeStruct((rows, model), F32), jax.ShapeDtypeStruct((1, model), F32)],
        scratch_shapes=[
            pltpu.VMEM((2, *shard), BF), pltpu.VMEM((3, RANKS, rows, width), BF), pltpu.VMEM((3, model, width), BF),
            pltpu.VMEM(shard, BF), pltpu.VMEM(shard, BF), pltpu.VMEM((2, WB // share, share, width), BF), pltpu.VMEM(shard, BF),
            pltpu.VMEM((rows, model), F32), pltpu.VMEM((rows, model), BF), pltpu.VMEM((rows, model), F32), pltpu.VMEM((1, model), F32),
            *LineScatter.sems(2), DMA((7,)), DMA((2,)),
        ],
        compiler_params=pltpu.CompilerParams(collective_id=3, has_side_effects=True, vmem_limit_bytes=63 << 20),
        name="mlp_scatter",
    )(a2, dy, w_gate, w_up, w_down, hidden_own, cot_own, granularity, gain)


def attention_back_body(dp, dh, wo_all, downs, grads, q, k, v, p_all, hid, cosine, sine,
                        out_out, dq_out, dk_out, dv_out, gf_out,
                        dhs, low, wos, parts, inbox, dobs, dos, qkv, ps, ds, dqkv, hs, outs, kept, finals, *rest):
    rank, group = lax.axis_index("tensor"), lax.axis_index("dp")
    rounds = 2 * (dp.bit_length() - 1)
    first, boxes, rest = rest[0], rest[1 : rounds - 1], rest[rounds - 1 :]
    sems, (r_ss, r_rs, a_ss, a_rs, l_sem, p_sem, f_sem) = rest[:rounds], rest[rounds:]
    rows, model = dh.shape
    length, width = q.shape
    heads, half, scale = width // HD, HD // 2, HD ** (-0.5)
    count = grads.shape[0]
    parity = lax.rem(group, 2)
    loads = [local(dh, dhs, l_sem.at[0]), local(wo_all, wos, l_sem.at[1]), local(downs, parts, l_sem.at[2])]
    owns = [local(grads.at[w, :, parity], kept.at[w], f_sem.at[w]) for w in range(count)]
    late = [local(t, qkv.at[i], l_sem.at[3 + i]) for i, t in enumerate((q, k, v))] + [local(hid, hs, l_sem.at[6])]
    for c in loads + owns + late:
        c.start()

    def probs(h):
        return local(p_all.at[h], ps.at[lax.rem(h, 2)], p_sem.at[lax.rem(h, 2)])

    probs(0).start()
    probs(1).start()
    reduce = GroupReduce(
        group, dp, lambda w, d: grads.at[w, lax.div(d, 2), lax.rem(d, 2)], lambda w, j: kept.at[w, j], first, boxes, model // 2, sems)
    greet(line_peers(rank) + reduce.peers())
    for w in range(count):
        reduce.start0(w)
    scatter = LineScatter(rank, parts, inbox, r_ss, r_rs, 2)

    def exchange(k, source):
        where = pl.ds(pl.multiple_of(source * rows, rows), rows)
        return pltpu.make_async_remote_copy(
            src_ref=dobs.at[k - 1], dst_ref=dos.at[where], send_sem=a_ss.at[k], recv_sem=a_rs.at[source],
            device_id={"tensor": across(rank, k)}, device_id_type=MESH)

    loads[0].wait()
    low[...] = dhs[...].astype(BF)
    loads[1].wait()
    for k in (3, 2, 1):
        dobs[k - 1] = dot(low[...], wos[across(rank, k)], ((1,), (1,))).astype(BF)
        exchange(k, rank).start()
    dos[pl.ds(pl.multiple_of(rank * rows, rows), rows), :] = dot(low[...], wos[rank], ((1,), (1,))).astype(BF)
    loads[2].wait()
    scatter.send_far()
    scatter.send_two_end()
    scatter.send_near()
    for c in owns:
        c.wait()

    def fold(w, carry):
        reduce.add0(w)
        return carry

    lax.fori_loop(0, count, fold, 0)
    for c in late:
        c.wait()
    for k in (3, 2, 1):
        exchange(k, across(rank, k)).wait_recv()

    def head(h, carry):
        cols = pl.ds(pl.multiple_of(h * HD, HD), HD)
        slot = lax.rem(h, 2)
        probs(h).wait()

        def unrope(grad, start):
            where = slice(start, start + QB)
            return (grad * cosine[where, :] - pltpu.roll(grad, half, 1) * sine[where, :]).astype(BF)

        for start in range(0, length, QB):
            extent = start + QB
            where = slice(start, extent)
            grad_p = dot(dos[where, cols], qkv[2, :extent, cols], ((1,), (1,)))
            p = ps[slot, where, :extent].astype(F32)
            weighted = p * grad_p
            delta = jnp.sum(weighted, axis=-1, keepdims=True)
            ds[where, :extent] = ((weighted - p * delta) * scale).astype(BF)
            dqkv[0, where, cols] = unrope(dot(ds[where, :extent], qkv[1, :extent, cols]), start)
        for start in range(0, length, QB):
            where = slice(start, start + QB)
            dqkv[1, where, cols] = unrope(dot(ds[start:, where], qkv[0, start:, cols], ((0,), (0,))), start)
            dqkv[2, where, cols] = dot(ps[slot, start:, where], dos[start:, cols], ((0,), (0,))).astype(BF)
        pl.when(h + 2 < heads)(lambda: probs(h + 2).start())
        return carry

    lax.fori_loop(0, heads, head, 0)
    done = [local(dqkv.at[i], t, l_sem.at[i]) for i, t in enumerate((dq_out, dk_out, dv_out))]
    for c in done:
        c.start()
    reduce.add(1, 0)
    scatter.send_two_inner()
    reduce.add(1, 1)
    reduce.add(1, 2)
    for t in range(2, reduce.bits - 1):
        for w in range(count):
            reduce.add(t, w)

    def put(w):
        return local(finals.at[w], gf_out.at[w], f_sem.at[w])

    for w in range(count):
        reduce.add(reduce.bits - 1, w, finals.at[w])
        put(w).start()
    scatter.total(dhs)
    outs[...] = (hs[...] + dhs[...]).astype(BF)
    last = local(outs, out_out, l_sem.at[3])
    last.start()
    scatter.finish()
    for k in (1, 2, 3):
        exchange(k, rank).wait_send()
    reduce.finish(count)
    for w in range(count):
        put(w).wait()
    for c in done + [last]:
        c.wait()


def attention_back_kernel(dp, grad_hidden, w_out_all, down_parts, grads_ff, query, key, value, probs_low, hidden_own, cosine, sine):
    rows, model = grad_hidden.shape
    length, width = query.shape
    count, _, share, columns = grads_ff.shape
    mates = dp // 2
    shard = (RANKS, rows, model)
    heads = jax.ShapeDtypeStruct((length, width), BF)
    return pl.pallas_call(
        functools.partial(attention_back_body, dp),
        in_specs=[ANY] * 9 + [VM, VM],
        out_specs=[ANY] * 5,
        out_shape=[jax.ShapeDtypeStruct((rows, model), BF), heads, heads, heads, jax.ShapeDtypeStruct((count, share, columns), F32)],
        scratch_shapes=[
            pltpu.VMEM((rows, model), F32), pltpu.VMEM((rows, model), BF), pltpu.VMEM((RANKS, width, model), BF),
            pltpu.VMEM(shard, BF), pltpu.VMEM(shard, BF), pltpu.VMEM((3, rows, width), BF), pltpu.VMEM((length, width), BF),
            pltpu.VMEM((3, length, width), BF), pltpu.VMEM((2, length, length), BF), pltpu.VMEM((length, length), BF),
            pltpu.VMEM((3, length, width), BF), pltpu.VMEM((rows, model), F32), pltpu.VMEM((rows, model), BF),
            pltpu.VMEM((count, mates, share, columns), BF), pltpu.VMEM((count, share, columns), F32),
            *GroupReduce.box_shapes(dp, count, share, columns, columns // 2), *GroupReduce.sem_shapes(dp, count),
            *LineScatter.sems(2), DMA((4,)), DMA((RANKS,)), DMA((7,)), DMA((2,)), DMA((count,)),
        ],
        compiler_params=pltpu.CompilerParams(collective_id=4, has_side_effects=True, vmem_limit_bytes=63 << 20),
        name="attention_back",
    )(grad_hidden, w_out_all, down_parts, grads_ff.reshape(count, mates, 2, share, columns),
      query, key, value, probs_low, hidden_own, cosine, sine)


def input_back_body(dp, dq, dk, dv, a1, wq, wk, wv, tok, dh, ob, gain, gain2,
                    dx_out, gains_out, gqkv_out, gout_out,
                    dqkv, a1s, ws, xs, dhs, low, obs, parts, inbox, g1, g2, f1, f2, f2_low, box2, f3, gbuf, gbox, total, dxs, *rest):
    rank, group = lax.axis_index("tensor"), lax.axis_index("dp")
    bits = dp.bit_length() - 1
    boxes = [rest[: 2 * bits - 1], rest[2 * bits - 1 : 4 * bits - 2]]
    rest = rest[4 * bits - 2 :]
    sems = [rest[: 2 * bits], rest[2 * bits : 4 * bits]]
    r_ss, r_rs, z_ss, z_rs, g_ss, g_rs, l_sem = rest[4 * bits :]
    rows, model = tok.shape
    width = dq.shape[1]
    share = g1.shape[1]
    per = WB // share
    parity = lax.rem(group, 2)
    loads = [local(t, dqkv.at[i], l_sem.at[i]) for i, t in enumerate((dq, dk, dv))]
    loads += [local(t, ws.at[i], l_sem.at[3 + i]) for i, t in enumerate((wq, wk, wv))]
    late = [local(dh, dhs, l_sem.at[6]), local(ob, obs, l_sem.at[7]), local(a1, a1s, l_sem.at[8]), local(tok, xs, l_sem.at[9])]
    for c in loads + late:
        c.start()
    scatter = LineScatter(rank, parts, inbox, r_ss, r_rs, 2)
    mixed = GroupReduce(group, dp, lambda w, d: g1.at[d], lambda w, j: g1.at[2 * j + parity], boxes[0][0], boxes[0][1:], f1.shape[1] // 256 * 128, sems[0])
    output = GroupReduce(group, dp, lambda w, d: g2.at[d], lambda w, j: g2.at[2 * j + parity], boxes[1][0], boxes[1][1:], f2.shape[1] // 256 * 128, sems[1])
    greet(line_peers(rank) + mixed.peers())
    order = [across(rank, k) for k in (3, 2, 1, 0)]
    for c in loads:
        c.wait()

    def step(i, carry):
        where = pl.ds(pl.multiple_of(pick(i, order) * rows, rows), rows)
        value = dot(dqkv[0, where, :], ws[0], ((1,), (1,)))
        for s in (1, 2):
            value += dot(dqkv[s, where, :], ws[s], ((1,), (1,)))
        parts[3 - i] = value.astype(BF)
        pl.when(i == 0)(scatter.send_far)
        pl.when(i == 1)(scatter.send_two_end)
        pl.when(i == 2)(scatter.send_near)
        return carry

    lax.fori_loop(0, 4, step, 0)
    for c in late:
        c.wait()
    low[...] = dhs[...].astype(BF)

    def out_block(b, carry):
        cols = pl.ds(pl.multiple_of(b * WB, WB), WB)
        for r in range(RANKS):
            value = dot(low[:, cols], obs[r], ((0,), (0,))).astype(BF)
            for p in range(per):
                g2[b * per + p, :, r * width : (r + 1) * width] = value[p * share : (p + 1) * share]
        return carry

    lax.fori_loop(0, model // WB, out_block, 0)
    output.start0(0)

    def mixed_block(b, carry):
        cols = pl.ds(pl.multiple_of(b * WB, WB), WB)
        for s in range(3):
            value = dot(a1s[:, cols], dqkv[s], ((0,), (0,))).astype(BF)
            for p in range(per):
                g1[b * per + p, :, s * width : (s + 1) * width] = value[p * share : (p + 1) * share]
        return carry

    lax.fori_loop(0, model // WB, mixed_block, 0)
    mixed.start0(0)
    output.add0(0)
    mixed.add0(0)
    scatter.send_two_inner()
    for t in range(1, bits - 1):
        output.add(t, 0)
        mixed.add(t, 0)
    output.add(bits - 1, 0, f2)
    ends = LineScatter(rank, f2_low, box2, z_ss, z_rs, 1)
    for k in range(4):
        column = pl.ds(pl.multiple_of(across(rank, k) * width, HD), width)
        f2_low[k] = f2[:, column].astype(BF)
    ends.send_far()
    ends.send_two_end()
    ends.send_near()
    mixed.add(bits - 1, 0, f1)
    done = [local(f1, gqkv_out, l_sem.at[0])]
    done[0].start()
    scatter.total(total)
    values, gradient = xs[...].astype(F32), total[...]
    back_rows, gain_rows = norm_back(values, norm_factor(values), gain[...], gradient)
    dxs[...] = (dhs[...] + back_rows).astype(BF)
    done.append(local(dxs, dx_out, l_sem.at[1]))
    done[1].start()
    gbuf[0, 0:1, :] = gain_rows.reshape(1, model)
    gbuf[0, 1:2, :] = gain2[...]
    turns = [{"tensor": across(rank, 1)}, {"tensor": across(rank, 2)}] + [{"dp": flip(group, b)} for b in range(bits)]

    def swap(t):
        return pltpu.make_async_remote_copy(
            src_ref=gbuf.at[t], dst_ref=gbox.at[t], send_sem=g_ss.at[t], recv_sem=g_rs.at[t], device_id=turns[t], device_id_type=MESH)

    swap(0).start()
    ends.send_two_inner()
    for t in range(len(turns)):
        swap(t).wait_recv()
        gbuf[t + 1] = gbuf[t] + gbox[t]
        if t + 1 < len(turns):
            swap(t + 1).start()
    done.append(local(gbuf.at[len(turns)], gains_out, l_sem.at[2]))
    done[2].start()
    ends.total(f3)
    done.append(local(f3, gout_out, l_sem.at[3]))
    done[3].start()
    scatter.finish()
    ends.finish()
    mixed.finish(1)
    output.finish(1)
    for t in range(len(turns)):
        swap(t).wait_send()
    for c in done:
        c.wait()


def input_back_kernel(dp, grad_q, grad_k, grad_v, a1_all, w_query, w_key, w_value, tokens, grad_hidden, attended_own, gain, gain_two):
    rows, model = tokens.shape
    length, width = grad_q.shape
    share = model // dp
    bits = dp.bit_length() - 1
    shard = (RANKS, rows, model)
    wide = (3 * width, RANKS * width)
    splits = [w // 256 * 128 for w in wide]
    return pl.pallas_call(
        functools.partial(input_back_body, dp),
        in_specs=[ANY] * 10 + [VM, VM],
        out_specs=[ANY] * 4,
        out_shape=[jax.ShapeDtypeStruct((rows, model), BF), jax.ShapeDtypeStruct((2, model), F32),
                   jax.ShapeDtypeStruct((share, wide[0]), F32), jax.ShapeDtypeStruct((share, width), F32)],
        scratch_shapes=[
            pltpu.VMEM((3, length, width), BF), pltpu.VMEM((length, model), BF), pltpu.VMEM((3, model, width), BF),
            pltpu.VMEM((rows, model), BF), pltpu.VMEM((rows, model), F32), pltpu.VMEM((rows, model), BF), pltpu.VMEM((RANKS, rows, width), BF),
            pltpu.VMEM(shard, BF), pltpu.VMEM(shard, BF),
            pltpu.VMEM((dp, share, wide[0]), BF), pltpu.VMEM((dp, share, wide[1]), BF),
            pltpu.VMEM((share, wide[0]), F32), pltpu.VMEM((share, wide[1]), F32),
            pltpu.VMEM((RANKS, share, width), BF), pltpu.VMEM((RANKS, share, width), BF), pltpu.VMEM((share, width), F32),
            pltpu.VMEM((bits + 3, 2, model), F32), pltpu.VMEM((bits + 2, 2, model), F32),
            pltpu.VMEM((rows, model), F32), pltpu.VMEM((rows, model), BF),
            *GroupReduce.box_shapes(dp, 1, share, wide[0], splits[0]), *GroupReduce.box_shapes(dp, 1, share, wide[1], splits[1]),
            *GroupReduce.sem_shapes(dp, 1), *GroupReduce.sem_shapes(dp, 1),
            *LineScatter.sems(2), *LineScatter.sems(1), DMA((bits + 2,)), DMA((bits + 2,)), DMA((10,)),
        ],
        compiler_params=pltpu.CompilerParams(collective_id=5, has_side_effects=True, vmem_limit_bytes=63 << 20),
        name="input_back",
    )(grad_q, grad_k, grad_v, a1_all.reshape(length, model), w_query, w_key, w_value, tokens, grad_hidden, attended_own, gain, gain_two)


def on_device(tokens, segments, granularity, norm1_gain, norm2_gain, w_query, w_key, w_value, w_out, w_gate, w_up, w_down, cotangent):
    own_rows, model = tokens.shape
    length = segments.shape[1]
    heads_width = w_query.shape[1]
    width_here = w_gate.shape[1]
    ranks = length // own_rows
    tensor_rank = lax.axis_index("tensor")
    seg_ids = segments.reshape(length)
    cosine, sine = (jnp.asarray(t) for t in rope_numpy(length))
    dp = lax.axis_size("dp")
    seg_own = lax.dynamic_slice_in_dim(seg_ids, tensor_rank * own_rows, own_rows, 0).reshape(own_rows, 1)

    x_all, a1_all, query_rot, key_rot, value_low, w_out_all, cot_own = input_kernel(
        dp, tokens, cotangent, seg_own, w_out, w_query, w_key, w_value, norm1_gain.reshape(1, model), cosine, sine
    )
    probs_low, grad_rows, rows_two, hidden_own, attended_own = attend_kernel(
        query_rot, key_rot, value_low, cot_own, x_all, w_out_all, seg_ids, norm2_gain.reshape(1, model)
    )
    rows_one = a1_all.reshape(length, model)
    grads_ff, down_parts, grad_hidden, gain_two = mlp_kernel(
        dp, rows_two, grad_rows, w_gate, w_up, w_down, hidden_own, cot_own, granularity, norm2_gain.reshape(1, model)
    )
    output, grad_q, grad_k, grad_v, own_ff = attention_back_kernel(
        dp, grad_hidden, w_out_all, down_parts, grads_ff, query_rot, key_rot, value_low, probs_low, hidden_own, cosine, sine
    )
    grad_tokens, gains, own_qkv, own_out = input_back_kernel(
        dp, grad_q, grad_k, grad_v, a1_all, w_query, w_key, w_value, tokens, grad_hidden, attended_own, norm1_gain.reshape(1, model), gain_two
    )
    return (
        output,
        grad_tokens,
        gains[0],
        gains[1],
        own_qkv[:, :heads_width],
        own_qkv[:, heads_width : 2 * heads_width],
        own_qkv[:, 2 * heads_width :],
        own_out.T,
        own_ff[0],
        own_ff[1],
        own_ff[2].T,
    )


def solution(mesh):
    in_specs = (
        P(("dp", "tensor"), None), P("dp", None), P("dp"), P(), P(),
        P(None, "tensor"), P(None, "tensor"), P(None, "tensor"), P("tensor", None),
        P(None, "tensor"), P(None, "tensor"), P("tensor", None), P(("dp", "tensor"), None),
    )
    out_specs = (
        P(("dp", "tensor"), None), P(("dp", "tensor"), None), P(), P(),
        P("dp", "tensor"), P("dp", "tensor"), P("dp", "tensor"), P("tensor", "dp"),
        P("dp", "tensor"), P("dp", "tensor"), P("tensor", "dp"),
    )
    return jax.shard_map(on_device, mesh=mesh, in_specs=in_specs, out_specs=out_specs, check_vma=False)
```

```python
import functools

import jax
import jax.numpy as jnp
import numpy as np
from jax import lax
from jax.experimental import pallas as pl
from jax.experimental.pallas import tpu as pltpu
from jax.sharding import PartitionSpec as P

HD = 128
FF = 6144
EPS = 1e-06
NEG = -1e30
BF = jnp.bfloat16
F32 = jnp.float32
QB = 256


def norm_factor(values):
    return lax.rsqrt(jnp.mean(values * values, axis=-1, keepdims=True) + EPS)


def norm_back(values, factor, row_gain, gradient):
    scaled = gradient * row_gain
    inner_mean = jnp.mean(scaled * values, axis=-1, keepdims=True)
    back_rows = factor * scaled - values * (factor * factor * factor) * inner_mean
    return (back_rows, jnp.sum(gradient * values * factor, axis=0))


def dot(left, right, dims=((1,), (0,))):
    return lax.dot_general(left, right, (dims, ((), ())), preferred_element_type=F32)


MESH = pl.DeviceIdType.MESH
ANY = pl.BlockSpec(memory_space=pl.ANY)
VM = pl.BlockSpec(memory_space=pltpu.VMEM)
DMA = pltpu.SemaphoreType.DMA
RANKS = 4


def across(rank, k):
    if k == 3:
        return 3 - rank
    if k == 1:
        return rank + 1 - 2 * lax.rem(rank, 2)
    if k == 2:
        return rank + 2 - 4 * lax.div(rank, 2)
    return rank


def flip(index, bit):
    step = 2**bit
    return index + step - 2 * step * lax.rem(lax.div(index, step), 2)


def inner_plane(rank):
    return (rank == 1) | (rank == 2)


def greet(peers):
    barrier = pltpu.get_barrier_semaphore()
    for peer in peers:
        pl.semaphore_signal(barrier, inc=1, device_id=peer, device_id_type=MESH)
    pl.semaphore_wait(barrier, len(peers))


def line_peers(rank):
    return [{"tensor": across(rank, k)} for k in (1, 2, 3)]


class LineGather:
    def __init__(self, rank, view, pieces, send_sems, recv_sems):
        self.rank, self.view, self.pieces = rank, view, pieces
        self.send_sems, self.recv_sems = send_sems, recv_sems
        self.inner = inner_plane(rank)

    @staticmethod
    def sems(pieces):
        return [DMA((4, pieces)), DMA((RANKS, pieces))]

    def copy(self, source, piece, k, slot):
        return pltpu.make_async_remote_copy(
            src_ref=self.view(source, piece), dst_ref=self.view(source, piece),
            send_sem=self.send_sems.at[slot, piece], recv_sem=self.recv_sems.at[source, piece],
            device_id={"tensor": across(self.rank, k)}, device_id_type=MESH,
        )

    def start(self, piece):
        self.copy(self.rank, piece, 2, 0).start()
        self.copy(self.rank, piece, 1, 1).start()
        pl.when(self.inner)(lambda: self.copy(self.rank, piece, 3, 2).start())

    def arrive(self, k, piece):
        source = across(self.rank, k)
        self.copy(source, piece, 1, 3).wait_recv()
        if k == 2:
            pl.when(self.inner)(lambda: self.copy(source, piece, 1, 3).start())

    def finish(self):
        for piece in range(self.pieces):
            self.copy(self.rank, piece, 2, 0).wait_send()
            self.copy(self.rank, piece, 1, 1).wait_send()

        @pl.when(self.inner)
        def _():
            for piece in range(self.pieces):
                self.copy(self.rank, piece, 3, 2).wait_send()
                self.copy(across(self.rank, 2), piece, 1, 3).wait_send()


def local(source, target, sem):
    return pltpu.make_async_copy(source, target, sem)


class LineScatter:
    def __init__(self, rank, parts, inbox, send_sems, recv_sems, pieces):
        self.rank, self.parts, self.inbox, self.pieces = rank, parts, inbox, pieces
        self.send_sems, self.recv_sems = send_sems, recv_sems
        self.inner = inner_plane(rank)
        self.end = (rank == 0) | (rank == 3)
        self.rows = parts.shape[1] // pieces

    @staticmethod
    def sems(pieces):
        return [DMA((4, pieces)), DMA((4, pieces))]

    def where(self, piece):
        return pl.ds(piece * self.rows, self.rows)

    def copy(self, part, slot, k, piece):
        return pltpu.make_async_remote_copy(
            src_ref=self.parts.at[part, self.where(piece)], dst_ref=self.inbox.at[slot, self.where(piece)],
            send_sem=self.send_sems.at[part, piece], recv_sem=self.recv_sems.at[slot, piece],
            device_id={"tensor": across(self.rank, k)}, device_id_type=MESH,
        )

    def send_far(self):
        for piece in range(self.pieces):
            pl.when(self.inner)(lambda: self.copy(3, 3, 3, piece).start())
            pl.when(self.end)(lambda: self.copy(3, 0, 1, piece).start())

    def send_two_end(self):
        @pl.when(self.end)
        def _():
            for piece in range(self.pieces):
                self.copy(2, 2, 2, piece).start()

    def send_two_inner(self):
        @pl.when(self.inner)
        def _():
            for piece in range(self.pieces):
                where = self.where(piece)
                self.copy(3, 0, 1, piece).wait_recv()
                self.parts[2, where] = (self.parts[2, where].astype(F32) + self.inbox[0, where].astype(F32)).astype(BF)
                self.copy(2, 2, 2, piece).start()

    def send_near(self):
        for piece in range(self.pieces):
            self.copy(1, 1, 1, piece).start()

    def total(self, target):
        for piece in range(self.pieces):
            where = self.where(piece)
            self.copy(1, 1, 1, piece).wait_recv()
            self.copy(2, 2, 2, piece).wait_recv()
            target[where] = (self.parts[0, where].astype(F32) + self.inbox[1, where].astype(F32)) + self.inbox[2, where].astype(F32)

        @pl.when(self.inner)
        def _():
            for piece in range(self.pieces):
                where = self.where(piece)
                self.copy(3, 3, 3, piece).wait_recv()
                target[where] += self.inbox[3, where].astype(F32)

    def finish(self):
        for piece in range(self.pieces):
            for part in (1, 2, 3):
                self.copy(part, part, part, piece).wait_send()


class GroupReduce:
    def __init__(self, group, dp, send, keep, first, boxes, split, sems):
        self.group, self.dp, self.send, self.keep, self.first, self.boxes = group, dp, send, keep, first, boxes
        self.bits = dp.bit_length() - 1
        self.mates = dp // 2
        columns = first.shape[3]
        self.cols = (pl.ds(0, split), pl.ds(split, columns - split))
        self.sems = sems

    @staticmethod
    def sem_shapes(dp, count):
        mates, bits = dp // 2, dp.bit_length() - 1
        shapes = [DMA((count, mates)), DMA((count, mates))]
        for t in range(1, bits):
            shapes += [DMA((2, count, mates >> t)), DMA((2, count, mates >> t))]
        return shapes

    @staticmethod
    def box_shapes(dp, count, share, columns, split):
        mates, bits = dp // 2, dp.bit_length() - 1
        shapes = [pltpu.VMEM((count, mates, share, columns), BF)]
        for t in range(1, bits):
            shapes += [pltpu.VMEM((count, mates >> t, share, split), BF), pltpu.VMEM((count, mates >> t, share, columns - split), BF)]
        return shapes

    def peers(self):
        return [{"dp": flip(self.group, b)} for b in range(self.bits)]

    def bit(self, b):
        return lax.rem(lax.div(self.group, 2**b), 2)

    def copy0(self, w, j):
        return pltpu.make_async_remote_copy(
            src_ref=self.send(w, 2 * j + 1 - self.bit(0)), dst_ref=self.first.at[w, j],
            send_sem=self.sems[0].at[w, j], recv_sem=self.sems[1].at[w, j],
            device_id={"dp": flip(self.group, 0)}, device_id_type=MESH)

    def place(self, t, half, j, mine):
        n = self.bits
        if half == 0:
            low = sum((self.bit(i) * 2 ** (i - 1) for i in range(1, t)), 0)
            bit = self.bit(t)
            return (2 * j + (bit if mine else 1 - bit)) * 2 ** (t - 1) + low
        high = sum((self.bit(n - i) * 2 ** (n - 1 - i) for i in range(1, t)), 0)
        bit = self.bit(n - t)
        return high + (bit if mine else 1 - bit) * 2 ** (n - 1 - t) + j

    def copy(self, t, half, w, j):
        return pltpu.make_async_remote_copy(
            src_ref=self.keep(w, self.place(t, half, j, False)).at[:, self.cols[half]], dst_ref=self.boxes[2 * (t - 1) + half].at[w, j],
            send_sem=self.sems[2 * t].at[half, w, j], recv_sem=self.sems[2 * t + 1].at[half, w, j],
            device_id={"dp": flip(self.group, t if half == 0 else self.bits - t)}, device_id_type=MESH)

    def start0(self, w):
        for j in range(self.mates):
            self.copy0(w, j).start()

    def start(self, t, w):
        for j in range(self.mates >> t):
            for half in range(2):
                self.copy(t, half, w, j).start()

    def add0(self, w):
        def body(j, carry):
            self.copy0(w, j).wait_recv()
            mine = self.keep(w, j)
            mine[...] = (mine[...].astype(F32) + self.first[w, j].astype(F32)).astype(BF)
            return carry

        lax.fori_loop(0, self.mates, body, 0)
        self.start(1, w)

    def add(self, t, w, target=None):
        for half in range(2):
            def body(j, carry):
                self.copy(t, half, w, j).wait_recv()
                mine = self.keep(w, self.place(t, half, j, True)).at[:, self.cols[half]]
                value = mine[...].astype(F32) + self.boxes[2 * (t - 1) + half][w, j].astype(F32)
                if target is None:
                    mine[...] = value.astype(BF)
                else:
                    target[:, self.cols[half]] = value.astype(target.dtype)
                return carry

            lax.fori_loop(0, self.mates >> t, body, 0)
        if target is None:
            self.start(t + 1, w)

    def finish(self, count):
        def body(w, carry):
            for j in range(self.mates):
                self.copy0(w, j).wait_send()
            for t in range(1, self.bits):
                for j in range(self.mates >> t):
                    for half in range(2):
                        self.copy(t, half, w, j).wait_send()
            return carry

        lax.fori_loop(0, count, body, 0)


def rope_numpy(length):
    half = HD // 2
    frequency = np.float32(10000.0) ** (-np.arange(half, dtype=np.float32) / np.float32(half))
    angles = np.arange(length, dtype=np.float32)[:, None] * frequency[None, :]
    cosine, sine = np.cos(angles), np.sin(angles)
    return (np.concatenate([cosine, cosine], 1), np.concatenate([-sine, sine], 1))


def column_of(row, target):
    target[...] = jnp.transpose(jnp.broadcast_to(row.astype(F32), (HD, row.shape[1])))


def forward_body(dp, tok, cot, seg, wo, wq, wk, wv, gain, gain2, cosine, sine,
                 a1_out, q_out, k_out, v_out, wo_out, cot_out, p_out, dy_out, a2_out, h_out, ob_out,
                 xs, a1s, qkv, ws, wos, dys, obs, ps, hs, segs,
                 x_ss, x_rs, z_ss, z_rs, d_ss, d_rs, c_ss, y_ss, y_rs, o_ss, o_rs, l_sem, k_sem):
    rank, group = lax.axis_index("tensor"), lax.axis_index("dp")
    rows, model = tok.shape
    length, width = q_out.shape
    heads = width // HD
    scale = HD ** (-0.5)
    half_rows = rows // 2
    parts = wo.shape[0]
    mates = parts // 2
    member = lax.rem(group, parts)
    base = group - member
    parity = lax.rem(member, 2)
    pair = lax.div(member, 2)
    partner = flip(group, 0)

    def mate(step):
        return lax.rem(pair + step, mates) * 2 + parity

    first = [local(wo.at[member], wos.at[rank, member], l_sem.at[0]), local(tok, xs.at[rank], l_sem.at[1]), local(cot, dys.at[rank], l_sem.at[2])]
    weights = [local(w, ws.at[i], l_sem.at[3 + i]) for i, w in enumerate((wq, wk, wv))]
    for c in first + weights:
        c.start()
    column_of(seg[...], segs)
    greet(line_peers(rank) + [{"dp": partner}] + [{"dp": base + mate(s)} for s in range(1, mates)])
    out_gather = LineGather(rank, lambda s, p: wos.at[s, member], 1, z_ss, z_rs)
    gather = LineGather(rank, lambda s, p: xs.at[s, pl.ds(p * half_rows, half_rows)], 2, x_ss, x_rs)
    grads = LineGather(rank, lambda s, p: dys.at[s, pl.ds(p * half_rows, half_rows)], 2, y_ss, y_rs)
    attended = LineGather(rank, lambda s, p: obs.at[s, :, pl.ds(pl.multiple_of(p * HD, HD), HD)], heads, o_ss, o_rs)
    first[0].wait()
    out_gather.start(0)
    first[1].wait()
    gather.start(0)
    gather.start(1)
    first[2].wait()
    real = segs[pl.ds(pl.multiple_of(rank * rows, rows), rows), :1] >= 0.0
    dys[rank] = jnp.where(real, dys[rank], jnp.zeros((rows, model), BF))
    grads.start(0)
    grads.start(1)
    keep = [local(dys.at[rank], cot_out, k_sem.at[0])]
    keep[0].start()
    for w in weights:
        w.wait()

    def chunk(source):
        x = xs[source].astype(F32)
        a1s[source] = (x * norm_factor(x) * gain[...].reshape(1, model)).astype(BF)
        where = pl.ds(pl.multiple_of(source * rows, rows), rows)
        for i in range(3):
            product = dot(a1s[source], ws[i])
            for h in range(heads):
                head = product[:, h * HD : (h + 1) * HD]
                if i < 2:
                    head = head * cosine[where, :] + pltpu.roll(head, HD // 2, 1) * sine[where, :]
                qkv[i, where, h * HD : (h + 1) * HD] = head.astype(BF)

    def chunks(i, carry):
        @pl.when(i == 1)
        def _():
            for k in (1, 2, 3):
                out_gather.arrive(k, 0)
            for step in range(1, mates):
                mate_copy(step).start()
            core_copy(0, parity).start()
            for piece in range(2):
                gather.arrive(1, piece)
                gather.arrive(2, piece)

        @pl.when(i == 3)
        def _():
            for step in range(1, mates):
                mate_arrival(step).wait_recv()
                core_copy(step, parity).start()
            for piece in range(2):
                gather.arrive(3, piece)

        chunk(pick(i, [rank, across(rank, 1), across(rank, 2), across(rank, 3)]))
        return carry

    def mate_copy(step):
        return pltpu.make_async_remote_copy(
            src_ref=wos.at[:, member], dst_ref=wos.at[:, member], send_sem=d_ss.at[step], recv_sem=d_rs.at[member],
            device_id={"dp": base + mate(step)}, device_id_type=MESH)

    def mate_arrival(step):
        piece = mate(step)
        return pltpu.make_async_remote_copy(
            src_ref=wos.at[:, piece], dst_ref=wos.at[:, piece], send_sem=d_ss.at[step], recv_sem=d_rs.at[piece],
            device_id={"dp": base + piece}, device_id_type=MESH)

    def core_copy(step, owner):
        piece = lax.rem(pair + step, mates) * 2 + owner
        return pltpu.make_async_remote_copy(
            src_ref=wos.at[:, piece], dst_ref=wos.at[:, piece], send_sem=c_ss.at[step], recv_sem=d_rs.at[piece],
            device_id={"dp": partner}, device_id_type=MESH)

    lax.fori_loop(0, RANKS, chunks, 0)
    keep += [local(a1s, a1_out, k_sem.at[1])] + [local(qkv.at[i], t, k_sem.at[2 + i]) for i, t in enumerate((q_out, k_out, v_out))]
    for c in keep[1:]:
        c.start()

    def head(h, carry):
        cols = pl.ds(pl.multiple_of(h * HD, HD), HD)
        for start in range(0, length, QB):
            extent = start + QB
            scores = dot(qkv[0, start:extent, cols], qkv[1, :extent, cols], ((1,), (1,)))
            row_ids = lax.broadcasted_iota(jnp.int32, (QB, extent), 0) + start
            col_ids = lax.broadcasted_iota(jnp.int32, (QB, extent), 1)
            allowed = (col_ids <= row_ids) & (segs[start:extent, :1] == seg[:, :extent].astype(F32))
            logits = jnp.where(allowed, scores * scale, NEG)
            expo = jnp.exp(logits - jnp.max(logits, axis=-1, keepdims=True))
            probs = (expo * (1.0 / jnp.sum(expo, axis=-1, keepdims=True))).astype(BF)
            ps[h, start:extent, :extent] = probs
            obs[rank, start:extent, cols] = dot(probs, qkv[2, :extent, cols]).astype(BF)
        attended.start(h)
        return carry

    lax.fori_loop(0, heads, head, 0)
    for step in range(mates):
        core_copy(step, 1 - parity).wait_recv()
    more = [local(ps, p_out, k_sem.at[5]), local(wos, wo_out, k_sem.at[6])]
    for c in more:
        c.start()
    keep += more

    def add(source, first=False, last=False):
        def block(b, carry):
            weight = wos[source].reshape(width, model)
            part = dot(obs[source, pl.ds(pl.multiple_of(b * rows, rows), rows), :], weight)
            total = part + (xs[b].astype(F32) if first else hs[b])
            hs[b] = total
            if last:
                xs[b] = (total * norm_factor(total) * gain2[...].reshape(1, model)).astype(BF)
            return carry

        lax.fori_loop(0, RANKS, block, 0)

    add(rank, first=True)
    for piece in range(2):
        grads.arrive(2, piece)
    for piece in range(heads):
        attended.arrive(2, piece)
    for piece in range(heads):
        attended.arrive(1, piece)
    add(across(rank, 2))
    add(across(rank, 1))
    for piece in range(2):
        grads.arrive(1, piece)
        grads.arrive(3, piece)
    more = [local(dys, dy_out, l_sem.at[0])]
    more[0].start()
    for piece in range(heads):
        attended.arrive(3, piece)
    gather.finish()
    add(across(rank, 3), last=True)
    more += [local(xs, a2_out, l_sem.at[1]), local(hs.at[rank], h_out, l_sem.at[2]),
             local(obs.at[:, pl.ds(pl.multiple_of(rank * rows, rows), rows)], ob_out, l_sem.at[3])]
    for c in more[1:]:
        c.start()
    out_gather.finish()
    for step in range(1, mates):
        mate_copy(step).wait_send()
    for step in range(mates):
        core_copy(step, parity).wait_send()
    grads.finish()
    attended.finish()
    for c in keep + more:
        c.wait()


def forward_kernel(dp, tokens, cotangent, segments, w_out, w_query, w_key, w_value, gain, gain2, cosine, sine):
    rows, model = tokens.shape
    width = w_query.shape[1]
    heads = width // HD
    length = RANKS * rows
    parts = min(dp, 8)
    mates = parts // 2
    shape = (RANKS, rows, model)
    shard, wide = jax.ShapeDtypeStruct(shape, BF), jax.ShapeDtypeStruct((length, width), BF)
    outs = pl.pallas_call(
        functools.partial(forward_body, dp),
        in_specs=[ANY, ANY, VM, ANY, ANY, ANY, ANY, VM, VM, VM, VM],
        out_specs=[ANY] * 11,
        out_shape=[shard, wide, wide, wide, jax.ShapeDtypeStruct((RANKS, parts, width // parts, model), BF),
                   jax.ShapeDtypeStruct((rows, model), BF), jax.ShapeDtypeStruct((heads, length, length), BF), shard, shard,
                   jax.ShapeDtypeStruct((rows, model), F32), jax.ShapeDtypeStruct((RANKS, rows, width), BF)],
        scratch_shapes=[
            pltpu.VMEM(shape, BF), pltpu.VMEM(shape, BF), pltpu.VMEM((3, length, width), BF), pltpu.VMEM((3, model, width), BF),
            pltpu.VMEM((RANKS, parts, width // parts, model), BF), pltpu.VMEM(shape, BF), pltpu.VMEM((RANKS, length, width), BF),
            pltpu.VMEM((heads, length, length), BF), pltpu.VMEM(shape, F32), pltpu.VMEM((length, HD), F32),
            *LineGather.sems(2), *LineGather.sems(1), DMA((mates,)), DMA((parts,)), DMA((mates,)),
            *LineGather.sems(2), *LineGather.sems(heads), DMA((6,)), DMA((7,)),
        ],
        compiler_params=pltpu.CompilerParams(collective_id=1, has_side_effects=True, vmem_limit_bytes=62 << 20),
        name="forward_gather",
    )(tokens, cotangent, segments, w_out.reshape(parts, width // parts, model), w_query, w_key, w_value, gain, gain2, cosine, sine)
    a1_all, query, key, value, w_out_all, cot_own, probs, dy, a2, hidden, attended = outs
    return a1_all, query, key, value, w_out_all.reshape(RANKS, width, model), cot_own, probs, dy, a2, hidden, attended


def pick(step, choices):
    value = choices[-1]
    for i in range(len(choices) - 1):
        value = jnp.where(step == i, choices[i], value)
    return value


FT = 768
WB = 384


def mlp_body(a2, dy, wg, wu, wd, hid, cot, gran, gain,
             g_out, down_out, dh_out, gain_out,
             lefts, acts, ws, parts, inbox, stage, downs, hs, cots, total, gains, r_ss, r_rs, l_sem, s_sem):
    rank = lax.axis_index("tensor")
    rows, model = cot.shape
    width = wg.shape[1]
    per, share = stage.shape[1], stage.shape[2]
    loads = [local(wg, ws.at[0], l_sem.at[0]), local(a2, lefts.at[0], l_sem.at[1]), local(wu, ws.at[1], l_sem.at[2]),
             local(dy, lefts.at[1], l_sem.at[3]), local(wd, ws.at[2], l_sem.at[4])]
    late = [local(hid, hs, l_sem.at[5]), local(cot, cots, l_sem.at[6])]
    for c in loads + late:
        c.start()
    greet(line_peers(rank))
    scatter = LineScatter(rank, parts, inbox, r_ss, r_rs, 2)
    order = [across(rank, k) for k in (3, 2, 1, 0)]
    limit = FF // 8 * lax.shift_left(1, gran[0] - 1) - rank * width

    def step(i, carry):
        j = pick(i, order)

        def tile(t, inner_carry):
            cols = pl.ds(pl.multiple_of(t * FT, FT), FT)

            @pl.when((i == 0) & (t == 0))
            def _():
                loads[0].wait()
                loads[1].wait()

            gate = dot(lefts[0, j], ws[0, :, cols])

            @pl.when((i == 0) & (t == 0))
            def _():
                loads[2].wait()

            up = dot(lefts[0, j], ws[1, :, cols])

            @pl.when((i == 0) & (t == 0))
            def _():
                loads[3].wait()
                loads[4].wait()

            dz = dot(lefts[1, j], ws[2, cols, :], ((1,), (1,)))
            unit = lax.broadcasted_iota(jnp.int32, gate.shape, 1) + t * FT
            mask = unit < limit
            sigma = jax.nn.sigmoid(gate)
            active = jnp.where(mask, gate * sigma, 0.0)
            acts[2, j, :, cols] = (active * up).astype(BF)
            acts[0, j, :, cols] = jnp.where(mask, dz * up * sigma * (1.0 + gate * (1.0 - sigma)), 0.0).astype(BF)
            acts[1, j, :, cols] = (dz * active).astype(BF)
            return inner_carry

        lax.fori_loop(0, width // FT, tile, 0)

        def back(t, inner_carry):
            cols = pl.ds(pl.multiple_of(t * FT, FT), FT)
            parts[3 - i, :, cols] = (
                dot(acts[0, j], ws[0, cols, :], ((1,), (1,))) + dot(acts[1, j], ws[1, cols, :], ((1,), (1,)))
            ).astype(BF)
            return inner_carry

        lax.fori_loop(0, model // FT, back, 0)
        pl.when(i == 0)(scatter.send_far)
        pl.when(i == 1)(scatter.send_two_end)

        @pl.when(i == 2)
        def _():
            scatter.send_near()
            scatter.send_two_inner()

        return carry

    lax.fori_loop(0, 4, step, 0)
    blocks = model // WB

    def put(i, slot):
        w, b = lax.div(i, blocks), lax.rem(i, blocks)
        return local(stage.at[slot], g_out.at[w, pl.ds(b * per, per)], s_sem.at[slot])

    def grads(i, carry):
        slot = lax.rem(i, 2)
        w, b = lax.div(i, blocks), lax.rem(i, blocks)
        left = lax.div(w, 2)
        cols = pl.ds(pl.multiple_of(b * WB, WB), WB)
        value = dot(lefts[left, 0, :, cols], acts[w, 0], ((0,), (0,)))
        for s in range(1, RANKS):
            value += dot(lefts[left, s, :, cols], acts[w, s], ((0,), (0,)))
        pl.when(i >= 2)(lambda: put(i - 2, slot).wait())
        low = value.astype(BF)
        for p in range(per):
            stage[slot, p] = low[p * share : (p + 1) * share]
        put(i, slot).start()
        return carry

    lax.fori_loop(0, 3 * blocks, grads, 0)

    def down(i, carry):
        downs[3 - i] = dot(acts[2, pick(i, order)], ws[2]).astype(BF)
        return carry

    lax.fori_loop(0, 4, down, 0)
    keep = local(downs, down_out, l_sem.at[0])
    keep.start()
    for c in late:
        c.wait()
    scatter.total(total)
    values, gradient = hs[...], total[...]
    factor = norm_factor(values)
    back_rows, gain_rows = norm_back(values, factor, gain[...].reshape(1, model), gradient)
    total[...] = cots[...].astype(F32) + back_rows
    gains[...] = gain_rows.reshape(1, model)
    last = [local(total, dh_out, l_sem.at[1]), local(gains, gain_out, l_sem.at[2])]
    for c in last:
        c.start()
    scatter.finish()
    put(3 * blocks - 2, 0).wait()
    put(3 * blocks - 1, 1).wait()
    for c in last + [keep]:
        c.wait()


def mlp_kernel(dp, a2, dy, w_gate, w_up, w_down, hidden_own, cot_own, granularity, gain):
    rows, model = cot_own.shape
    width = w_gate.shape[1]
    share = model // dp
    shard = (RANKS, rows, model)
    return pl.pallas_call(
        mlp_body,
        in_specs=[ANY] * 7 + [pl.BlockSpec(memory_space=pltpu.SMEM), VM],
        out_specs=[ANY] * 4,
        out_shape=[jax.ShapeDtypeStruct((3, dp, share, width), BF), jax.ShapeDtypeStruct(shard, BF),
                   jax.ShapeDtypeStruct((rows, model), F32), jax.ShapeDtypeStruct((1, model), F32)],
        scratch_shapes=[
            pltpu.VMEM((2, *shard), BF), pltpu.VMEM((3, RANKS, rows, width), BF), pltpu.VMEM((3, model, width), BF),
            pltpu.VMEM(shard, BF), pltpu.VMEM(shard, BF), pltpu.VMEM((2, WB // share, share, width), BF), pltpu.VMEM(shard, BF),
            pltpu.VMEM((rows, model), F32), pltpu.VMEM((rows, model), BF), pltpu.VMEM((rows, model), F32), pltpu.VMEM((1, model), F32),
            *LineScatter.sems(2), DMA((7,)), DMA((2,)),
        ],
        compiler_params=pltpu.CompilerParams(collective_id=3, has_side_effects=True, vmem_limit_bytes=63 << 20),
        name="mlp_scatter",
    )(a2, dy, w_gate, w_up, w_down, hidden_own, cot_own, granularity, gain)


def attention_back_body(dp, dh, wo_all, downs, grads, q, k, v, p_all, hid, cosine, sine,
                        out_out, dq_out, dk_out, dv_out, gf_out,
                        dhs, low, wos, parts, inbox, dobs, dos, qkv, ps, ds, dqkv, hs, outs, kept, finals, *rest):
    rank, group = lax.axis_index("tensor"), lax.axis_index("dp")
    rounds = 2 * (dp.bit_length() - 1)
    first, boxes, rest = rest[0], rest[1 : rounds - 1], rest[rounds - 1 :]
    sems, (r_ss, r_rs, a_ss, a_rs, l_sem, p_sem, f_sem) = rest[:rounds], rest[rounds:]
    rows, model = dh.shape
    length, width = q.shape
    heads, half, scale = width // HD, HD // 2, HD ** (-0.5)
    count = grads.shape[0]
    parity = lax.rem(group, 2)
    loads = [local(dh, dhs, l_sem.at[0]), local(wo_all, wos, l_sem.at[1]), local(downs, parts, l_sem.at[2])]
    owns = [local(grads.at[w, :, parity], kept.at[w], f_sem.at[w]) for w in range(count)]
    late = [local(t, qkv.at[i], l_sem.at[3 + i]) for i, t in enumerate((q, k, v))] + [local(hid, hs, l_sem.at[6])]
    for c in loads + owns + late:
        c.start()

    def probs(h):
        return local(p_all.at[h], ps.at[lax.rem(h, 2)], p_sem.at[lax.rem(h, 2)])

    probs(0).start()
    probs(1).start()
    reduce = GroupReduce(
        group, dp, lambda w, d: grads.at[w, lax.div(d, 2), lax.rem(d, 2)], lambda w, j: kept.at[w, j], first, boxes, model // 2, sems)
    greet(line_peers(rank) + reduce.peers())
    for w in range(count):
        reduce.start0(w)
    scatter = LineScatter(rank, parts, inbox, r_ss, r_rs, 2)

    def exchange(k, source):
        where = pl.ds(pl.multiple_of(source * rows, rows), rows)
        return pltpu.make_async_remote_copy(
            src_ref=dobs.at[k - 1], dst_ref=dos.at[where], send_sem=a_ss.at[k], recv_sem=a_rs.at[source],
            device_id={"tensor": across(rank, k)}, device_id_type=MESH)

    loads[0].wait()
    low[...] = dhs[...].astype(BF)
    loads[1].wait()
    for k in (3, 2, 1):
        dobs[k - 1] = dot(low[...], wos[across(rank, k)], ((1,), (1,))).astype(BF)
        exchange(k, rank).start()
    dos[pl.ds(pl.multiple_of(rank * rows, rows), rows), :] = dot(low[...], wos[rank], ((1,), (1,))).astype(BF)
    loads[2].wait()
    scatter.send_far()
    scatter.send_two_end()
    scatter.send_near()
    for c in owns:
        c.wait()

    def fold(w, carry):
        reduce.add0(w)
        return carry

    lax.fori_loop(0, count, fold, 0)
    for c in late:
        c.wait()
    for k in (3, 2, 1):
        exchange(k, across(rank, k)).wait_recv()

    def head(h, carry):
        cols = pl.ds(pl.multiple_of(h * HD, HD), HD)
        slot = lax.rem(h, 2)
        probs(h).wait()

        def unrope(grad, start):
            where = slice(start, start + QB)
            return (grad * cosine[where, :] - pltpu.roll(grad, half, 1) * sine[where, :]).astype(BF)

        for start in range(0, length, QB):
            extent = start + QB
            where = slice(start, extent)
            grad_p = dot(dos[where, cols], qkv[2, :extent, cols], ((1,), (1,)))
            p = ps[slot, where, :extent].astype(F32)
            weighted = p * grad_p
            delta = jnp.sum(weighted, axis=-1, keepdims=True)
            ds[where, :extent] = ((weighted - p * delta) * scale).astype(BF)
            dqkv[0, where, cols] = unrope(dot(ds[where, :extent], qkv[1, :extent, cols]), start)
        for start in range(0, length, QB):
            where = slice(start, start + QB)
            dqkv[1, where, cols] = unrope(dot(ds[start:, where], qkv[0, start:, cols], ((0,), (0,))), start)
            dqkv[2, where, cols] = dot(ps[slot, start:, where], dos[start:, cols], ((0,), (0,))).astype(BF)
        pl.when(h + 2 < heads)(lambda: probs(h + 2).start())
        return carry

    lax.fori_loop(0, heads, head, 0)
    done = [local(dqkv.at[i], t, l_sem.at[i]) for i, t in enumerate((dq_out, dk_out, dv_out))]
    for c in done:
        c.start()
    reduce.add(1, 0)
    scatter.send_two_inner()
    reduce.add(1, 1)
    reduce.add(1, 2)
    for t in range(2, reduce.bits - 1):
        for w in range(count):
            reduce.add(t, w)

    def put(w):
        return local(finals.at[w], gf_out.at[w], f_sem.at[w])

    for w in range(count):
        reduce.add(reduce.bits - 1, w, finals.at[w])
        put(w).start()
    scatter.total(dhs)
    outs[...] = (hs[...] + dhs[...]).astype(BF)
    last = local(outs, out_out, l_sem.at[3])
    last.start()
    scatter.finish()
    for k in (1, 2, 3):
        exchange(k, rank).wait_send()
    reduce.finish(count)
    for w in range(count):
        put(w).wait()
    for c in done + [last]:
        c.wait()


def attention_back_kernel(dp, grad_hidden, w_out_all, down_parts, grads_ff, query, key, value, probs_low, hidden_own, cosine, sine):
    rows, model = grad_hidden.shape
    length, width = query.shape
    count, _, share, columns = grads_ff.shape
    mates = dp // 2
    shard = (RANKS, rows, model)
    heads = jax.ShapeDtypeStruct((length, width), BF)
    return pl.pallas_call(
        functools.partial(attention_back_body, dp),
        in_specs=[ANY] * 9 + [VM, VM],
        out_specs=[ANY] * 5,
        out_shape=[jax.ShapeDtypeStruct((rows, model), BF), heads, heads, heads, jax.ShapeDtypeStruct((count, share, columns), BF)],
        scratch_shapes=[
            pltpu.VMEM((rows, model), F32), pltpu.VMEM((rows, model), BF), pltpu.VMEM((RANKS, width, model), BF),
            pltpu.VMEM(shard, BF), pltpu.VMEM(shard, BF), pltpu.VMEM((3, rows, width), BF), pltpu.VMEM((length, width), BF),
            pltpu.VMEM((3, length, width), BF), pltpu.VMEM((2, length, length), BF), pltpu.VMEM((length, length), BF),
            pltpu.VMEM((3, length, width), BF), pltpu.VMEM((rows, model), F32), pltpu.VMEM((rows, model), BF),
            pltpu.VMEM((count, mates, share, columns), BF), pltpu.VMEM((count, share, columns), BF),
            *GroupReduce.box_shapes(dp, count, share, columns, columns // 2), *GroupReduce.sem_shapes(dp, count),
            *LineScatter.sems(2), DMA((4,)), DMA((RANKS,)), DMA((7,)), DMA((2,)), DMA((count,)),
        ],
        compiler_params=pltpu.CompilerParams(collective_id=4, has_side_effects=True, vmem_limit_bytes=63 << 20),
        name="attention_back",
    )(grad_hidden, w_out_all, down_parts, grads_ff.reshape(count, mates, 2, share, columns),
      query, key, value, probs_low, hidden_own, cosine, sine)


def input_back_body(dp, dq, dk, dv, a1, wq, wk, wv, tok, dh, ob, gain, gain2,
                    dx_out, gains_out, gqkv_out, gout_out,
                    dqkv, a1s, ws, xs, dhs, low, obs, parts, inbox, g1, g2, f1, f2, f2_low, box2, f3, gbuf, gbox, total, dxs, *rest):
    rank, group = lax.axis_index("tensor"), lax.axis_index("dp")
    bits = dp.bit_length() - 1
    boxes = [rest[: 2 * bits - 1], rest[2 * bits - 1 : 4 * bits - 2]]
    rest = rest[4 * bits - 2 :]
    sems = [rest[: 2 * bits], rest[2 * bits : 4 * bits]]
    r_ss, r_rs, z_ss, z_rs, g_ss, g_rs, l_sem = rest[4 * bits :]
    rows, model = tok.shape
    width = dq.shape[1]
    share = g1.shape[1]
    per = WB // share
    parity = lax.rem(group, 2)
    loads = [local(t, dqkv.at[i], l_sem.at[i]) for i, t in enumerate((dq, dk, dv))]
    loads += [local(t, ws.at[i], l_sem.at[3 + i]) for i, t in enumerate((wq, wk, wv))]
    late = [local(dh, dhs, l_sem.at[6]), local(ob, obs, l_sem.at[7]), local(a1, a1s, l_sem.at[8]), local(tok, xs, l_sem.at[9])]
    for c in loads + late:
        c.start()
    scatter = LineScatter(rank, parts, inbox, r_ss, r_rs, 2)
    mixed = GroupReduce(group, dp, lambda w, d: g1.at[d], lambda w, j: g1.at[2 * j + parity], boxes[0][0], boxes[0][1:], f1.shape[1] // 256 * 128, sems[0])
    output = GroupReduce(group, dp, lambda w, d: g2.at[d], lambda w, j: g2.at[2 * j + parity], boxes[1][0], boxes[1][1:], f2.shape[1] // 256 * 128, sems[1])
    greet(line_peers(rank) + mixed.peers())
    order = [across(rank, k) for k in (3, 2, 1, 0)]
    for c in loads:
        c.wait()

    def step(i, carry):
        where = pl.ds(pl.multiple_of(pick(i, order) * rows, rows), rows)
        value = dot(dqkv[0, where, :], ws[0], ((1,), (1,)))
        for s in (1, 2):
            value += dot(dqkv[s, where, :], ws[s], ((1,), (1,)))
        parts[3 - i] = value.astype(BF)
        pl.when(i == 0)(scatter.send_far)
        pl.when(i == 1)(scatter.send_two_end)
        pl.when(i == 2)(scatter.send_near)
        return carry

    lax.fori_loop(0, 4, step, 0)
    for c in late:
        c.wait()
    low[...] = dhs[...].astype(BF)

    def out_block(b, carry):
        cols = pl.ds(pl.multiple_of(b * WB, WB), WB)
        for r in range(RANKS):
            value = dot(low[:, cols], obs[r], ((0,), (0,))).astype(BF)
            for p in range(per):
                g2[b * per + p, :, r * width : (r + 1) * width] = value[p * share : (p + 1) * share]
        return carry

    lax.fori_loop(0, model // WB, out_block, 0)
    output.start0(0)

    def mixed_block(b, carry):
        cols = pl.ds(pl.multiple_of(b * WB, WB), WB)
        for s in range(3):
            value = dot(a1s[:, cols], dqkv[s], ((0,), (0,))).astype(BF)
            for p in range(per):
                g1[b * per + p, :, s * width : (s + 1) * width] = value[p * share : (p + 1) * share]
        return carry

    lax.fori_loop(0, model // WB, mixed_block, 0)
    mixed.start0(0)
    output.add0(0)
    mixed.add0(0)
    scatter.send_two_inner()
    for t in range(1, bits - 1):
        output.add(t, 0)
        mixed.add(t, 0)
    output.add(bits - 1, 0, f2)
    ends = LineScatter(rank, f2_low, box2, z_ss, z_rs, 1)
    for k in range(4):
        column = pl.ds(pl.multiple_of(across(rank, k) * width, HD), width)
        f2_low[k] = f2[:, column].astype(BF)
    ends.send_far()
    ends.send_two_end()
    ends.send_near()
    mixed.add(bits - 1, 0, f1)
    done = [local(f1, gqkv_out, l_sem.at[0])]
    done[0].start()
    scatter.total(total)
    values, gradient = xs[...].astype(F32), total[...]
    back_rows, gain_rows = norm_back(values, norm_factor(values), gain[...].reshape(1, model), gradient)
    dxs[...] = (dhs[...] + back_rows).astype(BF)
    done.append(local(dxs, dx_out, l_sem.at[1]))
    done[1].start()
    gbuf[0, 0:1, :] = gain_rows.reshape(1, model)
    gbuf[0, 1:2, :] = gain2[...]
    turns = [{"tensor": across(rank, 1)}, {"tensor": across(rank, 2)}] + [{"dp": flip(group, b)} for b in range(bits)]

    def swap(t):
        return pltpu.make_async_remote_copy(
            src_ref=gbuf.at[t], dst_ref=gbox.at[t], send_sem=g_ss.at[t], recv_sem=g_rs.at[t], device_id=turns[t], device_id_type=MESH)

    swap(0).start()
    ends.send_two_inner()
    for t in range(len(turns)):
        swap(t).wait_recv()
        gbuf[t + 1] = gbuf[t] + gbox[t]
        if t + 1 < len(turns):
            swap(t + 1).start()
    done.append(local(gbuf.at[len(turns)], gains_out, l_sem.at[2]))
    done[2].start()
    ends.total(f3)
    done.append(local(f3, gout_out, l_sem.at[3]))
    done[3].start()
    scatter.finish()
    ends.finish()
    mixed.finish(1)
    output.finish(1)
    for t in range(len(turns)):
        swap(t).wait_send()
    for c in done:
        c.wait()


def input_back_kernel(dp, grad_q, grad_k, grad_v, a1_all, w_query, w_key, w_value, tokens, grad_hidden, attended_own, gain, gain_two):
    rows, model = tokens.shape
    length, width = grad_q.shape
    share = model // dp
    bits = dp.bit_length() - 1
    shard = (RANKS, rows, model)
    wide = (3 * width, RANKS * width)
    splits = [w // 256 * 128 for w in wide]
    return pl.pallas_call(
        functools.partial(input_back_body, dp),
        in_specs=[ANY] * 10 + [VM, VM],
        out_specs=[ANY] * 4,
        out_shape=[jax.ShapeDtypeStruct((rows, model), BF), jax.ShapeDtypeStruct((2, model), F32),
                   jax.ShapeDtypeStruct((share, wide[0]), F32), jax.ShapeDtypeStruct((share, width), F32)],
        scratch_shapes=[
            pltpu.VMEM((3, length, width), BF), pltpu.VMEM((length, model), BF), pltpu.VMEM((3, model, width), BF),
            pltpu.VMEM((rows, model), BF), pltpu.VMEM((rows, model), F32), pltpu.VMEM((rows, model), BF), pltpu.VMEM((RANKS, rows, width), BF),
            pltpu.VMEM(shard, BF), pltpu.VMEM(shard, BF),
            pltpu.VMEM((dp, share, wide[0]), BF), pltpu.VMEM((dp, share, wide[1]), BF),
            pltpu.VMEM((share, wide[0]), F32), pltpu.VMEM((share, wide[1]), F32),
            pltpu.VMEM((RANKS, share, width), BF), pltpu.VMEM((RANKS, share, width), BF), pltpu.VMEM((share, width), F32),
            pltpu.VMEM((bits + 3, 2, model), F32), pltpu.VMEM((bits + 2, 2, model), F32),
            pltpu.VMEM((rows, model), F32), pltpu.VMEM((rows, model), BF),
            *GroupReduce.box_shapes(dp, 1, share, wide[0], splits[0]), *GroupReduce.box_shapes(dp, 1, share, wide[1], splits[1]),
            *GroupReduce.sem_shapes(dp, 1), *GroupReduce.sem_shapes(dp, 1),
            *LineScatter.sems(2), *LineScatter.sems(1), DMA((bits + 2,)), DMA((bits + 2,)), DMA((10,)),
        ],
        compiler_params=pltpu.CompilerParams(collective_id=5, has_side_effects=True, vmem_limit_bytes=63 << 20),
        name="input_back",
    )(grad_q, grad_k, grad_v, a1_all.reshape(length, model), w_query, w_key, w_value, tokens, grad_hidden, attended_own, gain, gain_two)


def finish_body(output, dx, gains, mixed, out_t, ff,
                output_out, dx_out, gain1_out, gain2_out, q_out, k_out, v_out, wo_out, gate_out, up_out, down_out,
                b0, b1, gs, g1, g2, ms, ot, fs, gate, up, down, i_sem, o_sem):
    width = q_out.shape[1]
    loads = [local(s, t, i_sem.at[i]) for i, (s, t) in enumerate(
        ((ff.at[2], fs.at[2]), (ff.at[0], fs.at[0]), (ff.at[1], fs.at[1]), (mixed, ms), (output, b0), (dx, b1), (out_t, ot), (gains, gs)))]
    for c in loads:
        c.start()
    sent = []

    def put(source, target):
        sent.append(local(source, target, o_sem.at[len(sent)]))
        sent[-1].start()

    loads[1].wait()
    gate[...] = fs[0].astype(F32)
    put(gate, gate_out)
    loads[2].wait()
    up[...] = fs[1].astype(F32)
    put(up, up_out)
    loads[4].wait()
    put(b0, output_out)
    loads[5].wait()
    put(b1, dx_out)
    loads[3].wait()
    for i, target in enumerate((q_out, k_out, v_out)):
        put(ms.at[:, pl.ds(i * width, width)], target)
    loads[0].wait()
    down[...] = fs[2].astype(F32)
    put(down, down_out)
    loads[6].wait()
    put(ot, wo_out)
    loads[7].wait()
    g1[...] = gs[0]
    put(g1, gain1_out)
    g2[...] = gs[1]
    put(g2, gain2_out)
    for c in sent:
        c.wait()


def finish_kernel(output, dx, gains, mixed, out_t, ff):
    rows, model = output.shape
    share, width = out_t.shape
    columns = ff.shape[2]
    gain, head, wide = ((model,), F32), ((share, width), F32), ((share, columns), F32)
    outs = [((rows, model), BF), ((rows, model), BF), gain, gain, head, head, head, head, wide, wide, wide]
    return pl.pallas_call(
        finish_body,
        in_specs=[ANY] * 6,
        out_specs=[ANY] * 11,
        out_shape=[jax.ShapeDtypeStruct(*o) for o in outs],
        scratch_shapes=[
            pltpu.VMEM((rows, model), BF), pltpu.VMEM((rows, model), BF), pltpu.VMEM((2, model), F32), pltpu.VMEM((model,), F32), pltpu.VMEM((model,), F32),
            pltpu.VMEM((share, 3 * width), F32), pltpu.VMEM((share, width), F32),
            pltpu.VMEM((3, share, columns), BF), pltpu.VMEM((share, columns), F32), pltpu.VMEM((share, columns), F32), pltpu.VMEM((share, columns), F32),
            DMA((8,)), DMA((11,)),
        ],
        compiler_params=pltpu.CompilerParams(vmem_limit_bytes=63 << 20),
        name="finish",
    )(output, dx, gains, mixed, out_t, ff)


def on_device(tokens, segments, granularity, norm1_gain, norm2_gain, w_query, w_key, w_value, w_out, w_gate, w_up, w_down, cotangent):
    length = segments.shape[1]
    cosine, sine = (jnp.asarray(t) for t in rope_numpy(length))
    dp = lax.axis_size("dp")
    a1_all, query_rot, key_rot, value_low, w_out_all, cot_own, probs_low, grad_rows, rows_two, hidden_own, attended_own = forward_kernel(
        dp, tokens, cotangent, segments, w_out, w_query, w_key, w_value, norm1_gain, norm2_gain, cosine, sine
    )
    grads_ff, down_parts, grad_hidden, gain_two = mlp_kernel(
        dp, rows_two, grad_rows, w_gate, w_up, w_down, hidden_own, cot_own, granularity, norm2_gain
    )
    output, grad_q, grad_k, grad_v, own_ff = attention_back_kernel(
        dp, grad_hidden, w_out_all, down_parts, grads_ff, query_rot, key_rot, value_low, probs_low, hidden_own, cosine, sine
    )
    grad_tokens, gains, own_qkv, own_out = input_back_kernel(
        dp, grad_q, grad_k, grad_v, a1_all, w_query, w_key, w_value, tokens, grad_hidden, attended_own, norm1_gain, gain_two
    )
    outs = finish_kernel(output, grad_tokens, gains, own_qkv, own_out, own_ff)
    return tuple(o.T if i in (7, 10) else o for i, o in enumerate(outs))


def solution(mesh):
    in_specs = (
        P(("dp", "tensor"), None), P("dp", None), P("dp"), P(), P(),
        P(None, "tensor"), P(None, "tensor"), P(None, "tensor"), P("tensor", None),
        P(None, "tensor"), P(None, "tensor"), P("tensor", None), P(("dp", "tensor"), None),
    )
    out_specs = (
        P(("dp", "tensor"), None), P(("dp", "tensor"), None), P(), P(),
        P("dp", "tensor"), P("dp", "tensor"), P("dp", "tensor"), P("tensor", "dp"),
        P("dp", "tensor"), P("dp", "tensor"), P("tensor", "dp"),
    )
    return jax.shard_map(on_device, mesh=mesh, in_specs=in_specs, out_specs=out_specs, check_vma=False)
```

```python
import functools

import jax
import jax.numpy as jnp
import numpy as np
from jax import lax
from jax.experimental import pallas as pl
from jax.experimental.pallas import tpu as pltpu
from jax.sharding import PartitionSpec as P

HD = 128
FF = 6144
EPS = 1e-06
NEG = -1e30
BF = jnp.bfloat16
F32 = jnp.float32
QB = 256


def norm_factor(values):
    return lax.rsqrt(jnp.mean(values * values, axis=-1, keepdims=True) + EPS)


def norm_back(values, factor, row_gain, gradient):
    scaled = gradient * row_gain
    inner_mean = jnp.mean(scaled * values, axis=-1, keepdims=True)
    back_rows = factor * scaled - values * (factor * factor * factor) * inner_mean
    return (back_rows, jnp.sum(gradient * values * factor, axis=0))


def dot(left, right, dims=((1,), (0,))):
    return lax.dot_general(left, right, (dims, ((), ())), preferred_element_type=F32)


MESH = pl.DeviceIdType.MESH
ANY = pl.BlockSpec(memory_space=pl.ANY)
VM = pl.BlockSpec(memory_space=pltpu.VMEM)
DMA = pltpu.SemaphoreType.DMA
RANKS = 4


def across(rank, k):
    if k == 3:
        return 3 - rank
    if k == 1:
        return rank + 1 - 2 * lax.rem(rank, 2)
    if k == 2:
        return rank + 2 - 4 * lax.div(rank, 2)
    return rank


def flip(index, bit):
    step = 2**bit
    return index + step - 2 * step * lax.rem(lax.div(index, step), 2)


def inner_plane(rank):
    return (rank == 1) | (rank == 2)


def greet(peers):
    barrier = pltpu.get_barrier_semaphore()
    for peer in peers:
        pl.semaphore_signal(barrier, inc=1, device_id=peer, device_id_type=MESH)
    pl.semaphore_wait(barrier, len(peers))


def line_peers(rank):
    return [{"tensor": across(rank, k)} for k in (1, 2, 3)]


class LineGather:
    def __init__(self, rank, view, pieces, send_sems, recv_sems):
        self.rank, self.view, self.pieces = rank, view, pieces
        self.send_sems, self.recv_sems = send_sems, recv_sems
        self.inner = inner_plane(rank)

    @staticmethod
    def sems(pieces):
        return [DMA((4, pieces)), DMA((RANKS, pieces))]

    def copy(self, source, piece, k, slot):
        return pltpu.make_async_remote_copy(
            src_ref=self.view(source, piece), dst_ref=self.view(source, piece),
            send_sem=self.send_sems.at[slot, piece], recv_sem=self.recv_sems.at[source, piece],
            device_id={"tensor": across(self.rank, k)}, device_id_type=MESH,
        )

    def start(self, piece):
        self.copy(self.rank, piece, 2, 0).start()
        self.copy(self.rank, piece, 1, 1).start()
        pl.when(self.inner)(lambda: self.copy(self.rank, piece, 3, 2).start())

    def arrive(self, k, piece):
        source = across(self.rank, k)
        self.copy(source, piece, 1, 3).wait_recv()
        if k == 2:
            pl.when(self.inner)(lambda: self.copy(source, piece, 1, 3).start())

    def finish(self):
        for piece in range(self.pieces):
            self.copy(self.rank, piece, 2, 0).wait_send()
            self.copy(self.rank, piece, 1, 1).wait_send()

        @pl.when(self.inner)
        def _():
            for piece in range(self.pieces):
                self.copy(self.rank, piece, 3, 2).wait_send()
                self.copy(across(self.rank, 2), piece, 1, 3).wait_send()


def local(source, target, sem):
    return pltpu.make_async_copy(source, target, sem)


class LineScatter:
    def __init__(self, rank, parts, inbox, send_sems, recv_sems, pieces):
        self.rank, self.parts, self.inbox, self.pieces = rank, parts, inbox, pieces
        self.send_sems, self.recv_sems = send_sems, recv_sems
        self.inner = inner_plane(rank)
        self.end = (rank == 0) | (rank == 3)
        self.rows = parts.shape[1] // pieces

    @staticmethod
    def sems(pieces):
        return [DMA((4, pieces)), DMA((4, pieces))]

    def where(self, piece):
        return pl.ds(piece * self.rows, self.rows)

    def copy(self, part, slot, k, piece):
        return pltpu.make_async_remote_copy(
            src_ref=self.parts.at[part, self.where(piece)], dst_ref=self.inbox.at[slot, self.where(piece)],
            send_sem=self.send_sems.at[part, piece], recv_sem=self.recv_sems.at[slot, piece],
            device_id={"tensor": across(self.rank, k)}, device_id_type=MESH,
        )

    def send_far(self, pieces=None):
        for piece in pieces or range(self.pieces):
            pl.when(self.inner)(lambda: self.copy(3, 3, 3, piece).start())
            pl.when(self.end)(lambda: self.copy(3, 0, 1, piece).start())

    def send_two_end(self):
        @pl.when(self.end)
        def _():
            for piece in range(self.pieces):
                self.copy(2, 2, 2, piece).start()

    def send_two_inner(self):
        @pl.when(self.inner)
        def _():
            for piece in range(self.pieces):
                where = self.where(piece)
                self.copy(3, 0, 1, piece).wait_recv()
                self.parts[2, where] = (self.parts[2, where].astype(F32) + self.inbox[0, where].astype(F32)).astype(BF)
                self.copy(2, 2, 2, piece).start()

    def send_near(self):
        for piece in range(self.pieces):
            self.copy(1, 1, 1, piece).start()

    def total(self, target):
        for piece in range(self.pieces):
            where = self.where(piece)
            self.copy(1, 1, 1, piece).wait_recv()
            self.copy(2, 2, 2, piece).wait_recv()
            target[where] = (self.parts[0, where].astype(F32) + self.inbox[1, where].astype(F32)) + self.inbox[2, where].astype(F32)

        @pl.when(self.inner)
        def _():
            for piece in range(self.pieces):
                where = self.where(piece)
                self.copy(3, 3, 3, piece).wait_recv()
                target[where] += self.inbox[3, where].astype(F32)

    def finish(self):
        for piece in range(self.pieces):
            for part in (1, 2, 3):
                self.copy(part, part, part, piece).wait_send()


class GroupReduce:
    def __init__(self, group, dp, send, keep, first, boxes, split, sems):
        self.group, self.dp, self.send, self.keep, self.first, self.boxes = group, dp, send, keep, first, boxes
        self.bits = dp.bit_length() - 1
        self.mates = dp // 2
        columns = first.shape[3]
        self.cols = (pl.ds(0, split), pl.ds(split, columns - split))
        self.sems = sems

    @staticmethod
    def sem_shapes(dp, count):
        mates, bits = dp // 2, dp.bit_length() - 1
        shapes = [DMA((count, mates)), DMA((count, mates))]
        for t in range(1, bits):
            shapes += [DMA((2, count, mates >> t)), DMA((2, count, mates >> t))]
        return shapes

    @staticmethod
    def box_shapes(dp, count, share, columns, split):
        mates, bits = dp // 2, dp.bit_length() - 1
        shapes = [pltpu.VMEM((count, mates, share, columns), BF)]
        for t in range(1, bits):
            shapes += [pltpu.VMEM((count, mates >> t, share, split), BF), pltpu.VMEM((count, mates >> t, share, columns - split), BF)]
        return shapes

    def peers(self):
        return [{"dp": flip(self.group, b)} for b in range(self.bits)]

    def bit(self, b):
        return lax.rem(lax.div(self.group, 2**b), 2)

    def copy0(self, w, j):
        return pltpu.make_async_remote_copy(
            src_ref=self.send(w, 2 * j + 1 - self.bit(0)), dst_ref=self.first.at[w, j],
            send_sem=self.sems[0].at[w, j], recv_sem=self.sems[1].at[w, j],
            device_id={"dp": flip(self.group, 0)}, device_id_type=MESH)

    def place(self, t, half, j, mine):
        n = self.bits
        if half == 0:
            low = sum((self.bit(i) * 2 ** (i - 1) for i in range(1, t)), 0)
            bit = self.bit(t)
            return (2 * j + (bit if mine else 1 - bit)) * 2 ** (t - 1) + low
        high = sum((self.bit(n - i) * 2 ** (n - 1 - i) for i in range(1, t)), 0)
        bit = self.bit(n - t)
        return high + (bit if mine else 1 - bit) * 2 ** (n - 1 - t) + j

    def copy(self, t, half, w, j):
        return pltpu.make_async_remote_copy(
            src_ref=self.keep(w, self.place(t, half, j, False)).at[:, self.cols[half]], dst_ref=self.boxes[2 * (t - 1) + half].at[w, j],
            send_sem=self.sems[2 * t].at[half, w, j], recv_sem=self.sems[2 * t + 1].at[half, w, j],
            device_id={"dp": flip(self.group, t if half == 0 else self.bits - t)}, device_id_type=MESH)

    def start0(self, w):
        for j in range(self.mates):
            self.copy0(w, j).start()

    def start(self, t, w):
        for j in range(self.mates >> t):
            for half in range(2):
                self.copy(t, half, w, j).start()

    def add0(self, w):
        def body(j, carry):
            self.copy0(w, j).wait_recv()
            mine = self.keep(w, j)
            mine[...] = (mine[...].astype(F32) + self.first[w, j].astype(F32)).astype(BF)
            return carry

        lax.fori_loop(0, self.mates, body, 0)
        self.start(1, w)

    def add(self, t, w, target=None):
        for half in range(2):
            def body(j, carry):
                self.copy(t, half, w, j).wait_recv()
                mine = self.keep(w, self.place(t, half, j, True)).at[:, self.cols[half]]
                value = mine[...].astype(F32) + self.boxes[2 * (t - 1) + half][w, j].astype(F32)
                if target is None:
                    mine[...] = value.astype(BF)
                else:
                    target[:, self.cols[half]] = value.astype(target.dtype)
                return carry

            lax.fori_loop(0, self.mates >> t, body, 0)
        if target is None:
            self.start(t + 1, w)

    def finish(self, count):
        def body(w, carry):
            for j in range(self.mates):
                self.copy0(w, j).wait_send()
            for t in range(1, self.bits):
                for j in range(self.mates >> t):
                    for half in range(2):
                        self.copy(t, half, w, j).wait_send()
            return carry

        lax.fori_loop(0, count, body, 0)


def rope_numpy(length):
    half = HD // 2
    frequency = np.float32(10000.0) ** (-np.arange(half, dtype=np.float32) / np.float32(half))
    angles = np.arange(length, dtype=np.float32)[:, None] * frequency[None, :]
    cosine, sine = np.cos(angles), np.sin(angles)
    return (np.concatenate([cosine, cosine], 1), np.concatenate([-sine, sine], 1))


def column_of(row, target):
    target[...] = jnp.transpose(jnp.broadcast_to(row.astype(F32), (HD, row.shape[1])))


def forward_body(dp, tok, cot, seg, wo, wq, wk, wv, gain, gain2, cosine, sine,
                 a1_out, q_out, k_out, v_out, wo_out, cot_out, p_out, dy_out, a2_out, h_out, ob_out,
                 xs, a1s, qkv, ws, wos, dys, obs, ps, hs, segs,
                 x_ss, x_rs, z_ss, z_rs, d_ss, d_rs, c_ss, y_ss, y_rs, o_ss, o_rs, l_sem, k_sem, b_sem):
    rank, group = lax.axis_index("tensor"), lax.axis_index("dp")
    rows, model = tok.shape
    length, width = q_out.shape
    heads = width // HD
    scale = HD ** (-0.5)
    half_rows = rows // 2
    parts = wo.shape[0]
    mates = parts // 2
    member = lax.rem(group, parts)
    base = group - member
    parity = lax.rem(member, 2)
    pair = lax.div(member, 2)
    partner = flip(group, 0)

    def mate(step):
        return lax.rem(pair + step, mates) * 2 + parity

    first = [local(wo.at[member], wos.at[rank, member], l_sem.at[0]), local(tok, xs.at[rank], l_sem.at[1]), local(cot, dys.at[rank], l_sem.at[2])]
    weights = [local(w, ws.at[i], l_sem.at[3 + i]) for i, w in enumerate((wq, wk, wv))]
    for c in first + weights:
        c.start()
    column_of(seg[...], segs)
    greet(line_peers(rank) + [{"dp": partner}] + [{"dp": base + mate(s)} for s in range(1, mates)])
    out_gather = LineGather(rank, lambda s, p: wos.at[s, member], 1, z_ss, z_rs)
    gather = LineGather(rank, lambda s, p: xs.at[s, pl.ds(p * half_rows, half_rows)], 2, x_ss, x_rs)
    grads = LineGather(rank, lambda s, p: dys.at[s, pl.ds(p * half_rows, half_rows)], 2, y_ss, y_rs)
    attended = LineGather(rank, lambda s, p: obs.at[s, :, pl.ds(pl.multiple_of(p * HD, HD), HD)], heads, o_ss, o_rs)
    first[0].wait()
    out_gather.start(0)
    first[1].wait()
    gather.start(0)
    gather.start(1)
    first[2].wait()
    real = segs[pl.ds(pl.multiple_of(rank * rows, rows), rows), :1] >= 0.0
    dys[rank] = jnp.where(real, dys[rank], jnp.zeros((rows, model), BF))
    grads.start(0)
    grads.start(1)
    keep = [local(dys.at[rank], cot_out, k_sem.at[0])]
    keep[0].start()
    for w in weights:
        w.wait()

    def chunk(source):
        x = xs[source].astype(F32)
        a1s[source] = (x * norm_factor(x) * gain[...].reshape(1, model)).astype(BF)
        where = pl.ds(pl.multiple_of(source * rows, rows), rows)
        for i in range(3):
            product = dot(a1s[source], ws[i])
            for h in range(heads):
                head = product[:, h * HD : (h + 1) * HD]
                if i < 2:
                    head = head * cosine[where, :] + pltpu.roll(head, HD // 2, 1) * sine[where, :]
                qkv[i, where, h * HD : (h + 1) * HD] = head.astype(BF)

    def chunks(i, carry):
        @pl.when(i == 1)
        def _():
            for k in (1, 2, 3):
                out_gather.arrive(k, 0)
            for step in range(1, mates):
                mate_copy(step).start()
            core_copy(0, parity).start()
            for piece in range(2):
                gather.arrive(1, piece)
                gather.arrive(2, piece)

        @pl.when(i == 3)
        def _():
            for step in range(1, mates):
                mate_arrival(step).wait_recv()
                core_copy(step, parity).start()
            for piece in range(2):
                gather.arrive(3, piece)

        chunk(pick(i, [rank, across(rank, 1), across(rank, 2), across(rank, 3)]))
        return carry

    def mate_copy(step):
        return pltpu.make_async_remote_copy(
            src_ref=wos.at[:, member], dst_ref=wos.at[:, member], send_sem=d_ss.at[step], recv_sem=d_rs.at[member],
            device_id={"dp": base + mate(step)}, device_id_type=MESH)

    def mate_arrival(step):
        piece = mate(step)
        return pltpu.make_async_remote_copy(
            src_ref=wos.at[:, piece], dst_ref=wos.at[:, piece], send_sem=d_ss.at[step], recv_sem=d_rs.at[piece],
            device_id={"dp": base + piece}, device_id_type=MESH)

    def core_copy(step, owner):
        piece = lax.rem(pair + step, mates) * 2 + owner
        return pltpu.make_async_remote_copy(
            src_ref=wos.at[:, piece], dst_ref=wos.at[:, piece], send_sem=c_ss.at[step], recv_sem=d_rs.at[piece],
            device_id={"dp": partner}, device_id_type=MESH)

    lax.fori_loop(0, RANKS, chunks, 0)
    keep += [local(a1s, a1_out, k_sem.at[1])] + [local(qkv.at[i], t, k_sem.at[2 + i]) for i, t in enumerate((q_out, k_out, v_out))]
    for c in keep[1:]:
        c.start()

    def head(h, carry):
        cols = pl.ds(pl.multiple_of(h * HD, HD), HD)
        for start in range(0, length, QB):
            extent = start + QB
            scores = dot(qkv[0, start:extent, cols], qkv[1, :extent, cols], ((1,), (1,)))
            row_ids = lax.broadcasted_iota(jnp.int32, (QB, extent), 0) + start
            col_ids = lax.broadcasted_iota(jnp.int32, (QB, extent), 1)
            allowed = (col_ids <= row_ids) & (segs[start:extent, :1] == seg[:, :extent].astype(F32))
            logits = jnp.where(allowed, scores * scale, NEG)
            expo = jnp.exp(logits - jnp.max(logits, axis=-1, keepdims=True))
            probs = (expo * (1.0 / jnp.sum(expo, axis=-1, keepdims=True))).astype(BF)
            ps[h, start:extent, :extent] = probs
            obs[rank, start:extent, cols] = dot(probs, qkv[2, :extent, cols]).astype(BF)
        attended.start(h)
        return carry

    lax.fori_loop(0, heads, head, 0)
    for step in range(mates):
        core_copy(step, 1 - parity).wait_recv()
    more = [local(ps, p_out, k_sem.at[5]), local(wos, wo_out, k_sem.at[6])]
    for c in more:
        c.start()
    keep += more

    def add(source, first=False, last=False):
        def block(b, carry):
            weight = wos[source].reshape(width, model)
            part = dot(obs[source, pl.ds(pl.multiple_of(b * rows, rows), rows), :], weight)
            total = part + (xs[b].astype(F32) if first else hs[b])
            hs[b] = total
            if last:
                xs[b] = (total * norm_factor(total) * gain2[...].reshape(1, model)).astype(BF)
                local(xs.at[b], a2_out.at[b], b_sem.at[b]).start()
            return carry

        lax.fori_loop(0, RANKS, block, 0)

    add(rank, first=True)
    for piece in range(2):
        grads.arrive(2, piece)
    for piece in range(heads):
        attended.arrive(2, piece)
    for piece in range(heads):
        attended.arrive(1, piece)
    add(across(rank, 2))
    add(across(rank, 1))
    for piece in range(2):
        grads.arrive(1, piece)
        grads.arrive(3, piece)
    more = [local(dys, dy_out, l_sem.at[0])]
    more[0].start()
    for piece in range(heads):
        attended.arrive(3, piece)
    gather.finish()
    add(across(rank, 3), last=True)
    more += [local(hs.at[rank], h_out, l_sem.at[2]),
             local(obs.at[:, pl.ds(pl.multiple_of(rank * rows, rows), rows)], ob_out, l_sem.at[3])]
    for c in more[1:]:
        c.start()
    out_gather.finish()
    for step in range(1, mates):
        mate_copy(step).wait_send()
    for step in range(mates):
        core_copy(step, parity).wait_send()
    grads.finish()
    attended.finish()
    for c in keep + more:
        c.wait()
    for b in range(RANKS):
        local(xs.at[b], a2_out.at[b], b_sem.at[b]).wait()


def forward_kernel(dp, tokens, cotangent, segments, w_out, w_query, w_key, w_value, gain, gain2, cosine, sine):
    rows, model = tokens.shape
    width = w_query.shape[1]
    heads = width // HD
    length = RANKS * rows
    parts = min(dp, 8)
    mates = parts // 2
    shape = (RANKS, rows, model)
    shard, wide = jax.ShapeDtypeStruct(shape, BF), jax.ShapeDtypeStruct((length, width), BF)
    outs = pl.pallas_call(
        functools.partial(forward_body, dp),
        in_specs=[ANY, ANY, VM, ANY, ANY, ANY, ANY, VM, VM, VM, VM],
        out_specs=[ANY] * 11,
        out_shape=[shard, wide, wide, wide, jax.ShapeDtypeStruct((RANKS, parts, width // parts, model), BF),
                   jax.ShapeDtypeStruct((rows, model), BF), jax.ShapeDtypeStruct((heads, length, length), BF), shard, shard,
                   jax.ShapeDtypeStruct((rows, model), F32), jax.ShapeDtypeStruct((RANKS, rows, width), BF)],
        scratch_shapes=[
            pltpu.VMEM(shape, BF), pltpu.VMEM(shape, BF), pltpu.VMEM((3, length, width), BF), pltpu.VMEM((3, model, width), BF),
            pltpu.VMEM((RANKS, parts, width // parts, model), BF), pltpu.VMEM(shape, BF), pltpu.VMEM((RANKS, length, width), BF),
            pltpu.VMEM((heads, length, length), BF), pltpu.VMEM(shape, F32), pltpu.VMEM((length, HD), F32),
            *LineGather.sems(2), *LineGather.sems(1), DMA((mates,)), DMA((parts,)), DMA((mates,)),
            *LineGather.sems(2), *LineGather.sems(heads), DMA((6,)), DMA((7,)), DMA((RANKS,)),
        ],
        compiler_params=pltpu.CompilerParams(collective_id=1, has_side_effects=True, vmem_limit_bytes=62 << 20),
        name="forward_gather",
    )(tokens, cotangent, segments, w_out.reshape(parts, width // parts, model), w_query, w_key, w_value, gain, gain2, cosine, sine)
    a1_all, query, key, value, w_out_all, cot_own, probs, dy, a2, hidden, attended = outs
    return a1_all, query, key, value, w_out_all.reshape(RANKS, width, model), cot_own, probs, dy, a2, hidden, attended


def pick(step, choices):
    value = choices[-1]
    for i in range(len(choices) - 1):
        value = jnp.where(step == i, choices[i], value)
    return value


FT = 768
WB = 384


def mlp_body(a2, dy, wg, wu, wd, hid, cot, gran, gain,
             g_out, down_out, dh_out, gain_out,
             lefts, acts, ws, parts, inbox, stage, downs, hs, cots, total, gains, r_ss, r_rs, l_sem, s_sem):
    rank = lax.axis_index("tensor")
    rows, model = cot.shape
    width = wg.shape[1]
    per, share = stage.shape[1], stage.shape[2]
    loads = [local(wg, ws.at[0], l_sem.at[0]), local(a2, lefts.at[0], l_sem.at[1]), local(wu, ws.at[1], l_sem.at[2]),
             local(dy, lefts.at[1], l_sem.at[3]), local(wd, ws.at[2], l_sem.at[4])]
    late = [local(hid, hs, l_sem.at[5]), local(cot, cots, l_sem.at[6])]
    for c in loads + late:
        c.start()
    greet(line_peers(rank))
    scatter = LineScatter(rank, parts, inbox, r_ss, r_rs, 2)
    order = [across(rank, k) for k in (3, 2, 1, 0)]
    limit = FF // 8 * lax.shift_left(1, gran[0] - 1) - rank * width

    def step(i, carry):
        where = pl.ds(pl.multiple_of(pick(i, order) * rows, rows), rows)

        def tile(t, inner_carry):
            cols = pl.ds(pl.multiple_of(t * FT, FT), FT)

            @pl.when((i == 0) & (t == 0))
            def _():
                loads[0].wait()
                loads[1].wait()

            gate = dot(lefts[0, where, :], ws[0, :, cols])

            @pl.when((i == 0) & (t == 0))
            def _():
                loads[2].wait()

            up = dot(lefts[0, where, :], ws[1, :, cols])

            @pl.when((i == 0) & (t == 0))
            def _():
                loads[3].wait()
                loads[4].wait()

            dz = dot(lefts[1, where, :], ws[2, cols, :], ((1,), (1,)))
            unit = lax.broadcasted_iota(jnp.int32, gate.shape, 1) + t * FT
            mask = unit < limit
            sigma = jax.nn.sigmoid(gate)
            active = jnp.where(mask, gate * sigma, 0.0)
            acts[2, where, cols] = (active * up).astype(BF)
            acts[0, where, cols] = jnp.where(mask, dz * up * sigma * (1.0 + gate * (1.0 - sigma)), 0.0).astype(BF)
            acts[1, where, cols] = (dz * active).astype(BF)
            return inner_carry

        lax.fori_loop(0, width // FT, tile, 0)

        def back(t, inner_carry):
            cols = pl.ds(pl.multiple_of(t * FT, FT), FT)
            parts[3 - i, :, cols] = (
                dot(acts[0, where, :], ws[0, cols, :], ((1,), (1,))) + dot(acts[1, where, :], ws[1, cols, :], ((1,), (1,)))
            ).astype(BF)
            return inner_carry

        lax.fori_loop(0, model // FT, back, 0)
        pl.when(i == 0)(scatter.send_far)
        pl.when(i == 1)(scatter.send_two_end)

        @pl.when(i == 2)
        def _():
            scatter.send_near()
            scatter.send_two_inner()

        return carry

    lax.fori_loop(0, 4, step, 0)
    blocks = model // WB

    def put(i, slot):
        w, b = lax.div(i, blocks), lax.rem(i, blocks)
        return local(stage.at[slot], g_out.at[w, pl.ds(b * per, per)], s_sem.at[slot])

    def grads(i, carry):
        slot = lax.rem(i, 2)
        w, b = lax.div(i, blocks), lax.rem(i, blocks)
        left = lax.div(w, 2)
        cols = pl.ds(pl.multiple_of(b * WB, WB), WB)
        value = dot(lefts[left, :, cols], acts[w], ((0,), (0,)))
        pl.when(i >= 2)(lambda: put(i - 2, slot).wait())
        low = value.astype(BF)
        for p in range(per):
            stage[slot, p] = low[p * share : (p + 1) * share]
        put(i, slot).start()
        return carry

    lax.fori_loop(0, 3 * blocks, grads, 0)

    def down(i, carry):
        where = pl.ds(pl.multiple_of(pick(i, order) * rows, rows), rows)
        downs[3 - i] = dot(acts[2, where, :], ws[2]).astype(BF)
        return carry

    lax.fori_loop(0, 4, down, 0)
    keep = local(downs, down_out, l_sem.at[0])
    keep.start()
    for c in late:
        c.wait()
    scatter.total(total)
    values, gradient = hs[...], total[...]
    factor = norm_factor(values)
    back_rows, gain_rows = norm_back(values, factor, gain[...].reshape(1, model), gradient)
    total[...] = cots[...].astype(F32) + back_rows
    gains[...] = gain_rows.reshape(1, model)
    last = [local(total, dh_out, l_sem.at[1]), local(gains, gain_out, l_sem.at[2])]
    for c in last:
        c.start()
    scatter.finish()
    put(3 * blocks - 2, 0).wait()
    put(3 * blocks - 1, 1).wait()
    for c in last + [keep]:
        c.wait()


def mlp_kernel(dp, a2, dy, w_gate, w_up, w_down, hidden_own, cot_own, granularity, gain):
    rows, model = cot_own.shape
    width = w_gate.shape[1]
    share = model // dp
    shard = (RANKS, rows, model)
    return pl.pallas_call(
        mlp_body,
        in_specs=[ANY] * 7 + [pl.BlockSpec(memory_space=pltpu.SMEM), VM],
        out_specs=[ANY] * 4,
        out_shape=[jax.ShapeDtypeStruct((3, dp, share, width), BF), jax.ShapeDtypeStruct(shard, BF),
                   jax.ShapeDtypeStruct((rows, model), F32), jax.ShapeDtypeStruct((1, model), F32)],
        scratch_shapes=[
            pltpu.VMEM((2, RANKS * rows, model), BF), pltpu.VMEM((3, RANKS * rows, width), BF), pltpu.VMEM((3, model, width), BF),
            pltpu.VMEM(shard, BF), pltpu.VMEM(shard, BF), pltpu.VMEM((2, WB // share, share, width), BF), pltpu.VMEM(shard, BF),
            pltpu.VMEM((rows, model), F32), pltpu.VMEM((rows, model), BF), pltpu.VMEM((rows, model), F32), pltpu.VMEM((1, model), F32),
            *LineScatter.sems(2), DMA((7,)), DMA((2,)),
        ],
        compiler_params=pltpu.CompilerParams(collective_id=3, has_side_effects=True, vmem_limit_bytes=63 << 20),
        name="mlp_scatter",
    )(a2.reshape(-1, model), dy.reshape(-1, model), w_gate, w_up, w_down, hidden_own, cot_own, granularity, gain)


def attention_back_body(dp, dh, wo_all, downs, grads, q, k, v, p_all, hid, cosine, sine,
                        out_out, dq_out, dk_out, dv_out, gf_out,
                        dhs, low, wos, parts, inbox, dobs, dos, qkv, ps, ds, dqkv, hs, outs, kept, finals, *rest):
    rank, group = lax.axis_index("tensor"), lax.axis_index("dp")
    rounds = 2 * (dp.bit_length() - 1)
    first, boxes, rest = rest[0], rest[1 : rounds - 1], rest[rounds - 1 :]
    sems, (r_ss, r_rs, a_ss, a_rs, l_sem, p_sem, f_sem) = rest[:rounds], rest[rounds:]
    rows, model = dh.shape
    length, width = q.shape
    heads, half, scale = width // HD, HD // 2, HD ** (-0.5)
    count = grads.shape[0]
    parity = lax.rem(group, 2)
    loads = [local(downs, parts, l_sem.at[2]), local(dh, dhs, l_sem.at[0]), local(wo_all, wos, l_sem.at[1])]
    owns = [local(grads.at[w, :, parity], kept.at[w], f_sem.at[w]) for w in range(count)]
    late = [local(t, qkv.at[i], l_sem.at[3 + i]) for i, t in enumerate((q, k, v))] + [local(hid, hs, l_sem.at[6])]
    for c in loads + owns + late:
        c.start()

    def probs(h):
        return local(p_all.at[h], ps.at[lax.rem(h, 2)], p_sem.at[lax.rem(h, 2)])

    probs(0).start()
    probs(1).start()
    reduce = GroupReduce(
        group, dp, lambda w, d: grads.at[w, lax.div(d, 2), lax.rem(d, 2)], lambda w, j: kept.at[w, j], first, boxes, model // 2, sems)
    greet(line_peers(rank) + reduce.peers())
    for w in range(count):
        reduce.start0(w)
    scatter = LineScatter(rank, parts, inbox, r_ss, r_rs, 2)
    loads[0].wait()
    scatter.send_far([0])

    def exchange(k, source):
        where = pl.ds(pl.multiple_of(source * rows, rows), rows)
        return pltpu.make_async_remote_copy(
            src_ref=dobs.at[k - 1], dst_ref=dos.at[where], send_sem=a_ss.at[k], recv_sem=a_rs.at[source],
            device_id={"tensor": across(rank, k)}, device_id_type=MESH)

    loads[1].wait()
    low[...] = dhs[...].astype(BF)
    loads[2].wait()
    for k in (3, 2, 1):
        dobs[k - 1] = dot(low[...], wos[across(rank, k)], ((1,), (1,))).astype(BF)
        exchange(k, rank).start()
    scatter.send_far([1])
    scatter.send_two_end()
    scatter.send_near()
    dos[pl.ds(pl.multiple_of(rank * rows, rows), rows), :] = dot(low[...], wos[rank], ((1,), (1,))).astype(BF)
    for c in owns:
        c.wait()

    def fold(w, carry):
        reduce.add0(w)
        return carry

    lax.fori_loop(0, count, fold, 0)
    for c in late:
        c.wait()
    for k in (3, 2, 1):
        exchange(k, across(rank, k)).wait_recv()

    def head(h, carry):
        cols = pl.ds(pl.multiple_of(h * HD, HD), HD)
        slot = lax.rem(h, 2)
        probs(h).wait()

        def unrope(grad, start):
            where = slice(start, start + QB)
            return (grad * cosine[where, :] - pltpu.roll(grad, half, 1) * sine[where, :]).astype(BF)

        for start in range(0, length, QB):
            extent = start + QB
            where = slice(start, extent)
            grad_p = dot(dos[where, cols], qkv[2, :extent, cols], ((1,), (1,)))
            p = ps[slot, where, :extent].astype(F32)
            weighted = p * grad_p
            delta = jnp.sum(weighted, axis=-1, keepdims=True)
            ds[where, :extent] = ((weighted - p * delta) * scale).astype(BF)
            dqkv[0, where, cols] = unrope(dot(ds[where, :extent], qkv[1, :extent, cols]), start)
        for start in range(0, length, QB):
            where = slice(start, start + QB)
            dqkv[1, where, cols] = unrope(dot(ds[start:, where], qkv[0, start:, cols], ((0,), (0,))), start)
            dqkv[2, where, cols] = dot(ps[slot, start:, where], dos[start:, cols], ((0,), (0,))).astype(BF)
        pl.when(h + 2 < heads)(lambda: probs(h + 2).start())
        return carry

    lax.fori_loop(0, heads, head, 0)
    done = [local(dqkv.at[i], t, l_sem.at[i]) for i, t in enumerate((dq_out, dk_out, dv_out))]
    for c in done:
        c.start()
    reduce.add(1, 0)
    scatter.send_two_inner()
    reduce.add(1, 1)
    reduce.add(1, 2)
    for t in range(2, reduce.bits - 1):
        for w in range(count):
            reduce.add(t, w)

    def put(w):
        return local(finals.at[w], gf_out.at[w], f_sem.at[w])

    for w in range(count):
        reduce.add(reduce.bits - 1, w, finals.at[w])
        put(w).start()
    scatter.total(dhs)
    outs[...] = (hs[...] + dhs[...]).astype(BF)
    last = local(outs, out_out, l_sem.at[3])
    last.start()
    scatter.finish()
    for k in (1, 2, 3):
        exchange(k, rank).wait_send()
    reduce.finish(count)
    for w in range(count):
        put(w).wait()
    for c in done + [last]:
        c.wait()


def attention_back_kernel(dp, grad_hidden, w_out_all, down_parts, grads_ff, query, key, value, probs_low, hidden_own, cosine, sine):
    rows, model = grad_hidden.shape
    length, width = query.shape
    count, _, share, columns = grads_ff.shape
    mates = dp // 2
    shard = (RANKS, rows, model)
    heads = jax.ShapeDtypeStruct((length, width), BF)
    return pl.pallas_call(
        functools.partial(attention_back_body, dp),
        in_specs=[ANY] * 9 + [VM, VM],
        out_specs=[ANY] * 5,
        out_shape=[jax.ShapeDtypeStruct((rows, model), BF), heads, heads, heads, jax.ShapeDtypeStruct((count, share, columns), BF)],
        scratch_shapes=[
            pltpu.VMEM((rows, model), F32), pltpu.VMEM((rows, model), BF), pltpu.VMEM((RANKS, width, model), BF),
            pltpu.VMEM(shard, BF), pltpu.VMEM(shard, BF), pltpu.VMEM((3, rows, width), BF), pltpu.VMEM((length, width), BF),
            pltpu.VMEM((3, length, width), BF), pltpu.VMEM((2, length, length), BF), pltpu.VMEM((length, length), BF),
            pltpu.VMEM((3, length, width), BF), pltpu.VMEM((rows, model), F32), pltpu.VMEM((rows, model), BF),
            pltpu.VMEM((count, mates, share, columns), BF), pltpu.VMEM((count, share, columns), BF),
            *GroupReduce.box_shapes(dp, count, share, columns, columns // 2), *GroupReduce.sem_shapes(dp, count),
            *LineScatter.sems(2), DMA((4,)), DMA((RANKS,)), DMA((7,)), DMA((2,)), DMA((count,)),
        ],
        compiler_params=pltpu.CompilerParams(collective_id=4, has_side_effects=True, vmem_limit_bytes=63 << 20),
        name="attention_back",
    )(grad_hidden, w_out_all, down_parts, grads_ff.reshape(count, mates, 2, share, columns),
      query, key, value, probs_low, hidden_own, cosine, sine)


def input_back_body(dp, dq, dk, dv, a1, wq, wk, wv, tok, dh, ob, gain, gain2,
                    dx_out, gains_out, gqkv_out, gout_out,
                    dqkv, a1s, ws, xs, dhs, low, obs, parts, inbox, g1, g2, f1, f2, f2_low, box2, f3, gbuf, gbox, total, dxs, *rest):
    rank, group = lax.axis_index("tensor"), lax.axis_index("dp")
    bits = dp.bit_length() - 1
    boxes = [rest[: 2 * bits - 1], rest[2 * bits - 1 : 4 * bits - 2]]
    rest = rest[4 * bits - 2 :]
    sems = [rest[: 2 * bits], rest[2 * bits : 4 * bits]]
    r_ss, r_rs, z_ss, z_rs, g_ss, g_rs, l_sem = rest[4 * bits :]
    rows, model = tok.shape
    width = dq.shape[1]
    share = g1.shape[1]
    per = WB // share
    parity = lax.rem(group, 2)
    loads = [local(t, dqkv.at[i], l_sem.at[i]) for i, t in enumerate((dq, dk, dv))]
    loads += [local(t, ws.at[i], l_sem.at[3 + i]) for i, t in enumerate((wq, wk, wv))]
    late = [local(a1, a1s, l_sem.at[8]), local(dh, dhs, l_sem.at[6]), local(ob, obs, l_sem.at[7]), local(tok, xs, l_sem.at[9])]
    for c in loads + late:
        c.start()
    scatter = LineScatter(rank, parts, inbox, r_ss, r_rs, 2)
    mixed = GroupReduce(group, dp, lambda w, d: g1.at[d], lambda w, j: g1.at[2 * j + parity], boxes[0][0], boxes[0][1:], f1.shape[1] // 256 * 128, sems[0])
    output = GroupReduce(group, dp, lambda w, d: g2.at[d], lambda w, j: g2.at[2 * j + parity], boxes[1][0], boxes[1][1:], f2.shape[1] // 256 * 128, sems[1])
    greet(line_peers(rank) + mixed.peers())
    order = [across(rank, k) for k in (3, 2, 1, 0)]
    for c in loads:
        c.wait()

    def step(i, carry):
        where = pl.ds(pl.multiple_of(pick(i, order) * rows, rows), rows)
        value = dot(dqkv[0, where, :], ws[0], ((1,), (1,)))
        for s in (1, 2):
            value += dot(dqkv[s, where, :], ws[s], ((1,), (1,)))
        parts[3 - i] = value.astype(BF)
        pl.when(i == 0)(scatter.send_far)
        pl.when(i == 1)(scatter.send_two_end)
        pl.when(i == 2)(scatter.send_near)

        @pl.when(i == 0)
        def _():
            late[0].wait()

        row = jnp.sum(value * a1s[where, :].astype(F32), axis=0, keepdims=True)
        gbuf[0, 0:1, :] = jnp.where(i == 0, row, gbuf[0, 0:1, :] + row)
        return carry

    gbuf[0, 0:1, :] = jnp.zeros((1, model), F32)
    lax.fori_loop(0, 4, step, 0)
    gbuf[0, 0:1, :] = gbuf[0, 0:1, :] / gain[...].reshape(1, model)
    gbuf[0, 1:2, :] = gain2[...]

    def swap(t):
        return pltpu.make_async_remote_copy(
            src_ref=gbuf.at[t], dst_ref=gbox.at[t], send_sem=g_ss.at[t], recv_sem=g_rs.at[t], device_id={"dp": flip(group, t)}, device_id_type=MESH)

    def advance(t):
        swap(t).wait_recv()
        gbuf[t + 1] = gbuf[t] + gbox[t]
        if t + 1 < bits:
            swap(t + 1).start()

    def share_gains(k, source):
        return pltpu.make_async_remote_copy(
            src_ref=gbuf.at[bits], dst_ref=gbox.at[bits + source], send_sem=g_ss.at[bits + k], recv_sem=g_rs.at[bits + source],
            device_id={"tensor": across(rank, k)}, device_id_type=MESH)

    swap(0).start()
    for c in late[1:]:
        c.wait()
    low[...] = dhs[...].astype(BF)

    def out_block(b, carry):
        cols = pl.ds(pl.multiple_of(b * WB, WB), WB)
        for r in range(RANKS):
            value = dot(low[:, cols], obs[r], ((0,), (0,))).astype(BF)
            for p in range(per):
                g2[b * per + p, :, r * width : (r + 1) * width] = value[p * share : (p + 1) * share]
        return carry

    lax.fori_loop(0, model // WB, out_block, 0)
    advance(0)
    output.start0(0)

    def mixed_block(b, carry):
        cols = pl.ds(pl.multiple_of(b * WB, WB), WB)
        for s in range(3):
            value = dot(a1s[:, cols], dqkv[s], ((0,), (0,))).astype(BF)
            for p in range(per):
                g1[b * per + p, :, s * width : (s + 1) * width] = value[p * share : (p + 1) * share]
        return carry

    lax.fori_loop(0, model // WB, mixed_block, 0)
    for t in range(1, bits):
        advance(t)
    for k in (1, 2, 3):
        share_gains(k, rank).start()
    gbox[bits + rank] = gbuf[bits]
    mixed.start0(0)
    output.add0(0)
    mixed.add0(0)
    scatter.send_two_inner()
    for t in range(1, bits - 1):
        output.add(t, 0)
        mixed.add(t, 0)
    output.add(bits - 1, 0, f2)
    ends = LineScatter(rank, f2_low, box2, z_ss, z_rs, 1)
    for k in range(4):
        column = pl.ds(pl.multiple_of(across(rank, k) * width, HD), width)
        f2_low[k] = f2[:, column].astype(BF)
    ends.send_far()
    ends.send_two_end()
    ends.send_near()
    mixed.add(bits - 1, 0, f1)
    done = [local(f1, gqkv_out, l_sem.at[0])]
    done[0].start()
    scatter.total(total)
    values, gradient = xs[...].astype(F32), total[...]
    back_rows, _ = norm_back(values, norm_factor(values), gain[...].reshape(1, model), gradient)
    dxs[...] = (dhs[...] + back_rows).astype(BF)
    done.append(local(dxs, dx_out, l_sem.at[1]))
    done[1].start()
    for k in (1, 2, 3):
        share_gains(k, across(rank, k)).wait_recv()
    for t in range(bits):
        swap(t).wait_send()
    gbuf[0] = ((gbox[bits] + gbox[bits + 1]) + gbox[bits + 2]) + gbox[bits + 3]
    done.append(local(gbuf.at[0], gains_out, l_sem.at[2]))
    done[2].start()
    ends.send_two_inner()
    ends.total(f3)
    done.append(local(f3, gout_out, l_sem.at[3]))
    done[3].start()
    scatter.finish()
    ends.finish()
    mixed.finish(1)
    output.finish(1)
    for k in (1, 2, 3):
        share_gains(k, rank).wait_send()
    for c in done:
        c.wait()


def input_back_kernel(dp, grad_q, grad_k, grad_v, a1_all, w_query, w_key, w_value, tokens, grad_hidden, attended_own, gain, gain_two):
    rows, model = tokens.shape
    length, width = grad_q.shape
    share = model // dp
    bits = dp.bit_length() - 1
    shard = (RANKS, rows, model)
    wide = (3 * width, RANKS * width)
    splits = [w // 256 * 128 for w in wide]
    return pl.pallas_call(
        functools.partial(input_back_body, dp),
        in_specs=[ANY] * 10 + [VM, VM],
        out_specs=[ANY] * 4,
        out_shape=[jax.ShapeDtypeStruct((rows, model), BF), jax.ShapeDtypeStruct((2, model), F32),
                   jax.ShapeDtypeStruct((share, wide[0]), F32), jax.ShapeDtypeStruct((share, width), F32)],
        scratch_shapes=[
            pltpu.VMEM((3, length, width), BF), pltpu.VMEM((length, model), BF), pltpu.VMEM((3, model, width), BF),
            pltpu.VMEM((rows, model), BF), pltpu.VMEM((rows, model), F32), pltpu.VMEM((rows, model), BF), pltpu.VMEM((RANKS, rows, width), BF),
            pltpu.VMEM(shard, BF), pltpu.VMEM(shard, BF),
            pltpu.VMEM((dp, share, wide[0]), BF), pltpu.VMEM((dp, share, wide[1]), BF),
            pltpu.VMEM((share, wide[0]), F32), pltpu.VMEM((share, wide[1]), F32),
            pltpu.VMEM((RANKS, share, width), BF), pltpu.VMEM((RANKS, share, width), BF), pltpu.VMEM((share, width), F32),
            pltpu.VMEM((bits + 1, 2, model), F32), pltpu.VMEM((bits + RANKS, 2, model), F32),
            pltpu.VMEM((rows, model), F32), pltpu.VMEM((rows, model), BF),
            *GroupReduce.box_shapes(dp, 1, share, wide[0], splits[0]), *GroupReduce.box_shapes(dp, 1, share, wide[1], splits[1]),
            *GroupReduce.sem_shapes(dp, 1), *GroupReduce.sem_shapes(dp, 1),
            *LineScatter.sems(2), *LineScatter.sems(1), DMA((bits + RANKS,)), DMA((bits + RANKS,)), DMA((10,)),
        ],
        compiler_params=pltpu.CompilerParams(collective_id=5, has_side_effects=True, vmem_limit_bytes=63 << 20),
        name="input_back",
    )(grad_q, grad_k, grad_v, a1_all.reshape(length, model), w_query, w_key, w_value, tokens, grad_hidden, attended_own, gain, gain_two)


def finish_body(output, dx, gains, mixed, out_t, ff,
                output_out, dx_out, gain1_out, gain2_out, q_out, k_out, v_out, wo_out, gate_out, up_out, down_out,
                b0, b1, gs, g1, g2, ms, ot, fs, gate, up, down, i_sem, o_sem):
    width = q_out.shape[1]
    loads = [local(s, t, i_sem.at[i]) for i, (s, t) in enumerate(
        ((ff.at[2], fs.at[2]), (ff.at[0], fs.at[0]), (ff.at[1], fs.at[1]), (mixed, ms), (output, b0), (dx, b1), (out_t, ot), (gains, gs)))]
    for c in loads:
        c.start()
    sent = []

    def put(source, target):
        sent.append(local(source, target, o_sem.at[len(sent)]))
        sent[-1].start()

    loads[1].wait()
    gate[...] = fs[0].astype(F32)
    put(gate, gate_out)
    loads[2].wait()
    up[...] = fs[1].astype(F32)
    put(up, up_out)
    loads[4].wait()
    put(b0, output_out)
    loads[5].wait()
    put(b1, dx_out)
    loads[3].wait()
    for i, target in enumerate((q_out, k_out, v_out)):
        put(ms.at[:, pl.ds(i * width, width)], target)
    loads[0].wait()
    down[...] = fs[2].astype(F32)
    put(down, down_out)
    loads[6].wait()
    put(ot, wo_out)
    loads[7].wait()
    g1[...] = gs[0]
    put(g1, gain1_out)
    g2[...] = gs[1]
    put(g2, gain2_out)
    for c in sent:
        c.wait()


def finish_kernel(output, dx, gains, mixed, out_t, ff):
    rows, model = output.shape
    share, width = out_t.shape
    columns = ff.shape[2]
    gain, head, wide = ((model,), F32), ((share, width), F32), ((share, columns), F32)
    outs = [((rows, model), BF), ((rows, model), BF), gain, gain, head, head, head, head, wide, wide, wide]
    return pl.pallas_call(
        finish_body,
        in_specs=[ANY] * 6,
        out_specs=[ANY] * 11,
        out_shape=[jax.ShapeDtypeStruct(*o) for o in outs],
        scratch_shapes=[
            pltpu.VMEM((rows, model), BF), pltpu.VMEM((rows, model), BF), pltpu.VMEM((2, model), F32), pltpu.VMEM((model,), F32), pltpu.VMEM((model,), F32),
            pltpu.VMEM((share, 3 * width), F32), pltpu.VMEM((share, width), F32),
            pltpu.VMEM((3, share, columns), BF), pltpu.VMEM((share, columns), F32), pltpu.VMEM((share, columns), F32), pltpu.VMEM((share, columns), F32),
            DMA((8,)), DMA((11,)),
        ],
        compiler_params=pltpu.CompilerParams(vmem_limit_bytes=63 << 20),
        name="finish",
    )(output, dx, gains, mixed, out_t, ff)


def on_device(tokens, segments, granularity, norm1_gain, norm2_gain, w_query, w_key, w_value, w_out, w_gate, w_up, w_down, cotangent):
    length = segments.shape[1]
    cosine, sine = (jnp.asarray(t) for t in rope_numpy(length))
    dp = lax.axis_size("dp")
    a1_all, query_rot, key_rot, value_low, w_out_all, cot_own, probs_low, grad_rows, rows_two, hidden_own, attended_own = forward_kernel(
        dp, tokens, cotangent, segments, w_out, w_query, w_key, w_value, norm1_gain, norm2_gain, cosine, sine
    )
    grads_ff, down_parts, grad_hidden, gain_two = mlp_kernel(
        dp, rows_two, grad_rows, w_gate, w_up, w_down, hidden_own, cot_own, granularity, norm2_gain
    )
    output, grad_q, grad_k, grad_v, own_ff = attention_back_kernel(
        dp, grad_hidden, w_out_all, down_parts, grads_ff, query_rot, key_rot, value_low, probs_low, hidden_own, cosine, sine
    )
    grad_tokens, gains, own_qkv, own_out = input_back_kernel(
        dp, grad_q, grad_k, grad_v, a1_all, w_query, w_key, w_value, tokens, grad_hidden, attended_own, norm1_gain, gain_two
    )
    outs = finish_kernel(output, grad_tokens, gains, own_qkv, own_out, own_ff)
    return tuple(o.T if i in (7, 10) else o for i, o in enumerate(outs))


def solution(mesh):
    in_specs = (
        P(("dp", "tensor"), None), P("dp", None), P("dp"), P(), P(),
        P(None, "tensor"), P(None, "tensor"), P(None, "tensor"), P("tensor", None),
        P(None, "tensor"), P(None, "tensor"), P("tensor", None), P(("dp", "tensor"), None),
    )
    out_specs = (
        P(("dp", "tensor"), None), P(("dp", "tensor"), None), P(), P(),
        P("dp", "tensor"), P("dp", "tensor"), P("dp", "tensor"), P("tensor", "dp"),
        P("dp", "tensor"), P("dp", "tensor"), P("tensor", "dp"),
    )
    return jax.shard_map(on_device, mesh=mesh, in_specs=in_specs, out_specs=out_specs, check_vma=False)
```

```python
import functools

import jax
import jax.numpy as jnp
import numpy as np
from jax import lax
from jax.experimental import pallas as pl
from jax.experimental.pallas import tpu as pltpu
from jax.sharding import PartitionSpec as P

HD = 128
FF = 6144
EPS = 1e-06
NEG = -1e30
BF = jnp.bfloat16
F32 = jnp.float32
QB = 256


def norm_factor(values):
    return lax.rsqrt(jnp.mean(values * values, axis=-1, keepdims=True) + EPS)


def norm_back(values, factor, row_gain, gradient):
    scaled = gradient * row_gain
    inner_mean = jnp.mean(scaled * values, axis=-1, keepdims=True)
    back_rows = factor * scaled - values * (factor * factor * factor) * inner_mean
    return (back_rows, jnp.sum(gradient * values * factor, axis=0))


def dot(left, right, dims=((1,), (0,))):
    return lax.dot_general(left, right, (dims, ((), ())), preferred_element_type=F32)


MESH = pl.DeviceIdType.MESH
ANY = pl.BlockSpec(memory_space=pl.ANY)
VM = pl.BlockSpec(memory_space=pltpu.VMEM)
DMA = pltpu.SemaphoreType.DMA
RANKS = 4


def across(rank, k):
    if k == 3:
        return 3 - rank
    if k == 1:
        return rank + 1 - 2 * lax.rem(rank, 2)
    if k == 2:
        return rank + 2 - 4 * lax.div(rank, 2)
    return rank


def flip(index, bit):
    step = 2**bit
    return index + step - 2 * step * lax.rem(lax.div(index, step), 2)


def inner_plane(rank):
    return (rank == 1) | (rank == 2)


def greet(peers):
    barrier = pltpu.get_barrier_semaphore()
    for peer in peers:
        pl.semaphore_signal(barrier, inc=1, device_id=peer, device_id_type=MESH)
    pl.semaphore_wait(barrier, len(peers))


def line_peers(rank):
    return [{"tensor": across(rank, k)} for k in (1, 2, 3)]


class LineGather:
    def __init__(self, rank, view, pieces, send_sems, recv_sems):
        self.rank, self.view, self.pieces = rank, view, pieces
        self.send_sems, self.recv_sems = send_sems, recv_sems
        self.inner = inner_plane(rank)

    @staticmethod
    def sems(pieces):
        return [DMA((4, pieces)), DMA((RANKS, pieces))]

    def copy(self, source, piece, k, slot):
        return pltpu.make_async_remote_copy(
            src_ref=self.view(source, piece), dst_ref=self.view(source, piece),
            send_sem=self.send_sems.at[slot, piece], recv_sem=self.recv_sems.at[source, piece],
            device_id={"tensor": across(self.rank, k)}, device_id_type=MESH,
        )

    def start(self, piece):
        self.copy(self.rank, piece, 2, 0).start()
        self.copy(self.rank, piece, 1, 1).start()
        pl.when(self.inner)(lambda: self.copy(self.rank, piece, 3, 2).start())

    def arrive(self, k, piece):
        source = across(self.rank, k)
        self.copy(source, piece, 1, 3).wait_recv()
        if k == 2:
            pl.when(self.inner)(lambda: self.copy(source, piece, 1, 3).start())

    def finish(self):
        for piece in range(self.pieces):
            self.copy(self.rank, piece, 2, 0).wait_send()
            self.copy(self.rank, piece, 1, 1).wait_send()

        @pl.when(self.inner)
        def _():
            for piece in range(self.pieces):
                self.copy(self.rank, piece, 3, 2).wait_send()
                self.copy(across(self.rank, 2), piece, 1, 3).wait_send()


def local(source, target, sem):
    return pltpu.make_async_copy(source, target, sem)


class LineScatter:
    def __init__(self, rank, parts, inbox, send_sems, recv_sems, pieces):
        self.rank, self.parts, self.inbox, self.pieces = rank, parts, inbox, pieces
        self.send_sems, self.recv_sems = send_sems, recv_sems
        self.inner = inner_plane(rank)
        self.end = (rank == 0) | (rank == 3)
        self.rows = parts.shape[1] // pieces

    @staticmethod
    def sems(pieces):
        return [DMA((4, pieces)), DMA((4, pieces))]

    def where(self, piece):
        return pl.ds(piece * self.rows, self.rows)

    def copy(self, part, slot, k, piece):
        return pltpu.make_async_remote_copy(
            src_ref=self.parts.at[part, self.where(piece)], dst_ref=self.inbox.at[slot, self.where(piece)],
            send_sem=self.send_sems.at[part, piece], recv_sem=self.recv_sems.at[slot, piece],
            device_id={"tensor": across(self.rank, k)}, device_id_type=MESH,
        )

    def send_far(self, pieces=None):
        for piece in pieces or range(self.pieces):
            pl.when(self.inner)(lambda: self.copy(3, 3, 3, piece).start())
            pl.when(self.end)(lambda: self.copy(3, 0, 1, piece).start())

    def send_two_end(self):
        @pl.when(self.end)
        def _():
            for piece in range(self.pieces):
                self.copy(2, 2, 2, piece).start()

    def send_two_inner(self):
        @pl.when(self.inner)
        def _():
            for piece in range(self.pieces):
                where = self.where(piece)
                self.copy(3, 0, 1, piece).wait_recv()
                self.parts[2, where] = (self.parts[2, where].astype(F32) + self.inbox[0, where].astype(F32)).astype(BF)
                self.copy(2, 2, 2, piece).start()

    def send_near(self):
        for piece in range(self.pieces):
            self.copy(1, 1, 1, piece).start()

    def total(self, target):
        for piece in range(self.pieces):
            where = self.where(piece)
            self.copy(1, 1, 1, piece).wait_recv()
            self.copy(2, 2, 2, piece).wait_recv()
            target[where] = (self.parts[0, where].astype(F32) + self.inbox[1, where].astype(F32)) + self.inbox[2, where].astype(F32)

        @pl.when(self.inner)
        def _():
            for piece in range(self.pieces):
                where = self.where(piece)
                self.copy(3, 3, 3, piece).wait_recv()
                target[where] += self.inbox[3, where].astype(F32)

    def finish(self):
        for piece in range(self.pieces):
            for part in (1, 2, 3):
                self.copy(part, part, part, piece).wait_send()


class GroupReduce:
    def __init__(self, group, dp, send, keep, first, boxes, split, sems):
        self.group, self.dp, self.send, self.keep, self.first, self.boxes = group, dp, send, keep, first, boxes
        self.bits = dp.bit_length() - 1
        self.mates = dp // 2
        columns = first.shape[3]
        self.cols = (pl.ds(0, split), pl.ds(split, columns - split))
        self.sems = sems

    @staticmethod
    def sem_shapes(dp, count):
        mates, bits = dp // 2, dp.bit_length() - 1
        shapes = [DMA((count, mates)), DMA((count, mates))]
        for t in range(1, bits):
            shapes += [DMA((2, count, mates >> t)), DMA((2, count, mates >> t))]
        return shapes

    @staticmethod
    def box_shapes(dp, count, share, columns, split):
        mates, bits = dp // 2, dp.bit_length() - 1
        shapes = [pltpu.VMEM((count, mates, share, columns), BF)]
        for t in range(1, bits):
            shapes += [pltpu.VMEM((count, mates >> t, share, split), BF), pltpu.VMEM((count, mates >> t, share, columns - split), BF)]
        return shapes

    def peers(self):
        return [{"dp": flip(self.group, b)} for b in range(self.bits)]

    def bit(self, b):
        return lax.rem(lax.div(self.group, 2**b), 2)

    def copy0(self, w, j):
        return pltpu.make_async_remote_copy(
            src_ref=self.send(w, 2 * j + 1 - self.bit(0)), dst_ref=self.first.at[w, j],
            send_sem=self.sems[0].at[w, j], recv_sem=self.sems[1].at[w, j],
            device_id={"dp": flip(self.group, 0)}, device_id_type=MESH)

    def place(self, t, half, j, mine):
        n = self.bits
        if half == 0:
            low = sum((self.bit(i) * 2 ** (i - 1) for i in range(1, t)), 0)
            bit = self.bit(t)
            return (2 * j + (bit if mine else 1 - bit)) * 2 ** (t - 1) + low
        high = sum((self.bit(n - i) * 2 ** (n - 1 - i) for i in range(1, t)), 0)
        bit = self.bit(n - t)
        return high + (bit if mine else 1 - bit) * 2 ** (n - 1 - t) + j

    def copy(self, t, half, w, j):
        return pltpu.make_async_remote_copy(
            src_ref=self.keep(w, self.place(t, half, j, False)).at[:, self.cols[half]], dst_ref=self.boxes[2 * (t - 1) + half].at[w, j],
            send_sem=self.sems[2 * t].at[half, w, j], recv_sem=self.sems[2 * t + 1].at[half, w, j],
            device_id={"dp": flip(self.group, t if half == 0 else self.bits - t)}, device_id_type=MESH)

    def start0(self, w):
        for j in range(self.mates):
            self.copy0(w, j).start()

    def start(self, t, w):
        for j in range(self.mates >> t):
            for half in range(2):
                self.copy(t, half, w, j).start()

    def add0(self, w):
        def body(j, carry):
            self.copy0(w, j).wait_recv()
            mine = self.keep(w, j)
            mine[...] = (mine[...].astype(F32) + self.first[w, j].astype(F32)).astype(BF)
            return carry

        lax.fori_loop(0, self.mates, body, 0)
        self.start(1, w)

    def add(self, t, w, target=None):
        for half in range(2):
            def body(j, carry):
                self.copy(t, half, w, j).wait_recv()
                mine = self.keep(w, self.place(t, half, j, True)).at[:, self.cols[half]]
                value = mine[...].astype(F32) + self.boxes[2 * (t - 1) + half][w, j].astype(F32)
                if target is None:
                    mine[...] = value.astype(BF)
                else:
                    target[:, self.cols[half]] = value.astype(target.dtype)
                return carry

            lax.fori_loop(0, self.mates >> t, body, 0)
        if target is None:
            self.start(t + 1, w)

    def finish(self, count):
        def body(w, carry):
            for j in range(self.mates):
                self.copy0(w, j).wait_send()
            for t in range(1, self.bits):
                for j in range(self.mates >> t):
                    for half in range(2):
                        self.copy(t, half, w, j).wait_send()
            return carry

        lax.fori_loop(0, count, body, 0)


def rope_numpy(length):
    half = HD // 2
    frequency = np.float32(10000.0) ** (-np.arange(half, dtype=np.float32) / np.float32(half))
    angles = np.arange(length, dtype=np.float32)[:, None] * frequency[None, :]
    cosine, sine = np.cos(angles), np.sin(angles)
    return (np.concatenate([cosine, cosine], 1), np.concatenate([-sine, sine], 1))


def column_of(row, target):
    target[...] = jnp.transpose(jnp.broadcast_to(row.astype(F32), (HD, row.shape[1])))


def forward_body(dp, tok, cot, seg, wo, wq, wk, wv, gain, gain2, cosine, sine,
                 a1_out, q_out, k_out, v_out, wo_out, cot_out, p_out, dy_out, a2_out, h_out, ob_out,
                 xs, a1s, qkv, ws, wos, dys, obs, ps, hs, segs,
                 x_ss, x_rs, z_ss, z_rs, d_ss, d_rs, c_ss, y_ss, y_rs, o_ss, o_rs, l_sem, k_sem, b_sem):
    rank, group = lax.axis_index("tensor"), lax.axis_index("dp")
    rows, model = tok.shape
    length, width = q_out.shape
    heads = width // HD
    scale = HD ** (-0.5)
    half_rows = rows // 2
    parts = wo.shape[0]
    mates = parts // 2
    member = lax.rem(group, parts)
    base = group - member
    parity = lax.rem(member, 2)
    pair = lax.div(member, 2)
    partner = flip(group, 0)

    def mate(step):
        return lax.rem(pair + step, mates) * 2 + parity

    first = [local(wo.at[member], wos.at[rank, member], l_sem.at[0]), local(tok, xs.at[rank], l_sem.at[1]), local(cot, dys.at[rank], l_sem.at[2])]
    weights = [local(w, ws.at[i], l_sem.at[3 + i]) for i, w in enumerate((wq, wk, wv))]
    for c in first + weights:
        c.start()
    column_of(seg[...], segs)
    greet(line_peers(rank) + [{"dp": partner}] + [{"dp": base + mate(s)} for s in range(1, mates)])
    out_gather = LineGather(rank, lambda s, p: wos.at[s, member], 1, z_ss, z_rs)
    gather = LineGather(rank, lambda s, p: xs.at[s, pl.ds(p * half_rows, half_rows)], 2, x_ss, x_rs)

    def near(k, source):
        return pltpu.make_async_remote_copy(
            src_ref=dys.at[source], dst_ref=dys.at[source], send_sem=y_ss.at[k], recv_sem=y_rs.at[k],
            device_id={"tensor": across(rank, k)}, device_id_type=MESH)

    inner = inner_plane(rank)
    attended = LineGather(rank, lambda s, p: obs.at[s, :, pl.ds(pl.multiple_of(p * HD, HD), HD)], heads, o_ss, o_rs)
    first[0].wait()
    out_gather.start(0)
    first[1].wait()
    gather.start(0)
    gather.start(1)
    first[2].wait()
    real = segs[pl.ds(pl.multiple_of(rank * rows, rows), rows), :1] >= 0.0
    dys[rank] = jnp.where(real, dys[rank], jnp.zeros((rows, model), BF))
    near(1, rank).start()
    pl.when(inner)(near(3, rank).start)
    keep = [local(dys.at[rank], cot_out, k_sem.at[0])]
    keep[0].start()
    for w in weights:
        w.wait()

    def chunk(source):
        x = xs[source].astype(F32)
        a1s[source] = (x * norm_factor(x) * gain[...].reshape(1, model)).astype(BF)
        where = pl.ds(pl.multiple_of(source * rows, rows), rows)
        for i in range(3):
            product = dot(a1s[source], ws[i])
            for h in range(heads):
                head = product[:, h * HD : (h + 1) * HD]
                if i < 2:
                    head = head * cosine[where, :] + pltpu.roll(head, HD // 2, 1) * sine[where, :]
                qkv[i, where, h * HD : (h + 1) * HD] = head.astype(BF)

    def chunks(i, carry):
        @pl.when(i == 1)
        def _():
            for k in (1, 2, 3):
                out_gather.arrive(k, 0)
            for step in range(1, mates):
                mate_copy(step).start()
            core_copy(0, parity).start()
            for piece in range(2):
                gather.arrive(1, piece)
                gather.arrive(2, piece)

        @pl.when(i == 3)
        def _():
            for step in range(1, mates):
                mate_arrival(step).wait_recv()
                core_copy(step, parity).start()
            for piece in range(2):
                gather.arrive(3, piece)

        chunk(pick(i, [rank, across(rank, 1), across(rank, 2), across(rank, 3)]))
        return carry

    def mate_copy(step):
        return pltpu.make_async_remote_copy(
            src_ref=wos.at[:, member], dst_ref=wos.at[:, member], send_sem=d_ss.at[step], recv_sem=d_rs.at[member],
            device_id={"dp": base + mate(step)}, device_id_type=MESH)

    def mate_arrival(step):
        piece = mate(step)
        return pltpu.make_async_remote_copy(
            src_ref=wos.at[:, piece], dst_ref=wos.at[:, piece], send_sem=d_ss.at[step], recv_sem=d_rs.at[piece],
            device_id={"dp": base + piece}, device_id_type=MESH)

    def core_copy(step, owner):
        piece = lax.rem(pair + step, mates) * 2 + owner
        return pltpu.make_async_remote_copy(
            src_ref=wos.at[:, piece], dst_ref=wos.at[:, piece], send_sem=c_ss.at[step], recv_sem=d_rs.at[piece],
            device_id={"dp": partner}, device_id_type=MESH)

    lax.fori_loop(0, RANKS, chunks, 0)
    keep += [local(a1s, a1_out, k_sem.at[1])] + [local(qkv.at[i], t, k_sem.at[2 + i]) for i, t in enumerate((q_out, k_out, v_out))]
    for c in keep[1:]:
        c.start()

    def head(h, carry):
        cols = pl.ds(pl.multiple_of(h * HD, HD), HD)
        for start in range(0, length, QB):
            extent = start + QB
            scores = dot(qkv[0, start:extent, cols], qkv[1, :extent, cols], ((1,), (1,)))
            row_ids = lax.broadcasted_iota(jnp.int32, (QB, extent), 0) + start
            col_ids = lax.broadcasted_iota(jnp.int32, (QB, extent), 1)
            allowed = (col_ids <= row_ids) & (segs[start:extent, :1] == seg[:, :extent].astype(F32))
            logits = jnp.where(allowed, scores * scale, NEG)
            expo = jnp.exp(logits - jnp.max(logits, axis=-1, keepdims=True))
            probs = (expo * (1.0 / jnp.sum(expo, axis=-1, keepdims=True))).astype(BF)
            ps[h, start:extent, :extent] = probs
            obs[rank, start:extent, cols] = dot(probs, qkv[2, :extent, cols]).astype(BF)
        attended.start(h)
        return carry

    lax.fori_loop(0, heads, head, 0)
    for step in range(mates):
        core_copy(step, 1 - parity).wait_recv()
    more = [local(ps, p_out, k_sem.at[5]), local(wos, wo_out, k_sem.at[6])]
    for c in more:
        c.start()
    keep += more

    def add(source, first=False, last=False):
        def block(b, carry):
            weight = wos[source].reshape(width, model)
            part = dot(obs[source, pl.ds(pl.multiple_of(b * rows, rows), rows), :], weight)
            total = part + (xs[b].astype(F32) if first else hs[b])
            hs[b] = total
            if last:
                xs[b] = (total * norm_factor(total) * gain2[...].reshape(1, model)).astype(BF)
                local(xs.at[b], a2_out.at[b], b_sem.at[b]).start()
            return carry

        lax.fori_loop(0, RANKS, block, 0)

    add(rank, first=True)
    for piece in range(heads):
        attended.arrive(2, piece)
    for piece in range(heads):
        attended.arrive(1, piece)
    add(across(rank, 2))
    add(across(rank, 1))
    one, three = across(rank, 1), across(rank, 3)
    near(1, one).wait_recv()
    more = [local(dys.at[one], dy_out.at[one], l_sem.at[0])]
    more[0].start()
    inner_copy = local(dys.at[three], dy_out.at[three], l_sem.at[1])

    @pl.when(inner)
    def _():
        near(3, three).wait_recv()
        inner_copy.start()

    for piece in range(heads):
        attended.arrive(3, piece)
    gather.finish()
    add(across(rank, 3), last=True)
    more += [local(hs.at[rank], h_out, l_sem.at[2]),
             local(obs.at[:, pl.ds(pl.multiple_of(rank * rows, rows), rows)], ob_out, l_sem.at[3])]
    for c in more[1:]:
        c.start()
    out_gather.finish()
    for step in range(1, mates):
        mate_copy(step).wait_send()
    for step in range(mates):
        core_copy(step, parity).wait_send()
    attended.finish()
    near(1, rank).wait_send()

    @pl.when(inner)
    def _():
        near(3, rank).wait_send()
        inner_copy.wait()

    for c in keep + more:
        c.wait()
    for b in range(RANKS):
        local(xs.at[b], a2_out.at[b], b_sem.at[b]).wait()


def forward_kernel(dp, tokens, cotangent, segments, w_out, w_query, w_key, w_value, gain, gain2, cosine, sine):
    rows, model = tokens.shape
    width = w_query.shape[1]
    heads = width // HD
    length = RANKS * rows
    parts = min(dp, 8)
    mates = parts // 2
    shape = (RANKS, rows, model)
    shard, wide = jax.ShapeDtypeStruct(shape, BF), jax.ShapeDtypeStruct((length, width), BF)
    outs = pl.pallas_call(
        functools.partial(forward_body, dp),
        in_specs=[ANY, ANY, VM, ANY, ANY, ANY, ANY, VM, VM, VM, VM],
        out_specs=[ANY] * 11,
        out_shape=[shard, wide, wide, wide, jax.ShapeDtypeStruct((RANKS, parts, width // parts, model), BF),
                   jax.ShapeDtypeStruct((rows, model), BF), jax.ShapeDtypeStruct((heads, length, length), BF), shard, shard,
                   jax.ShapeDtypeStruct((rows, model), F32), jax.ShapeDtypeStruct((RANKS, rows, width), BF)],
        scratch_shapes=[
            pltpu.VMEM(shape, BF), pltpu.VMEM(shape, BF), pltpu.VMEM((3, length, width), BF), pltpu.VMEM((3, model, width), BF),
            pltpu.VMEM((RANKS, parts, width // parts, model), BF), pltpu.VMEM(shape, BF), pltpu.VMEM((RANKS, length, width), BF),
            pltpu.VMEM((heads, length, length), BF), pltpu.VMEM(shape, F32), pltpu.VMEM((length, HD), F32),
            *LineGather.sems(2), *LineGather.sems(1), DMA((mates,)), DMA((parts,)), DMA((mates,)),
            DMA((4,)), DMA((4,)), *LineGather.sems(heads), DMA((6,)), DMA((7,)), DMA((RANKS,)),
        ],
        compiler_params=pltpu.CompilerParams(collective_id=1, has_side_effects=True, vmem_limit_bytes=62 << 20),
        name="forward_gather",
    )(tokens, cotangent, segments, w_out.reshape(parts, width // parts, model), w_query, w_key, w_value, gain, gain2, cosine, sine)
    a1_all, query, key, value, w_out_all, cot_own, probs, dy, a2, hidden, attended = outs
    return a1_all, query, key, value, w_out_all.reshape(RANKS, width, model), cot_own, probs, dy, a2, hidden, attended


def pick(step, choices):
    value = choices[-1]
    for i in range(len(choices) - 1):
        value = jnp.where(step == i, choices[i], value)
    return value


FT = 768
WB = 384


def mlp_body(a2, dy, wg, wu, wd, hid, cot, gran, gain,
             g_out, down_out, dh_out, gain_out,
             lefts, acts, ws, parts, inbox, stage, downs, hs, cots, total, gains, r_ss, r_rs, y_ss, y_rs, l_sem, s_sem):
    rank = lax.axis_index("tensor")
    rows, model = cot.shape
    width = wg.shape[1]
    per, share = stage.shape[1], stage.shape[2]
    end = (rank == 0) | (rank == 3)

    def part(source):
        return pl.ds(pl.multiple_of(source * rows, rows), rows)

    def dy_load(k, sem):
        return local(dy.at[across(rank, k)], lefts.at[1, part(across(rank, k))], l_sem.at[sem])

    inner = inner_plane(rank)
    half = rows // 2

    def piece_of(source, piece):
        return pl.ds(pl.multiple_of(source * rows + piece * half, half), half)

    def hand(slot, shard, piece, k, kept=True):
        where = piece_of(across(rank, shard), piece)
        source = dy.at[across(rank, shard), pl.ds(piece * half, half)] if kept else lefts.at[1, where]
        return pltpu.make_async_remote_copy(
            src_ref=source, dst_ref=lefts.at[1, where], send_sem=y_ss.at[slot, piece], recv_sem=y_rs.at[slot, piece],
            device_id={"tensor": across(rank, k)}, device_id_type=MESH)

    def mid(piece):
        return hand(0, 1, piece, 3)

    def second(piece):
        return hand(1, 3, piece, 1)

    def third(piece):
        return hand(2, 2, piece, 1, False)

    def arrived(slot, shard, piece):
        where = piece_of(across(rank, shard), piece)
        return pltpu.make_async_remote_copy(
            src_ref=lefts.at[1, where], dst_ref=lefts.at[1, where], send_sem=y_ss.at[slot, piece], recv_sem=y_rs.at[slot, piece],
            device_id={"tensor": across(rank, 1)}, device_id_type=MESH)

    own = local(cot, lefts.at[1, part(rank)], l_sem.at[7])
    own.start()
    loads = [local(wg, ws.at[0], l_sem.at[0]), local(a2, lefts.at[0], l_sem.at[1]), local(wu, ws.at[1], l_sem.at[2]),
             dy_load(1, 3), local(wd, ws.at[2], l_sem.at[4])]
    inner_load = dy_load(3, 8)
    pl.when(inner)(inner_load.start)
    late = [local(hid, hs, l_sem.at[5]), local(cot, cots, l_sem.at[6])]
    for c in loads + late:
        c.start()
    greet(line_peers(rank))

    @pl.when(inner)
    def _():
        mid(0).start()
        second(0).start()
        mid(1).start()
        second(1).start()

    scatter = LineScatter(rank, parts, inbox, r_ss, r_rs, 2)
    planes = [rank] + [across(rank, k) for k in (1, 2, 3)]
    kinds = [jnp.where(end, a, b) for a, b in zip((1, 2, 0, 3), (3, 1, 2, 0))]
    order = [jnp.where(end, planes[a], planes[b]) for a, b in zip((1, 2, 0, 3), (3, 1, 2, 0))]
    limit = FF // 8 * lax.shift_left(1, gran[0] - 1) - rank * width

    def step(i, carry):
        where = pl.ds(pl.multiple_of(pick(i, order) * rows, rows), rows)

        def tile(t, inner_carry):
            cols = pl.ds(pl.multiple_of(t * FT, FT), FT)

            @pl.when((i == 0) & (t == 0))
            def _():
                loads[0].wait()
                loads[1].wait()

            gate = dot(lefts[0, where, :], ws[0, :, cols])

            @pl.when((i == 0) & (t == 0))
            def _():
                loads[2].wait()

            up = dot(lefts[0, where, :], ws[1, :, cols])

            @pl.when((i == 0) & (t == 0))
            def _():
                loads[3].wait()
                pl.when(inner)(inner_load.wait)
                own.wait()
                loads[4].wait()

            @pl.when((i == 1) & (t == 0) & end)
            def _():
                for piece in range(2):
                    arrived(1, 2, piece).wait_recv()

            @pl.when((i == 3) & (t == 0) & end)
            def _():
                for piece in range(2):
                    arrived(2, 3, piece).wait_recv()

            dz = dot(lefts[1, where, :], ws[2, cols, :], ((1,), (1,)))
            unit = lax.broadcasted_iota(jnp.int32, gate.shape, 1) + t * FT
            mask = unit < limit
            sigma = jax.nn.sigmoid(gate)
            active = jnp.where(mask, gate * sigma, 0.0)
            acts[2, where, cols] = (active * up).astype(BF)
            acts[0, where, cols] = jnp.where(mask, dz * up * sigma * (1.0 + gate * (1.0 - sigma)), 0.0).astype(BF)
            acts[1, where, cols] = (dz * active).astype(BF)
            return inner_carry

        lax.fori_loop(0, width // FT, tile, 0)

        def back(t, inner_carry):
            cols = pl.ds(pl.multiple_of(t * FT, FT), FT)
            parts[pick(i, kinds), :, cols] = (
                dot(acts[0, where, :], ws[0, cols, :], ((1,), (1,))) + dot(acts[1, where, :], ws[1, cols, :], ((1,), (1,)))
            ).astype(BF)
            return inner_carry

        lax.fori_loop(0, model // FT, back, 0)

        @pl.when(inner & (i == 0))
        def _():
            scatter.send_far()
            arrived(0, 2, 0).wait_recv()
            third(0).start()

        @pl.when(inner & (i == 1))
        def _():
            arrived(0, 2, 1).wait_recv()
            third(1).start()
            scatter.send_near()

        pl.when(end & (i == 0))(scatter.send_near)
        pl.when(end & (i == 1))(scatter.send_two_end)
        pl.when(end & (i == 3))(scatter.send_far)
        return carry

    lax.fori_loop(0, 4, step, 0)
    blocks = model // WB

    def put(i, slot):
        w, b = lax.div(i, blocks), lax.rem(i, blocks)
        return local(stage.at[slot], g_out.at[w, pl.ds(b * per, per)], s_sem.at[slot])

    def grads(i, carry):
        slot = lax.rem(i, 2)
        w, b = lax.div(i, blocks), lax.rem(i, blocks)
        left = lax.div(w, 2)
        cols = pl.ds(pl.multiple_of(b * WB, WB), WB)
        value = dot(lefts[left, :, cols], acts[w], ((0,), (0,)))
        pl.when(i >= 2)(lambda: put(i - 2, slot).wait())
        low = value.astype(BF)
        for p in range(per):
            stage[slot, p] = low[p * share : (p + 1) * share]
        put(i, slot).start()
        return carry

    lax.fori_loop(0, 3 * blocks - 3, grads, 0)
    scatter.send_two_inner()
    lax.fori_loop(3 * blocks - 3, 3 * blocks, grads, 0)

    def down(i, carry):
        where = pl.ds(pl.multiple_of(pick(i, order) * rows, rows), rows)
        downs[pick(i, kinds)] = dot(acts[2, where, :], ws[2]).astype(BF)
        return carry

    lax.fori_loop(0, 4, down, 0)
    keep = local(downs, down_out, l_sem.at[0])
    keep.start()
    for c in late:
        c.wait()
    scatter.total(total)
    values, gradient = hs[...], total[...]
    factor = norm_factor(values)
    back_rows, gain_rows = norm_back(values, factor, gain[...].reshape(1, model), gradient)
    total[...] = cots[...].astype(F32) + back_rows
    gains[...] = gain_rows.reshape(1, model)
    last = [local(total, dh_out, l_sem.at[1]), local(gains, gain_out, l_sem.at[2])]
    for c in last:
        c.start()
    scatter.finish()

    @pl.when(inner)
    def _():
        for piece in range(2):
            mid(piece).wait_send()
            second(piece).wait_send()
            third(piece).wait_send()

    put(3 * blocks - 2, 0).wait()
    put(3 * blocks - 1, 1).wait()
    for c in last + [keep]:
        c.wait()


def mlp_kernel(dp, a2, dy, w_gate, w_up, w_down, hidden_own, cot_own, granularity, gain):
    rows, model = cot_own.shape
    width = w_gate.shape[1]
    share = model // dp
    shard = (RANKS, rows, model)
    return pl.pallas_call(
        mlp_body,
        in_specs=[ANY] * 7 + [pl.BlockSpec(memory_space=pltpu.SMEM), VM],
        out_specs=[ANY] * 4,
        out_shape=[jax.ShapeDtypeStruct((3, dp, share, width), BF), jax.ShapeDtypeStruct(shard, BF),
                   jax.ShapeDtypeStruct((rows, model), F32), jax.ShapeDtypeStruct((1, model), F32)],
        scratch_shapes=[
            pltpu.VMEM((2, RANKS * rows, model), BF), pltpu.VMEM((3, RANKS * rows, width), BF), pltpu.VMEM((3, model, width), BF),
            pltpu.VMEM(shard, BF), pltpu.VMEM(shard, BF), pltpu.VMEM((2, WB // share, share, width), BF), pltpu.VMEM(shard, BF),
            pltpu.VMEM((rows, model), F32), pltpu.VMEM((rows, model), BF), pltpu.VMEM((rows, model), F32), pltpu.VMEM((1, model), F32),
            *LineScatter.sems(2), DMA((3, 2)), DMA((3, 2)), DMA((9,)), DMA((2,)),
        ],
        compiler_params=pltpu.CompilerParams(collective_id=3, has_side_effects=True, vmem_limit_bytes=63 << 20),
        name="mlp_scatter",
    )(a2.reshape(-1, model), dy, w_gate, w_up, w_down, hidden_own, cot_own, granularity, gain)


def attention_back_body(dp, dh, wo_all, downs, grads, q, k, v, p_all, hid, cosine, sine,
                        out_out, dq_out, dk_out, dv_out, gf_out,
                        dhs, low, wos, parts, inbox, dobs, dos, qkv, ps, ds, dqkv, hs, outs, kept, finals, *rest):
    rank, group = lax.axis_index("tensor"), lax.axis_index("dp")
    rounds = 2 * (dp.bit_length() - 1)
    first, boxes, rest = rest[0], rest[1 : rounds - 1], rest[rounds - 1 :]
    sems, (r_ss, r_rs, a_ss, a_rs, l_sem, p_sem, f_sem) = rest[:rounds], rest[rounds:]
    rows, model = dh.shape
    length, width = q.shape
    heads, half, scale = width // HD, HD // 2, HD ** (-0.5)
    count = grads.shape[0]
    parity = lax.rem(group, 2)
    loads = [local(downs, parts, l_sem.at[2]), local(dh, dhs, l_sem.at[0]), local(wo_all, wos, l_sem.at[1])]
    owns = [local(grads.at[w, :, parity], kept.at[w], f_sem.at[w]) for w in range(count)]
    late = [local(t, qkv.at[i], l_sem.at[3 + i]) for i, t in enumerate((q, k, v))] + [local(hid, hs, l_sem.at[6])]
    for c in loads + owns + late:
        c.start()

    def probs(h):
        return local(p_all.at[h], ps.at[lax.rem(h, 2)], p_sem.at[lax.rem(h, 2)])

    probs(0).start()
    probs(1).start()
    reduce = GroupReduce(
        group, dp, lambda w, d: grads.at[w, lax.div(d, 2), lax.rem(d, 2)], lambda w, j: kept.at[w, j], first, boxes, model // 2, sems)
    greet(line_peers(rank) + reduce.peers())
    for w in range(count):
        reduce.start0(w)
    scatter = LineScatter(rank, parts, inbox, r_ss, r_rs, 2)
    loads[0].wait()
    scatter.send_far([0])

    def exchange(k, source):
        where = pl.ds(pl.multiple_of(source * rows, rows), rows)
        return pltpu.make_async_remote_copy(
            src_ref=dobs.at[k - 1], dst_ref=dos.at[where], send_sem=a_ss.at[k], recv_sem=a_rs.at[source],
            device_id={"tensor": across(rank, k)}, device_id_type=MESH)

    loads[1].wait()
    low[...] = dhs[...].astype(BF)
    loads[2].wait()
    for k in (3, 2, 1):
        dobs[k - 1] = dot(low[...], wos[across(rank, k)], ((1,), (1,))).astype(BF)
        exchange(k, rank).start()
    scatter.send_far([1])
    scatter.send_two_end()
    scatter.send_near()
    dos[pl.ds(pl.multiple_of(rank * rows, rows), rows), :] = dot(low[...], wos[rank], ((1,), (1,))).astype(BF)
    for c in owns:
        c.wait()

    def fold(w, carry):
        reduce.add0(w)
        return carry

    lax.fori_loop(0, count, fold, 0)
    for c in late:
        c.wait()
    for k in (3, 2, 1):
        exchange(k, across(rank, k)).wait_recv()

    def head(h, carry):
        cols = pl.ds(pl.multiple_of(h * HD, HD), HD)
        slot = lax.rem(h, 2)
        probs(h).wait()

        def unrope(grad, start):
            where = slice(start, start + QB)
            return (grad * cosine[where, :] - pltpu.roll(grad, half, 1) * sine[where, :]).astype(BF)

        for start in range(0, length, QB):
            extent = start + QB
            where = slice(start, extent)
            grad_p = dot(dos[where, cols], qkv[2, :extent, cols], ((1,), (1,)))
            p = ps[slot, where, :extent].astype(F32)
            weighted = p * grad_p
            delta = jnp.sum(weighted, axis=-1, keepdims=True)
            ds[where, :extent] = ((weighted - p * delta) * scale).astype(BF)
            dqkv[0, where, cols] = unrope(dot(ds[where, :extent], qkv[1, :extent, cols]), start)
        for start in range(0, length, QB):
            where = slice(start, start + QB)
            dqkv[1, where, cols] = unrope(dot(ds[start:, where], qkv[0, start:, cols], ((0,), (0,))), start)
            dqkv[2, where, cols] = dot(ps[slot, start:, where], dos[start:, cols], ((0,), (0,))).astype(BF)
        pl.when(h + 2 < heads)(lambda: probs(h + 2).start())
        return carry

    lax.fori_loop(0, heads, head, 0)
    done = [local(dqkv.at[i], t, l_sem.at[i]) for i, t in enumerate((dq_out, dk_out, dv_out))]
    for c in done:
        c.start()
    reduce.add(1, 0)
    scatter.send_two_inner()
    reduce.add(1, 1)
    reduce.add(1, 2)
    for t in range(2, reduce.bits - 1):
        for w in range(count):
            reduce.add(t, w)

    def put(w):
        return local(finals.at[w], gf_out.at[w], f_sem.at[w])

    for w in range(count):
        reduce.add(reduce.bits - 1, w, finals.at[w])
        put(w).start()
    scatter.total(dhs)
    outs[...] = (hs[...] + dhs[...]).astype(BF)
    last = local(outs, out_out, l_sem.at[3])
    last.start()
    scatter.finish()
    for k in (1, 2, 3):
        exchange(k, rank).wait_send()
    reduce.finish(count)
    for w in range(count):
        put(w).wait()
    for c in done + [last]:
        c.wait()


def attention_back_kernel(dp, grad_hidden, w_out_all, down_parts, grads_ff, query, key, value, probs_low, hidden_own, cosine, sine):
    rows, model = grad_hidden.shape
    length, width = query.shape
    count, _, share, columns = grads_ff.shape
    mates = dp // 2
    shard = (RANKS, rows, model)
    heads = jax.ShapeDtypeStruct((length, width), BF)
    return pl.pallas_call(
        functools.partial(attention_back_body, dp),
        in_specs=[ANY] * 9 + [VM, VM],
        out_specs=[ANY] * 5,
        out_shape=[jax.ShapeDtypeStruct((rows, model), BF), heads, heads, heads, jax.ShapeDtypeStruct((count, share, columns), BF)],
        scratch_shapes=[
            pltpu.VMEM((rows, model), F32), pltpu.VMEM((rows, model), BF), pltpu.VMEM((RANKS, width, model), BF),
            pltpu.VMEM(shard, BF), pltpu.VMEM(shard, BF), pltpu.VMEM((3, rows, width), BF), pltpu.VMEM((length, width), BF),
            pltpu.VMEM((3, length, width), BF), pltpu.VMEM((2, length, length), BF), pltpu.VMEM((length, length), BF),
            pltpu.VMEM((3, length, width), BF), pltpu.VMEM((rows, model), F32), pltpu.VMEM((rows, model), BF),
            pltpu.VMEM((count, mates, share, columns), BF), pltpu.VMEM((count, share, columns), BF),
            *GroupReduce.box_shapes(dp, count, share, columns, columns // 2), *GroupReduce.sem_shapes(dp, count),
            *LineScatter.sems(2), DMA((4,)), DMA((RANKS,)), DMA((7,)), DMA((2,)), DMA((count,)),
        ],
        compiler_params=pltpu.CompilerParams(collective_id=4, has_side_effects=True, vmem_limit_bytes=63 << 20),
        name="attention_back",
    )(grad_hidden, w_out_all, down_parts, grads_ff.reshape(count, mates, 2, share, columns),
      query, key, value, probs_low, hidden_own, cosine, sine)


def input_back_body(dp, dq, dk, dv, a1, wq, wk, wv, tok, dh, ob, gain, gain2,
                    dx_out, gains_out, gqkv_out, gout_out,
                    dqkv, a1s, ws, xs, dhs, low, obs, parts, inbox, g1, g2, f1, f2, f2_low, box2, f3, gbuf, gbox, total, dxs, *rest):
    rank, group = lax.axis_index("tensor"), lax.axis_index("dp")
    bits = dp.bit_length() - 1
    boxes = [rest[: 2 * bits - 1], rest[2 * bits - 1 : 4 * bits - 2]]
    rest = rest[4 * bits - 2 :]
    sems = [rest[: 2 * bits], rest[2 * bits : 4 * bits]]
    r_ss, r_rs, z_ss, z_rs, g_ss, g_rs, l_sem = rest[4 * bits :]
    rows, model = tok.shape
    width = dq.shape[1]
    share = g1.shape[1]
    per = WB // share
    parity = lax.rem(group, 2)
    loads = [local(t, dqkv.at[i], l_sem.at[i]) for i, t in enumerate((dq, dk, dv))]
    loads += [local(t, ws.at[i], l_sem.at[3 + i]) for i, t in enumerate((wq, wk, wv))]
    late = [local(a1, a1s, l_sem.at[8]), local(dh, dhs, l_sem.at[6]), local(ob, obs, l_sem.at[7]), local(tok, xs, l_sem.at[9])]
    for c in loads + late:
        c.start()
    scatter = LineScatter(rank, parts, inbox, r_ss, r_rs, 2)
    mixed = GroupReduce(group, dp, lambda w, d: g1.at[d], lambda w, j: g1.at[2 * j + parity], boxes[0][0], boxes[0][1:], f1.shape[1] // 256 * 128, sems[0])
    output = GroupReduce(group, dp, lambda w, d: g2.at[d], lambda w, j: g2.at[2 * j + parity], boxes[1][0], boxes[1][1:], f2.shape[1] // 256 * 128, sems[1])
    greet(line_peers(rank) + mixed.peers())
    order = [across(rank, k) for k in (3, 2, 1, 0)]
    for c in loads:
        c.wait()

    def step(i, carry):
        where = pl.ds(pl.multiple_of(pick(i, order) * rows, rows), rows)
        value = dot(dqkv[0, where, :], ws[0], ((1,), (1,)))
        for s in (1, 2):
            value += dot(dqkv[s, where, :], ws[s], ((1,), (1,)))
        parts[3 - i] = value.astype(BF)
        pl.when(i == 0)(scatter.send_far)
        pl.when(i == 1)(scatter.send_two_end)
        pl.when(i == 2)(scatter.send_near)

        @pl.when(i == 0)
        def _():
            late[0].wait()

        row = jnp.sum(value * a1s[where, :].astype(F32), axis=0, keepdims=True)
        gbuf[0, 0:1, :] = jnp.where(i == 0, row, gbuf[0, 0:1, :] + row)
        return carry

    gbuf[0, 0:1, :] = jnp.zeros((1, model), F32)
    lax.fori_loop(0, 4, step, 0)
    gbuf[0, 0:1, :] = gbuf[0, 0:1, :] / gain[...].reshape(1, model)
    gbuf[0, 1:2, :] = gain2[...]

    def swap(t):
        return pltpu.make_async_remote_copy(
            src_ref=gbuf.at[t], dst_ref=gbox.at[t], send_sem=g_ss.at[t], recv_sem=g_rs.at[t], device_id={"dp": flip(group, t)}, device_id_type=MESH)

    def advance(t):
        swap(t).wait_recv()
        gbuf[t + 1] = gbuf[t] + gbox[t]
        if t + 1 < bits:
            swap(t + 1).start()

    def share_gains(k, source):
        return pltpu.make_async_remote_copy(
            src_ref=gbuf.at[bits], dst_ref=gbox.at[bits + source], send_sem=g_ss.at[bits + k], recv_sem=g_rs.at[bits + source],
            device_id={"tensor": across(rank, k)}, device_id_type=MESH)

    swap(0).start()
    for c in late[1:]:
        c.wait()
    low[...] = dhs[...].astype(BF)

    def out_block(b, carry):
        cols = pl.ds(pl.multiple_of(b * WB, WB), WB)
        for r in range(RANKS):
            value = dot(low[:, cols], obs[r], ((0,), (0,))).astype(BF)
            for p in range(per):
                g2[b * per + p, :, r * width : (r + 1) * width] = value[p * share : (p + 1) * share]
        return carry

    lax.fori_loop(0, model // WB, out_block, 0)
    advance(0)
    output.start0(0)

    def mixed_block(b, carry):
        cols = pl.ds(pl.multiple_of(b * WB, WB), WB)
        for s in range(3):
            value = dot(a1s[:, cols], dqkv[s], ((0,), (0,))).astype(BF)
            for p in range(per):
                g1[b * per + p, :, s * width : (s + 1) * width] = value[p * share : (p + 1) * share]
        return carry

    lax.fori_loop(0, model // WB, mixed_block, 0)
    for t in range(1, bits):
        advance(t)
    for k in (1, 2, 3):
        share_gains(k, rank).start()
    gbox[bits + rank] = gbuf[bits]
    mixed.start0(0)
    output.add0(0)
    mixed.add0(0)
    scatter.send_two_inner()
    for t in range(1, bits - 1):
        output.add(t, 0)
        mixed.add(t, 0)
    output.add(bits - 1, 0, f2)
    ends = LineScatter(rank, f2_low, box2, z_ss, z_rs, 1)
    for k in range(4):
        column = pl.ds(pl.multiple_of(across(rank, k) * width, HD), width)
        f2_low[k] = f2[:, column].astype(BF)
    ends.send_far()
    ends.send_two_end()
    ends.send_near()
    mixed.add(bits - 1, 0, f1)
    done = [local(f1, gqkv_out, l_sem.at[0])]
    done[0].start()
    scatter.total(total)
    values, gradient = xs[...].astype(F32), total[...]
    back_rows, _ = norm_back(values, norm_factor(values), gain[...].reshape(1, model), gradient)
    dxs[...] = (dhs[...] + back_rows).astype(BF)
    done.append(local(dxs, dx_out, l_sem.at[1]))
    done[1].start()
    for k in (1, 2, 3):
        share_gains(k, across(rank, k)).wait_recv()
    for t in range(bits):
        swap(t).wait_send()
    gbuf[0] = ((gbox[bits] + gbox[bits + 1]) + gbox[bits + 2]) + gbox[bits + 3]
    done.append(local(gbuf.at[0], gains_out, l_sem.at[2]))
    done[2].start()
    ends.send_two_inner()
    ends.total(f3)
    done.append(local(f3, gout_out, l_sem.at[3]))
    done[3].start()
    scatter.finish()
    ends.finish()
    mixed.finish(1)
    output.finish(1)
    for k in (1, 2, 3):
        share_gains(k, rank).wait_send()
    for c in done:
        c.wait()


def input_back_kernel(dp, grad_q, grad_k, grad_v, a1_all, w_query, w_key, w_value, tokens, grad_hidden, attended_own, gain, gain_two):
    rows, model = tokens.shape
    length, width = grad_q.shape
    share = model // dp
    bits = dp.bit_length() - 1
    shard = (RANKS, rows, model)
    wide = (3 * width, RANKS * width)
    splits = [w // 256 * 128 for w in wide]
    return pl.pallas_call(
        functools.partial(input_back_body, dp),
        in_specs=[ANY] * 10 + [VM, VM],
        out_specs=[ANY] * 4,
        out_shape=[jax.ShapeDtypeStruct((rows, model), BF), jax.ShapeDtypeStruct((2, model), F32),
                   jax.ShapeDtypeStruct((share, wide[0]), F32), jax.ShapeDtypeStruct((share, width), F32)],
        scratch_shapes=[
            pltpu.VMEM((3, length, width), BF), pltpu.VMEM((length, model), BF), pltpu.VMEM((3, model, width), BF),
            pltpu.VMEM((rows, model), BF), pltpu.VMEM((rows, model), F32), pltpu.VMEM((rows, model), BF), pltpu.VMEM((RANKS, rows, width), BF),
            pltpu.VMEM(shard, BF), pltpu.VMEM(shard, BF),
            pltpu.VMEM((dp, share, wide[0]), BF), pltpu.VMEM((dp, share, wide[1]), BF),
            pltpu.VMEM((share, wide[0]), F32), pltpu.VMEM((share, wide[1]), F32),
            pltpu.VMEM((RANKS, share, width), BF), pltpu.VMEM((RANKS, share, width), BF), pltpu.VMEM((share, width), F32),
            pltpu.VMEM((bits + 1, 2, model), F32), pltpu.VMEM((bits + RANKS, 2, model), F32),
            pltpu.VMEM((rows, model), F32), pltpu.VMEM((rows, model), BF),
            *GroupReduce.box_shapes(dp, 1, share, wide[0], splits[0]), *GroupReduce.box_shapes(dp, 1, share, wide[1], splits[1]),
            *GroupReduce.sem_shapes(dp, 1), *GroupReduce.sem_shapes(dp, 1),
            *LineScatter.sems(2), *LineScatter.sems(1), DMA((bits + RANKS,)), DMA((bits + RANKS,)), DMA((10,)),
        ],
        compiler_params=pltpu.CompilerParams(collective_id=5, has_side_effects=True, vmem_limit_bytes=63 << 20),
        name="input_back",
    )(grad_q, grad_k, grad_v, a1_all.reshape(length, model), w_query, w_key, w_value, tokens, grad_hidden, attended_own, gain, gain_two)


def finish_body(output, dx, gains, mixed, out_t, ff,
                output_out, dx_out, gain1_out, gain2_out, q_out, k_out, v_out, wo_out, gate_out, up_out, down_out,
                b0, b1, gs, g1, g2, ms, ot, fs, gate, up, down, i_sem, o_sem):
    width = q_out.shape[1]
    loads = [local(s, t, i_sem.at[i]) for i, (s, t) in enumerate(
        ((ff.at[2], fs.at[2]), (ff.at[0], fs.at[0]), (ff.at[1], fs.at[1]), (mixed, ms), (output, b0), (dx, b1), (out_t, ot), (gains, gs)))]
    for c in loads:
        c.start()
    sent = []

    def put(source, target):
        sent.append(local(source, target, o_sem.at[len(sent)]))
        sent[-1].start()

    loads[1].wait()
    gate[...] = fs[0].astype(F32)
    put(gate, gate_out)
    loads[2].wait()
    up[...] = fs[1].astype(F32)
    put(up, up_out)
    loads[4].wait()
    put(b0, output_out)
    loads[5].wait()
    put(b1, dx_out)
    loads[3].wait()
    for i, target in enumerate((q_out, k_out, v_out)):
        put(ms.at[:, pl.ds(i * width, width)], target)
    loads[0].wait()
    down[...] = fs[2].astype(F32)
    put(down, down_out)
    loads[6].wait()
    put(ot, wo_out)
    loads[7].wait()
    g1[...] = gs[0]
    put(g1, gain1_out)
    g2[...] = gs[1]
    put(g2, gain2_out)
    for c in sent:
        c.wait()


def finish_kernel(output, dx, gains, mixed, out_t, ff):
    rows, model = output.shape
    share, width = out_t.shape
    columns = ff.shape[2]
    gain, head, wide = ((model,), F32), ((share, width), F32), ((share, columns), F32)
    outs = [((rows, model), BF), ((rows, model), BF), gain, gain, head, head, head, head, wide, wide, wide]
    return pl.pallas_call(
        finish_body,
        in_specs=[ANY] * 6,
        out_specs=[ANY] * 11,
        out_shape=[jax.ShapeDtypeStruct(*o) for o in outs],
        scratch_shapes=[
            pltpu.VMEM((rows, model), BF), pltpu.VMEM((rows, model), BF), pltpu.VMEM((2, model), F32), pltpu.VMEM((model,), F32), pltpu.VMEM((model,), F32),
            pltpu.VMEM((share, 3 * width), F32), pltpu.VMEM((share, width), F32),
            pltpu.VMEM((3, share, columns), BF), pltpu.VMEM((share, columns), F32), pltpu.VMEM((share, columns), F32), pltpu.VMEM((share, columns), F32),
            DMA((8,)), DMA((11,)),
        ],
        compiler_params=pltpu.CompilerParams(vmem_limit_bytes=63 << 20),
        name="finish",
    )(output, dx, gains, mixed, out_t, ff)


def on_device(tokens, segments, granularity, norm1_gain, norm2_gain, w_query, w_key, w_value, w_out, w_gate, w_up, w_down, cotangent):
    length = segments.shape[1]
    cosine, sine = (jnp.asarray(t) for t in rope_numpy(length))
    dp = lax.axis_size("dp")
    a1_all, query_rot, key_rot, value_low, w_out_all, cot_own, probs_low, grad_rows, rows_two, hidden_own, attended_own = forward_kernel(
        dp, tokens, cotangent, segments, w_out, w_query, w_key, w_value, norm1_gain, norm2_gain, cosine, sine
    )
    grads_ff, down_parts, grad_hidden, gain_two = mlp_kernel(
        dp, rows_two, grad_rows, w_gate, w_up, w_down, hidden_own, cot_own, granularity, norm2_gain
    )
    output, grad_q, grad_k, grad_v, own_ff = attention_back_kernel(
        dp, grad_hidden, w_out_all, down_parts, grads_ff, query_rot, key_rot, value_low, probs_low, hidden_own, cosine, sine
    )
    grad_tokens, gains, own_qkv, own_out = input_back_kernel(
        dp, grad_q, grad_k, grad_v, a1_all, w_query, w_key, w_value, tokens, grad_hidden, attended_own, norm1_gain, gain_two
    )
    outs = finish_kernel(output, grad_tokens, gains, own_qkv, own_out, own_ff)
    return tuple(o.T if i in (7, 10) else o for i, o in enumerate(outs))


def solution(mesh):
    in_specs = (
        P(("dp", "tensor"), None), P("dp", None), P("dp"), P(), P(),
        P(None, "tensor"), P(None, "tensor"), P(None, "tensor"), P("tensor", None),
        P(None, "tensor"), P(None, "tensor"), P("tensor", None), P(("dp", "tensor"), None),
    )
    out_specs = (
        P(("dp", "tensor"), None), P(("dp", "tensor"), None), P(), P(),
        P("dp", "tensor"), P("dp", "tensor"), P("dp", "tensor"), P("tensor", "dp"),
        P("dp", "tensor"), P("dp", "tensor"), P("tensor", "dp"),
    )
    return jax.shard_map(on_device, mesh=mesh, in_specs=in_specs, out_specs=out_specs, check_vma=False)
```

```python
import functools

import jax
import jax.numpy as jnp
import numpy as np
from jax import lax
from jax.experimental import pallas as pl
from jax.experimental.pallas import tpu as pltpu
from jax.sharding import PartitionSpec as P

HD = 128
FF = 6144
EPS = 1e-06
NEG = -1e30
BF = jnp.bfloat16
F32 = jnp.float32
QB = 256


def norm_factor(values):
    return lax.rsqrt(jnp.mean(values * values, axis=-1, keepdims=True) + EPS)


def norm_back(values, factor, row_gain, gradient):
    scaled = gradient * row_gain
    inner_mean = jnp.mean(scaled * values, axis=-1, keepdims=True)
    back_rows = factor * scaled - values * (factor * factor * factor) * inner_mean
    return (back_rows, jnp.sum(gradient * values * factor, axis=0))


def dot(left, right, dims=((1,), (0,))):
    return lax.dot_general(left, right, (dims, ((), ())), preferred_element_type=F32)


MESH = pl.DeviceIdType.MESH
ANY = pl.BlockSpec(memory_space=pl.ANY)
VM = pl.BlockSpec(memory_space=pltpu.VMEM)
DMA = pltpu.SemaphoreType.DMA
RANKS = 4


def across(rank, k):
    if k == 3:
        return 3 - rank
    if k == 1:
        return rank + 1 - 2 * lax.rem(rank, 2)
    if k == 2:
        return rank + 2 - 4 * lax.div(rank, 2)
    return rank


def flip(index, bit):
    step = 2**bit
    return index + step - 2 * step * lax.rem(lax.div(index, step), 2)


def inner_plane(rank):
    return (rank == 1) | (rank == 2)


def greet(peers):
    barrier = pltpu.get_barrier_semaphore()
    for peer in peers:
        pl.semaphore_signal(barrier, inc=1, device_id=peer, device_id_type=MESH)
    pl.semaphore_wait(barrier, len(peers))


def line_peers(rank):
    return [{"tensor": across(rank, k)} for k in (1, 2, 3)]


class LineGather:
    def __init__(self, rank, view, pieces, send_sems, recv_sems):
        self.rank, self.view, self.pieces = rank, view, pieces
        self.send_sems, self.recv_sems = send_sems, recv_sems
        self.inner = inner_plane(rank)

    @staticmethod
    def sems(pieces):
        return [DMA((4, pieces)), DMA((RANKS, pieces))]

    def copy(self, source, piece, k, slot):
        return pltpu.make_async_remote_copy(
            src_ref=self.view(source, piece), dst_ref=self.view(source, piece),
            send_sem=self.send_sems.at[slot, piece], recv_sem=self.recv_sems.at[source, piece],
            device_id={"tensor": across(self.rank, k)}, device_id_type=MESH,
        )

    def start(self, piece):
        self.copy(self.rank, piece, 2, 0).start()
        self.copy(self.rank, piece, 1, 1).start()
        pl.when(self.inner)(lambda: self.copy(self.rank, piece, 3, 2).start())

    def arrive(self, k, piece):
        source = across(self.rank, k)
        self.copy(source, piece, 1, 3).wait_recv()
        if k == 2:
            pl.when(self.inner)(lambda: self.copy(source, piece, 1, 3).start())

    def finish(self):
        for piece in range(self.pieces):
            self.copy(self.rank, piece, 2, 0).wait_send()
            self.copy(self.rank, piece, 1, 1).wait_send()

        @pl.when(self.inner)
        def _():
            for piece in range(self.pieces):
                self.copy(self.rank, piece, 3, 2).wait_send()
                self.copy(across(self.rank, 2), piece, 1, 3).wait_send()


def local(source, target, sem):
    return pltpu.make_async_copy(source, target, sem)


class LineScatter:
    def __init__(self, rank, parts, inbox, send_sems, recv_sems, pieces):
        self.rank, self.parts, self.inbox, self.pieces = rank, parts, inbox, pieces
        self.send_sems, self.recv_sems = send_sems, recv_sems
        self.inner = inner_plane(rank)
        self.end = (rank == 0) | (rank == 3)
        self.rows = parts.shape[1] // pieces

    @staticmethod
    def sems(pieces):
        return [DMA((4, pieces)), DMA((4, pieces))]

    def where(self, piece):
        return pl.ds(piece * self.rows, self.rows)

    def copy(self, part, slot, k, piece):
        return pltpu.make_async_remote_copy(
            src_ref=self.parts.at[part, self.where(piece)], dst_ref=self.inbox.at[slot, self.where(piece)],
            send_sem=self.send_sems.at[part, piece], recv_sem=self.recv_sems.at[slot, piece],
            device_id={"tensor": across(self.rank, k)}, device_id_type=MESH,
        )

    def send_far(self, pieces=None):
        for piece in pieces or range(self.pieces):
            pl.when(self.inner)(lambda: self.copy(3, 3, 3, piece).start())
            pl.when(self.end)(lambda: self.copy(3, 0, 1, piece).start())

    def send_two_end(self):
        @pl.when(self.end)
        def _():
            for piece in range(self.pieces):
                self.copy(2, 2, 2, piece).start()

    def send_two_inner(self, pieces=None):
        @pl.when(self.inner)
        def _():
            for piece in pieces or range(self.pieces):
                where = self.where(piece)
                self.copy(3, 0, 1, piece).wait_recv()
                self.parts[2, where] = (self.parts[2, where].astype(F32) + self.inbox[0, where].astype(F32)).astype(BF)
                self.copy(2, 2, 2, piece).start()

    def send_near(self, pieces=None):
        for piece in pieces or range(self.pieces):
            self.copy(1, 1, 1, piece).start()

    def total(self, target):
        for piece in range(self.pieces):
            where = self.where(piece)
            self.copy(1, 1, 1, piece).wait_recv()
            self.copy(2, 2, 2, piece).wait_recv()
            target[where] = (self.parts[0, where].astype(F32) + self.inbox[1, where].astype(F32)) + self.inbox[2, where].astype(F32)

        @pl.when(self.inner)
        def _():
            for piece in range(self.pieces):
                where = self.where(piece)
                self.copy(3, 3, 3, piece).wait_recv()
                target[where] += self.inbox[3, where].astype(F32)

    def finish(self):
        for piece in range(self.pieces):
            for part in (1, 2, 3):
                self.copy(part, part, part, piece).wait_send()


class GroupReduce:
    def __init__(self, group, dp, send, keep, first, boxes, split, sems):
        self.group, self.dp, self.send, self.keep, self.first, self.boxes = group, dp, send, keep, first, boxes
        self.bits = dp.bit_length() - 1
        self.mates = dp // 2
        columns = first.shape[3]
        self.cols = (pl.ds(0, split), pl.ds(split, columns - split))
        self.sems = sems

    @staticmethod
    def sem_shapes(dp, count):
        mates, bits = dp // 2, dp.bit_length() - 1
        shapes = [DMA((count, mates)), DMA((count, mates))]
        for t in range(1, bits):
            shapes += [DMA((2, count, mates >> t)), DMA((2, count, mates >> t))]
        return shapes

    @staticmethod
    def box_shapes(dp, count, share, columns, split):
        mates, bits = dp // 2, dp.bit_length() - 1
        shapes = [pltpu.VMEM((count, mates, share, columns), BF)]
        for t in range(1, bits):
            shapes += [pltpu.VMEM((count, mates >> t, share, split), BF), pltpu.VMEM((count, mates >> t, share, columns - split), BF)]
        return shapes

    def peers(self):
        return [{"dp": flip(self.group, b)} for b in range(self.bits)]

    def bit(self, b):
        return lax.rem(lax.div(self.group, 2**b), 2)

    def copy0(self, w, j):
        return pltpu.make_async_remote_copy(
            src_ref=self.send(w, 2 * j + 1 - self.bit(0)), dst_ref=self.first.at[w, j],
            send_sem=self.sems[0].at[w, j], recv_sem=self.sems[1].at[w, j],
            device_id={"dp": flip(self.group, 0)}, device_id_type=MESH)

    def place(self, t, half, j, mine):
        n = self.bits
        if half == 0:
            low = sum((self.bit(i) * 2 ** (i - 1) for i in range(1, t)), 0)
            bit = self.bit(t)
            return (2 * j + (bit if mine else 1 - bit)) * 2 ** (t - 1) + low
        high = sum((self.bit(n - i) * 2 ** (n - 1 - i) for i in range(1, t)), 0)
        bit = self.bit(n - t)
        return high + (bit if mine else 1 - bit) * 2 ** (n - 1 - t) + j

    def copy(self, t, half, w, j):
        return pltpu.make_async_remote_copy(
            src_ref=self.keep(w, self.place(t, half, j, False)).at[:, self.cols[half]], dst_ref=self.boxes[2 * (t - 1) + half].at[w, j],
            send_sem=self.sems[2 * t].at[half, w, j], recv_sem=self.sems[2 * t + 1].at[half, w, j],
            device_id={"dp": flip(self.group, t if half == 0 else self.bits - t)}, device_id_type=MESH)

    def start0(self, w):
        for j in range(self.mates):
            self.copy0(w, j).start()

    def start(self, t, w):
        for j in range(self.mates >> t):
            for half in range(2):
                self.copy(t, half, w, j).start()

    def add0(self, w):
        def body(j, carry):
            self.copy0(w, j).wait_recv()
            mine = self.keep(w, j)
            mine[...] = (mine[...].astype(F32) + self.first[w, j].astype(F32)).astype(BF)
            return carry

        lax.fori_loop(0, self.mates, body, 0)
        self.start(1, w)

    def add(self, t, w, target=None):
        for half in range(2):
            def body(j, carry):
                self.copy(t, half, w, j).wait_recv()
                mine = self.keep(w, self.place(t, half, j, True)).at[:, self.cols[half]]
                value = mine[...].astype(F32) + self.boxes[2 * (t - 1) + half][w, j].astype(F32)
                if target is None:
                    mine[...] = value.astype(BF)
                else:
                    target[:, self.cols[half]] = value.astype(target.dtype)
                return carry

            lax.fori_loop(0, self.mates >> t, body, 0)
        if target is None:
            self.start(t + 1, w)

    def finish(self, count):
        def body(w, carry):
            for j in range(self.mates):
                self.copy0(w, j).wait_send()
            for t in range(1, self.bits):
                for j in range(self.mates >> t):
                    for half in range(2):
                        self.copy(t, half, w, j).wait_send()
            return carry

        lax.fori_loop(0, count, body, 0)


def rope_numpy(length):
    half = HD // 2
    frequency = np.float32(10000.0) ** (-np.arange(half, dtype=np.float32) / np.float32(half))
    angles = np.arange(length, dtype=np.float32)[:, None] * frequency[None, :]
    cosine, sine = np.cos(angles), np.sin(angles)
    return (np.concatenate([cosine, cosine], 1), np.concatenate([-sine, sine], 1))


def column_of(row, target):
    target[...] = jnp.transpose(jnp.broadcast_to(row.astype(F32), (HD, row.shape[1])))


def forward_body(dp, tok, cot, seg, wo, wq, wk, wv, gain, gain2, cosine, sine,
                 a1_out, q_out, k_out, v_out, wo_out, cot_out, p_out, dy_out, a2_out, h_out, ob_out,
                 xs, a1s, qkv, ws, wos, dys, obs, ps, hs, segs,
                 x_ss, x_rs, z_ss, z_rs, d_ss, d_rs, c_ss, y_ss, y_rs, o_ss, o_rs, l_sem, k_sem, b_sem):
    rank, group = lax.axis_index("tensor"), lax.axis_index("dp")
    rows, model = tok.shape
    length, width = q_out.shape
    heads = width // HD
    scale = HD ** (-0.5)
    half_rows = rows // 2
    parts = wo.shape[0]
    mates = parts // 2
    member = lax.rem(group, parts)
    base = group - member
    parity = lax.rem(member, 2)
    pair = lax.div(member, 2)
    partner = flip(group, 0)

    def mate(step):
        return lax.rem(pair + step, mates) * 2 + parity

    first = [local(wo.at[member], wos.at[rank, member], l_sem.at[0]), local(tok, xs.at[rank], l_sem.at[1]), local(cot, dys.at[rank], l_sem.at[2])]
    weights = [local(w, ws.at[i], l_sem.at[3 + i]) for i, w in enumerate((wq, wk, wv))]
    for c in first + weights:
        c.start()
    column_of(seg[...], segs)
    greet(line_peers(rank) + [{"dp": partner}] + [{"dp": base + mate(s)} for s in range(1, mates)])
    out_gather = LineGather(rank, lambda s, p: wos.at[s, member], 1, z_ss, z_rs)
    gather = LineGather(rank, lambda s, p: xs.at[s, pl.ds(p * half_rows, half_rows)], 2, x_ss, x_rs)

    def near(k, source):
        return pltpu.make_async_remote_copy(
            src_ref=dys.at[source], dst_ref=dys.at[source], send_sem=y_ss.at[k], recv_sem=y_rs.at[k],
            device_id={"tensor": across(rank, k)}, device_id_type=MESH)

    inner = inner_plane(rank)
    attended = LineGather(rank, lambda s, p: obs.at[s, :, pl.ds(pl.multiple_of(p * HD, HD), HD)], heads, o_ss, o_rs)
    first[0].wait()
    out_gather.start(0)
    first[1].wait()
    gather.start(0)
    gather.start(1)
    first[2].wait()
    real = segs[pl.ds(pl.multiple_of(rank * rows, rows), rows), :1] >= 0.0
    dys[rank] = jnp.where(real, dys[rank], jnp.zeros((rows, model), BF))
    near(1, rank).start()
    pl.when(inner)(near(3, rank).start)
    keep = [local(dys.at[rank], cot_out, k_sem.at[0])]
    keep[0].start()
    for w in weights:
        w.wait()

    def chunk(source):
        x = xs[source].astype(F32)
        a1s[source] = (x * norm_factor(x) * gain[...].reshape(1, model)).astype(BF)
        where = pl.ds(pl.multiple_of(source * rows, rows), rows)
        for i in range(3):
            product = dot(a1s[source], ws[i])
            for h in range(heads):
                head = product[:, h * HD : (h + 1) * HD]
                if i < 2:
                    head = head * cosine[where, :] + pltpu.roll(head, HD // 2, 1) * sine[where, :]
                qkv[i, where, h * HD : (h + 1) * HD] = head.astype(BF)

    def chunks(i, carry):
        @pl.when(i == 1)
        def _():
            for k in (1, 2, 3):
                out_gather.arrive(k, 0)
            for step in range(1, mates):
                mate_copy(step).start()
            core_copy(0, parity).start()
            for piece in range(2):
                gather.arrive(1, piece)
                gather.arrive(2, piece)

        @pl.when(i == 3)
        def _():
            for step in range(1, mates):
                mate_arrival(step).wait_recv()
                core_copy(step, parity).start()
            for piece in range(2):
                gather.arrive(3, piece)

        chunk(pick(i, [rank, across(rank, 1), across(rank, 2), across(rank, 3)]))
        return carry

    def mate_copy(step):
        return pltpu.make_async_remote_copy(
            src_ref=wos.at[:, member], dst_ref=wos.at[:, member], send_sem=d_ss.at[step], recv_sem=d_rs.at[member],
            device_id={"dp": base + mate(step)}, device_id_type=MESH)

    def mate_arrival(step):
        piece = mate(step)
        return pltpu.make_async_remote_copy(
            src_ref=wos.at[:, piece], dst_ref=wos.at[:, piece], send_sem=d_ss.at[step], recv_sem=d_rs.at[piece],
            device_id={"dp": base + piece}, device_id_type=MESH)

    def core_copy(step, owner):
        piece = lax.rem(pair + step, mates) * 2 + owner
        return pltpu.make_async_remote_copy(
            src_ref=wos.at[:, piece], dst_ref=wos.at[:, piece], send_sem=c_ss.at[step], recv_sem=d_rs.at[piece],
            device_id={"dp": partner}, device_id_type=MESH)

    lax.fori_loop(0, RANKS, chunks, 0)
    keep += [local(a1s, a1_out, k_sem.at[1])] + [local(qkv.at[i], t, k_sem.at[2 + i]) for i, t in enumerate((q_out, k_out, v_out))]
    for c in keep[1:]:
        c.start()

    def head(h, carry):
        cols = pl.ds(pl.multiple_of(h * HD, HD), HD)
        for start in range(0, length, QB):
            extent = start + QB
            scores = dot(qkv[0, start:extent, cols], qkv[1, :extent, cols], ((1,), (1,)))
            row_ids = lax.broadcasted_iota(jnp.int32, (QB, extent), 0) + start
            col_ids = lax.broadcasted_iota(jnp.int32, (QB, extent), 1)
            allowed = (col_ids <= row_ids) & (segs[start:extent, :1] == seg[:, :extent].astype(F32))
            logits = jnp.where(allowed, scores * scale, NEG)
            expo = jnp.exp(logits - jnp.max(logits, axis=-1, keepdims=True))
            probs = (expo * (1.0 / jnp.sum(expo, axis=-1, keepdims=True))).astype(BF)
            ps[h, start:extent, :extent] = probs
            obs[rank, start:extent, cols] = dot(probs, qkv[2, :extent, cols]).astype(BF)
        attended.start(h)
        return carry

    lax.fori_loop(0, heads, head, 0)
    for step in range(mates):
        core_copy(step, 1 - parity).wait_recv()
    more = [local(ps, p_out, k_sem.at[5]), local(wos, wo_out, k_sem.at[6])]
    for c in more:
        c.start()
    keep += more

    def add(source, first=False, last=False):
        def block(b, carry):
            weight = wos[source].reshape(width, model)
            part = dot(obs[source, pl.ds(pl.multiple_of(b * rows, rows), rows), :], weight)
            total = part + (xs[b].astype(F32) if first else hs[b])
            hs[b] = total
            if last:
                xs[b] = (total * norm_factor(total) * gain2[...].reshape(1, model)).astype(BF)
                local(xs.at[b], a2_out.at[b], b_sem.at[b]).start()
            return carry

        lax.fori_loop(0, RANKS, block, 0)

    add(rank, first=True)
    for piece in range(heads):
        attended.arrive(2, piece)
    for piece in range(heads):
        attended.arrive(1, piece)
    add(across(rank, 2))
    add(across(rank, 1))
    one, three = across(rank, 1), across(rank, 3)
    near(1, one).wait_recv()
    more = [local(dys.at[one], dy_out.at[one], l_sem.at[0])]
    more[0].start()
    inner_copy = local(dys.at[three], dy_out.at[three], l_sem.at[1])

    @pl.when(inner)
    def _():
        near(3, three).wait_recv()
        inner_copy.start()

    for piece in range(heads):
        attended.arrive(3, piece)
    gather.finish()
    add(across(rank, 3), last=True)
    more += [local(hs.at[rank], h_out, l_sem.at[2]),
             local(obs.at[:, pl.ds(pl.multiple_of(rank * rows, rows), rows)], ob_out, l_sem.at[3])]
    for c in more[1:]:
        c.start()
    out_gather.finish()
    for step in range(1, mates):
        mate_copy(step).wait_send()
    for step in range(mates):
        core_copy(step, parity).wait_send()
    attended.finish()
    near(1, rank).wait_send()

    @pl.when(inner)
    def _():
        near(3, rank).wait_send()
        inner_copy.wait()

    for c in keep + more:
        c.wait()
    for b in range(RANKS):
        local(xs.at[b], a2_out.at[b], b_sem.at[b]).wait()


def forward_kernel(dp, tokens, cotangent, segments, w_out, w_query, w_key, w_value, gain, gain2, cosine, sine):
    rows, model = tokens.shape
    width = w_query.shape[1]
    heads = width // HD
    length = RANKS * rows
    parts = min(dp, 8)
    mates = parts // 2
    shape = (RANKS, rows, model)
    shard, wide = jax.ShapeDtypeStruct(shape, BF), jax.ShapeDtypeStruct((length, width), BF)
    outs = pl.pallas_call(
        functools.partial(forward_body, dp),
        in_specs=[ANY, ANY, VM, ANY, ANY, ANY, ANY, VM, VM, VM, VM],
        out_specs=[ANY] * 11,
        out_shape=[shard, wide, wide, wide, jax.ShapeDtypeStruct((RANKS, parts, width // parts, model), BF),
                   jax.ShapeDtypeStruct((rows, model), BF), jax.ShapeDtypeStruct((heads, length, length), BF), shard, shard,
                   jax.ShapeDtypeStruct((rows, model), F32), jax.ShapeDtypeStruct((RANKS, rows, width), BF)],
        scratch_shapes=[
            pltpu.VMEM(shape, BF), pltpu.VMEM(shape, BF), pltpu.VMEM((3, length, width), BF), pltpu.VMEM((3, model, width), BF),
            pltpu.VMEM((RANKS, parts, width // parts, model), BF), pltpu.VMEM(shape, BF), pltpu.VMEM((RANKS, length, width), BF),
            pltpu.VMEM((heads, length, length), BF), pltpu.VMEM(shape, F32), pltpu.VMEM((length, HD), F32),
            *LineGather.sems(2), *LineGather.sems(1), DMA((mates,)), DMA((parts,)), DMA((mates,)),
            DMA((4,)), DMA((4,)), *LineGather.sems(heads), DMA((6,)), DMA((7,)), DMA((RANKS,)),
        ],
        compiler_params=pltpu.CompilerParams(collective_id=1, has_side_effects=True, vmem_limit_bytes=62 << 20),
        name="forward_gather",
    )(tokens, cotangent, segments, w_out.reshape(parts, width // parts, model), w_query, w_key, w_value, gain, gain2, cosine, sine)
    a1_all, query, key, value, w_out_all, cot_own, probs, dy, a2, hidden, attended = outs
    return a1_all, query, key, value, w_out_all.reshape(RANKS, width, model), cot_own, probs, dy, a2, hidden, attended


def pick(step, choices):
    value = choices[-1]
    for i in range(len(choices) - 1):
        value = jnp.where(step == i, choices[i], value)
    return value


FT = 768
WB = 384


def mlp_body(a2, dy, wg, wu, wd, hid, cot, gran, gain,
             g_out, down_out, dh_out, gain_out,
             lefts, acts, ws, parts, inbox, stage, downs, hs, cots, total, gains, r_ss, r_rs, y_ss, y_rs, l_sem, s_sem):
    rank = lax.axis_index("tensor")
    rows, model = cot.shape
    width = wg.shape[1]
    per, share = stage.shape[1], stage.shape[2]
    end = (rank == 0) | (rank == 3)

    def part(source):
        return pl.ds(pl.multiple_of(source * rows, rows), rows)

    def dy_load(k, sem):
        return local(dy.at[across(rank, k)], lefts.at[1, part(across(rank, k))], l_sem.at[sem])

    inner = inner_plane(rank)
    half = rows // 2

    def piece_of(source, piece):
        return pl.ds(pl.multiple_of(source * rows + piece * half, half), half)

    def hand(slot, shard, piece, k, kept=True):
        where = piece_of(across(rank, shard), piece)
        source = dy.at[across(rank, shard), pl.ds(piece * half, half)] if kept else lefts.at[1, where]
        return pltpu.make_async_remote_copy(
            src_ref=source, dst_ref=lefts.at[1, where], send_sem=y_ss.at[slot, piece], recv_sem=y_rs.at[slot, piece],
            device_id={"tensor": across(rank, k)}, device_id_type=MESH)

    def mid(piece):
        return hand(0, 1, piece, 3)

    def second(piece):
        return hand(1, 3, piece, 1)

    def third(piece):
        return hand(2, 2, piece, 1, False)

    def arrived(slot, shard, piece):
        where = piece_of(across(rank, shard), piece)
        return pltpu.make_async_remote_copy(
            src_ref=lefts.at[1, where], dst_ref=lefts.at[1, where], send_sem=y_ss.at[slot, piece], recv_sem=y_rs.at[slot, piece],
            device_id={"tensor": across(rank, 1)}, device_id_type=MESH)

    own = local(cot, lefts.at[1, part(rank)], l_sem.at[7])
    own.start()
    loads = [local(wg, ws.at[0], l_sem.at[0]), local(a2, lefts.at[0], l_sem.at[1]), local(wu, ws.at[1], l_sem.at[2]),
             dy_load(1, 3), local(wd, ws.at[2], l_sem.at[4])]
    inner_load = dy_load(3, 8)
    pl.when(inner)(inner_load.start)
    late = [local(hid, hs, l_sem.at[5]), local(cot, cots, l_sem.at[6])]
    for c in loads + late:
        c.start()
    greet(line_peers(rank))

    @pl.when(inner)
    def _():
        mid(0).start()
        second(0).start()
        mid(1).start()
        second(1).start()

    scatter = LineScatter(rank, parts, inbox, r_ss, r_rs, 4)
    planes = [rank] + [across(rank, k) for k in (1, 2, 3)]
    kinds = [jnp.where(end, a, b) for a, b in zip((1, 2, 0, 3), (3, 1, 2, 0))]
    order = [jnp.where(end, planes[a], planes[b]) for a, b in zip((1, 2, 0, 3), (3, 1, 2, 0))]
    limit = FF // 8 * lax.shift_left(1, gran[0] - 1) - rank * width

    def step(i, carry):
        where = pl.ds(pl.multiple_of(pick(i, order) * rows, rows), rows)

        def tile(t, inner_carry):
            cols = pl.ds(pl.multiple_of(t * FT, FT), FT)

            @pl.when((i == 0) & (t == 0))
            def _():
                loads[0].wait()
                loads[1].wait()

            gate = dot(lefts[0, where, :], ws[0, :, cols])

            @pl.when((i == 0) & (t == 0))
            def _():
                loads[2].wait()

            up = dot(lefts[0, where, :], ws[1, :, cols])

            @pl.when((i == 0) & (t == 0))
            def _():
                loads[3].wait()
                pl.when(inner)(inner_load.wait)
                own.wait()
                loads[4].wait()

            @pl.when((i == 1) & (t == 0) & end)
            def _():
                for piece in range(2):
                    arrived(1, 2, piece).wait_recv()

            @pl.when((i == 3) & (t == 0) & end)
            def _():
                for piece in range(2):
                    arrived(2, 3, piece).wait_recv()

            dz = dot(lefts[1, where, :], ws[2, cols, :], ((1,), (1,)))
            unit = lax.broadcasted_iota(jnp.int32, gate.shape, 1) + t * FT
            mask = unit < limit
            sigma = jax.nn.sigmoid(gate)
            active = jnp.where(mask, gate * sigma, 0.0)
            acts[2, where, cols] = (active * up).astype(BF)
            acts[0, where, cols] = jnp.where(mask, dz * up * sigma * (1.0 + gate * (1.0 - sigma)), 0.0).astype(BF)
            acts[1, where, cols] = (dz * active).astype(BF)
            return inner_carry

        lax.fori_loop(0, width // FT, tile, 0)

        def back(t, inner_carry):
            cols = pl.ds(pl.multiple_of(t * FT, FT), FT)
            parts[pick(i, kinds), :, cols] = (
                dot(acts[0, where, :], ws[0, cols, :], ((1,), (1,))) + dot(acts[1, where, :], ws[1, cols, :], ((1,), (1,)))
            ).astype(BF)
            return inner_carry

        lax.fori_loop(0, model // FT, back, 0)

        @pl.when(inner & (i == 0))
        def _():
            scatter.send_far()
            arrived(0, 2, 0).wait_recv()
            third(0).start()

        @pl.when(inner & (i == 1))
        def _():
            arrived(0, 2, 1).wait_recv()
            third(1).start()
            scatter.send_near()

        pl.when(end & (i == 0))(scatter.send_near)
        pl.when(end & (i == 1))(scatter.send_two_end)
        pl.when(end & (i == 3))(scatter.send_far)

        @pl.when((end & (i == 0)) | (inner & (i == 1)))
        def _():
            downs[1] = dot(acts[2, where, :], ws[2]).astype(BF)

        return carry

    lax.fori_loop(0, 4, step, 0)
    blocks = model // WB

    def put(i, slot):
        w, b = lax.div(i, blocks), lax.rem(i, blocks)
        return local(stage.at[slot], g_out.at[w, pl.ds(b * per, per)], s_sem.at[slot])

    def grads(i, carry):
        slot = lax.rem(i, 2)
        w, b = lax.div(i, blocks), lax.rem(i, blocks)
        left = lax.div(w, 2)
        cols = pl.ds(pl.multiple_of(b * WB, WB), WB)
        value = dot(lefts[left, :, cols], acts[w], ((0,), (0,)))
        pl.when(i >= 2)(lambda: put(i - 2, slot).wait())
        low = value.astype(BF)
        for p in range(per):
            stage[slot, p] = low[p * share : (p + 1) * share]
        put(i, slot).start()
        for piece in range(4):
            pl.when(i == 3 * blocks - 7 + 2 * piece)(lambda: scatter.send_two_inner([piece]))
        return carry

    lax.fori_loop(0, 3 * blocks, grads, 0)

    def down(i, carry):
        kind = jnp.where(i == 2, 0, i + 2)
        where = part(pick(i, [planes[2], planes[3], rank]))
        downs[kind] = dot(acts[2, where, :], ws[2]).astype(BF)
        return carry

    lax.fori_loop(0, 3, down, 0)
    keep = local(downs, down_out, l_sem.at[0])
    keep.start()
    for c in late:
        c.wait()
    scatter.total(total)
    values, gradient = hs[...], total[...]
    factor = norm_factor(values)
    back_rows, gain_rows = norm_back(values, factor, gain[...].reshape(1, model), gradient)
    total[...] = cots[...].astype(F32) + back_rows
    gains[...] = gain_rows.reshape(1, model)
    last = [local(total, dh_out, l_sem.at[1]), local(gains, gain_out, l_sem.at[2])]
    for c in last:
        c.start()
    scatter.finish()

    @pl.when(inner)
    def _():
        for piece in range(2):
            mid(piece).wait_send()
            second(piece).wait_send()
            third(piece).wait_send()

    put(3 * blocks - 2, 0).wait()
    put(3 * blocks - 1, 1).wait()
    for c in last + [keep]:
        c.wait()


def mlp_kernel(dp, a2, dy, w_gate, w_up, w_down, hidden_own, cot_own, granularity, gain):
    rows, model = cot_own.shape
    width = w_gate.shape[1]
    share = model // dp
    shard = (RANKS, rows, model)
    return pl.pallas_call(
        mlp_body,
        in_specs=[ANY] * 7 + [pl.BlockSpec(memory_space=pltpu.SMEM), VM],
        out_specs=[ANY] * 4,
        out_shape=[jax.ShapeDtypeStruct((3, dp, share, width), BF), jax.ShapeDtypeStruct(shard, BF),
                   jax.ShapeDtypeStruct((rows, model), F32), jax.ShapeDtypeStruct((1, model), F32)],
        scratch_shapes=[
            pltpu.VMEM((2, RANKS * rows, model), BF), pltpu.VMEM((3, RANKS * rows, width), BF), pltpu.VMEM((3, model, width), BF),
            pltpu.VMEM(shard, BF), pltpu.VMEM(shard, BF), pltpu.VMEM((2, WB // share, share, width), BF), pltpu.VMEM(shard, BF),
            pltpu.VMEM((rows, model), F32), pltpu.VMEM((rows, model), BF), pltpu.VMEM((rows, model), F32), pltpu.VMEM((1, model), F32),
            *LineScatter.sems(4), DMA((3, 2)), DMA((3, 2)), DMA((9,)), DMA((2,)),
        ],
        compiler_params=pltpu.CompilerParams(collective_id=3, has_side_effects=True, vmem_limit_bytes=63 << 20),
        name="mlp_scatter",
    )(a2.reshape(-1, model), dy, w_gate, w_up, w_down, hidden_own, cot_own, granularity, gain)


def attention_back_body(dp, dh, wo_all, downs, grads, q, k, v, p_all, hid, wq, wk, wv, cosine, sine,
                        out_out, dq_out, dk_out, dv_out, gf_out, da_out,
                        dhs, low, wos, parts, inbox, dobs, dos, qkv, ps, ds, dqkv, hs, outs, kept, finals, ws, shares, *rest):
    rank, group = lax.axis_index("tensor"), lax.axis_index("dp")
    rounds = 2 * (dp.bit_length() - 1)
    first, boxes, rest = rest[0], rest[1 : rounds - 1], rest[rounds - 1 :]
    sems, (r_ss, r_rs, a_ss, a_rs, l_sem, p_sem, f_sem) = rest[:rounds], rest[rounds:]
    rows, model = dh.shape
    length, width = q.shape
    heads, half, scale = width // HD, HD // 2, HD ** (-0.5)
    count = grads.shape[0]
    parity = lax.rem(group, 2)
    loads = [local(downs, parts, l_sem.at[2]), local(dh, dhs, l_sem.at[0]), local(wo_all, wos, l_sem.at[1])]
    owns = [local(grads.at[w, :, parity], kept.at[w], f_sem.at[w]) for w in range(count)]
    late = [local(t, qkv.at[i], l_sem.at[3 + i]) for i, t in enumerate((q, k, v))] + [local(hid, hs, l_sem.at[6])]
    late += [local(t, ws.at[i], l_sem.at[7 + i]) for i, t in enumerate((wq, wk, wv))]
    for c in loads + owns + late:
        c.start()

    def probs(h):
        return local(p_all.at[h], ps.at[lax.rem(h, 2)], p_sem.at[lax.rem(h, 2)])

    probs(0).start()
    probs(1).start()
    reduce = GroupReduce(
        group, dp, lambda w, d: grads.at[w, lax.div(d, 2), lax.rem(d, 2)], lambda w, j: kept.at[w, j], first, boxes, model // 2, sems)
    greet(line_peers(rank) + reduce.peers())
    for w in range(count):
        reduce.start0(w)
    scatter = LineScatter(rank, parts, inbox, r_ss, r_rs, 2)
    loads[0].wait()
    scatter.send_far([0])

    def exchange(k, source):
        where = pl.ds(pl.multiple_of(source * rows, rows), rows)
        return pltpu.make_async_remote_copy(
            src_ref=dobs.at[k - 1], dst_ref=dos.at[where], send_sem=a_ss.at[k], recv_sem=a_rs.at[source],
            device_id={"tensor": across(rank, k)}, device_id_type=MESH)

    loads[1].wait()
    low[...] = dhs[...].astype(BF)
    loads[2].wait()
    for k in (3, 2, 1):
        dobs[k - 1] = dot(low[...], wos[across(rank, k)], ((1,), (1,))).astype(BF)
        exchange(k, rank).start()
    scatter.send_far([1])
    scatter.send_two_end()
    scatter.send_near()
    dos[pl.ds(pl.multiple_of(rank * rows, rows), rows), :] = dot(low[...], wos[rank], ((1,), (1,))).astype(BF)
    for c in owns:
        c.wait()

    def fold(w, carry):
        reduce.add0(w)
        return carry

    lax.fori_loop(0, count, fold, 0)
    for c in late:
        c.wait()
    scatter.send_two_inner([0])
    for k in (3, 2, 1):
        exchange(k, across(rank, k)).wait_recv()

    def head(h, carry):
        cols = pl.ds(pl.multiple_of(h * HD, HD), HD)
        slot = lax.rem(h, 2)
        probs(h).wait()

        def unrope(grad, start):
            where = slice(start, start + QB)
            return (grad * cosine[where, :] - pltpu.roll(grad, half, 1) * sine[where, :]).astype(BF)

        for start in range(0, length, QB):
            extent = start + QB
            where = slice(start, extent)
            grad_p = dot(dos[where, cols], qkv[2, :extent, cols], ((1,), (1,)))
            p = ps[slot, where, :extent].astype(F32)
            weighted = p * grad_p
            delta = jnp.sum(weighted, axis=-1, keepdims=True)
            ds[where, :extent] = ((weighted - p * delta) * scale).astype(BF)
            dqkv[0, where, cols] = unrope(dot(ds[where, :extent], qkv[1, :extent, cols]), start)
        for start in range(0, length, QB):
            where = slice(start, start + QB)
            dqkv[1, where, cols] = unrope(dot(ds[start:, where], qkv[0, start:, cols], ((0,), (0,))), start)
            dqkv[2, where, cols] = dot(ps[slot, start:, where], dos[start:, cols], ((0,), (0,))).astype(BF)
        pl.when(h + 2 < heads)(lambda: probs(h + 2).start())
        pl.when(h == 0)(lambda: scatter.send_two_inner([1]))
        return carry

    lax.fori_loop(0, heads, head, 0)
    done = [local(dqkv.at[i], t, l_sem.at[i]) for i, t in enumerate((dq_out, dk_out, dv_out))]
    for c in done:
        c.start()

    def share_of(k, carry):
        where = pl.ds(pl.multiple_of(pick(k, [rank] + [across(rank, i) for i in (1, 2, 3)]) * rows, rows), rows)
        value = dot(dqkv[0, where, :], ws[0], ((1,), (1,)))
        for s in (1, 2):
            value += dot(dqkv[s, where, :], ws[s], ((1,), (1,)))
        shares[k] = value.astype(BF)
        return carry

    reduce.add(1, 0)
    lax.fori_loop(0, RANKS, share_of, 0)
    done.append(local(shares, da_out, l_sem.at[4]))
    done[-1].start()
    reduce.add(1, 1)
    reduce.add(1, 2)
    for t in range(2, reduce.bits - 1):
        for w in range(count):
            reduce.add(t, w)

    def put(w):
        return local(finals.at[w], gf_out.at[w], f_sem.at[w])

    for w in range(count):
        reduce.add(reduce.bits - 1, w, finals.at[w])
        put(w).start()
    scatter.total(dhs)
    outs[...] = (hs[...] + dhs[...]).astype(BF)
    last = local(outs, out_out, l_sem.at[3])
    last.start()
    scatter.finish()
    for k in (1, 2, 3):
        exchange(k, rank).wait_send()
    reduce.finish(count)
    for w in range(count):
        put(w).wait()
    for c in done + [last]:
        c.wait()


def attention_back_kernel(dp, grad_hidden, w_out_all, down_parts, grads_ff, query, key, value, probs_low, hidden_own, w_query, w_key, w_value, cosine, sine):
    rows, model = grad_hidden.shape
    length, width = query.shape
    count, _, share, columns = grads_ff.shape
    mates = dp // 2
    shard = (RANKS, rows, model)
    heads = jax.ShapeDtypeStruct((length, width), BF)
    return pl.pallas_call(
        functools.partial(attention_back_body, dp),
        in_specs=[ANY] * 12 + [VM, VM],
        out_specs=[ANY] * 6,
        out_shape=[jax.ShapeDtypeStruct((rows, model), BF), heads, heads, heads, jax.ShapeDtypeStruct((count, share, columns), BF),
                   jax.ShapeDtypeStruct(shard, BF)],
        scratch_shapes=[
            pltpu.VMEM((rows, model), F32), pltpu.VMEM((rows, model), BF), pltpu.VMEM((RANKS, width, model), BF),
            pltpu.VMEM(shard, BF), pltpu.VMEM(shard, BF), pltpu.VMEM((3, rows, width), BF), pltpu.VMEM((length, width), BF),
            pltpu.VMEM((3, length, width), BF), pltpu.VMEM((2, length, length), BF), pltpu.VMEM((length, length), BF),
            pltpu.VMEM((3, length, width), BF), pltpu.VMEM((rows, model), F32), pltpu.VMEM((rows, model), BF),
            pltpu.VMEM((count, mates, share, columns), BF), pltpu.VMEM((count, share, columns), BF),
            pltpu.VMEM((3, model, width), BF), pltpu.VMEM(shard, BF),
            *GroupReduce.box_shapes(dp, count, share, columns, columns // 2), *GroupReduce.sem_shapes(dp, count),
            *LineScatter.sems(2), DMA((4,)), DMA((RANKS,)), DMA((10,)), DMA((2,)), DMA((count,)),
        ],
        compiler_params=pltpu.CompilerParams(collective_id=4, has_side_effects=True, vmem_limit_bytes=63 << 20),
        name="attention_back",
    )(grad_hidden, w_out_all, down_parts, grads_ff.reshape(count, mates, 2, share, columns),
      query, key, value, probs_low, hidden_own, w_query, w_key, w_value, cosine, sine)


def input_back_body(dp, dq, dk, dv, a1, da, tok, dh, ob, gain, gain2,
                    dx_out, gains_out, gqkv_out, gout_out,
                    dqkv, a1s, xs, dhs, low, obs, parts, inbox, g1, g2, f1, f2, f2_low, box2, f3, gbuf, gbox, total, dxs, *rest):
    rank, group = lax.axis_index("tensor"), lax.axis_index("dp")
    bits = dp.bit_length() - 1
    boxes = [rest[: 2 * bits - 1], rest[2 * bits - 1 : 4 * bits - 2]]
    rest = rest[4 * bits - 2 :]
    sems = [rest[: 2 * bits], rest[2 * bits : 4 * bits]]
    r_ss, r_rs, z_ss, z_rs, g_ss, g_rs, l_sem = rest[4 * bits :]
    rows, model = tok.shape
    width = dq.shape[1]
    share = g1.shape[1]
    per = WB // share
    parity = lax.rem(group, 2)
    loads = [local(da, parts, l_sem.at[3])]
    late = [local(a1, a1s, l_sem.at[8]), local(dh, dhs, l_sem.at[6]), local(ob, obs, l_sem.at[7]), local(tok, xs, l_sem.at[9])]
    late += [local(t, dqkv.at[i], l_sem.at[i]) for i, t in enumerate((dq, dk, dv))]
    for c in loads + late:
        c.start()
    scatter = LineScatter(rank, parts, inbox, r_ss, r_rs, 2)
    mixed = GroupReduce(group, dp, lambda w, d: g1.at[d], lambda w, j: g1.at[2 * j + parity], boxes[0][0], boxes[0][1:], f1.shape[1] // 256 * 128, sems[0])
    output = GroupReduce(group, dp, lambda w, d: g2.at[d], lambda w, j: g2.at[2 * j + parity], boxes[1][0], boxes[1][1:], f2.shape[1] // 256 * 128, sems[1])
    greet(line_peers(rank) + mixed.peers())
    for c in loads:
        c.wait()
    scatter.send_far()
    scatter.send_two_end()
    scatter.send_near()
    late[0].wait()

    def gain_rows(k, carry):
        where = pl.ds(pl.multiple_of(pick(k, [rank] + [across(rank, i) for i in (1, 2, 3)]) * rows, rows), rows)
        row = jnp.sum(parts[k].astype(F32) * a1s[where, :].astype(F32), axis=0, keepdims=True)
        gbuf[0, 0:1, :] = jnp.where(k == 0, row, gbuf[0, 0:1, :] + row)
        return carry

    gbuf[0, 0:1, :] = jnp.zeros((1, model), F32)
    lax.fori_loop(0, RANKS, gain_rows, 0)
    gbuf[0, 0:1, :] = gbuf[0, 0:1, :] / gain[...].reshape(1, model)
    gbuf[0, 1:2, :] = gain2[...]

    def swap(t):
        return pltpu.make_async_remote_copy(
            src_ref=gbuf.at[t], dst_ref=gbox.at[t], send_sem=g_ss.at[t], recv_sem=g_rs.at[t], device_id={"dp": flip(group, t)}, device_id_type=MESH)

    def advance(t):
        swap(t).wait_recv()
        gbuf[t + 1] = gbuf[t] + gbox[t]
        if t + 1 < bits:
            swap(t + 1).start()

    def share_gains(k, source):
        return pltpu.make_async_remote_copy(
            src_ref=gbuf.at[bits], dst_ref=gbox.at[bits + source], send_sem=g_ss.at[bits + k], recv_sem=g_rs.at[bits + source],
            device_id={"tensor": across(rank, k)}, device_id_type=MESH)

    swap(0).start()
    for c in late[1:]:
        c.wait()
    low[...] = dhs[...].astype(BF)

    def out_block(b, carry):
        cols = pl.ds(pl.multiple_of(b * WB, WB), WB)
        for r in range(RANKS):
            value = dot(low[:, cols], obs[r], ((0,), (0,))).astype(BF)
            for p in range(per):
                g2[b * per + p, :, r * width : (r + 1) * width] = value[p * share : (p + 1) * share]
        return carry

    lax.fori_loop(0, model // WB, out_block, 0)
    advance(0)
    output.start0(0)

    def mixed_block(b, carry):
        cols = pl.ds(pl.multiple_of(b * WB, WB), WB)
        for s in range(3):
            value = dot(a1s[:, cols], dqkv[s], ((0,), (0,))).astype(BF)
            for p in range(per):
                g1[b * per + p, :, s * width : (s + 1) * width] = value[p * share : (p + 1) * share]
        return carry

    lax.fori_loop(0, model // WB, mixed_block, 0)
    for t in range(1, bits):
        advance(t)
    for k in (1, 2, 3):
        share_gains(k, rank).start()
    gbox[bits + rank] = gbuf[bits]
    mixed.start0(0)
    output.add0(0)
    mixed.add0(0)
    scatter.send_two_inner()
    for t in range(1, bits - 1):
        output.add(t, 0)
        mixed.add(t, 0)
    output.add(bits - 1, 0, f2)
    ends = LineScatter(rank, f2_low, box2, z_ss, z_rs, 1)
    for k in range(4):
        column = pl.ds(pl.multiple_of(across(rank, k) * width, HD), width)
        f2_low[k] = f2[:, column].astype(BF)
    ends.send_far()
    ends.send_two_end()
    ends.send_near()
    mixed.add(bits - 1, 0, f1)
    done = [local(f1, gqkv_out, l_sem.at[0])]
    done[0].start()
    scatter.total(total)
    values, gradient = xs[...].astype(F32), total[...]
    back_rows, _ = norm_back(values, norm_factor(values), gain[...].reshape(1, model), gradient)
    dxs[...] = (dhs[...] + back_rows).astype(BF)
    done.append(local(dxs, dx_out, l_sem.at[1]))
    done[1].start()
    for k in (1, 2, 3):
        share_gains(k, across(rank, k)).wait_recv()
    for t in range(bits):
        swap(t).wait_send()
    gbuf[0] = ((gbox[bits] + gbox[bits + 1]) + gbox[bits + 2]) + gbox[bits + 3]
    done.append(local(gbuf.at[0], gains_out, l_sem.at[2]))
    done[2].start()
    ends.send_two_inner()
    ends.total(f3)
    done.append(local(f3, gout_out, l_sem.at[3]))
    done[3].start()
    scatter.finish()
    ends.finish()
    mixed.finish(1)
    output.finish(1)
    for k in (1, 2, 3):
        share_gains(k, rank).wait_send()
    for c in done:
        c.wait()


def input_back_kernel(dp, grad_q, grad_k, grad_v, a1_all, grad_one, tokens, grad_hidden, attended_own, gain, gain_two):
    rows, model = tokens.shape
    length, width = grad_q.shape
    share = model // dp
    bits = dp.bit_length() - 1
    shard = (RANKS, rows, model)
    wide = (3 * width, RANKS * width)
    splits = [w // 256 * 128 for w in wide]
    return pl.pallas_call(
        functools.partial(input_back_body, dp),
        in_specs=[ANY] * 8 + [VM, VM],
        out_specs=[ANY] * 4,
        out_shape=[jax.ShapeDtypeStruct((rows, model), BF), jax.ShapeDtypeStruct((2, model), F32),
                   jax.ShapeDtypeStruct((share, wide[0]), F32), jax.ShapeDtypeStruct((share, width), F32)],
        scratch_shapes=[
            pltpu.VMEM((3, length, width), BF), pltpu.VMEM((length, model), BF),
            pltpu.VMEM((rows, model), BF), pltpu.VMEM((rows, model), F32), pltpu.VMEM((rows, model), BF), pltpu.VMEM((RANKS, rows, width), BF),
            pltpu.VMEM(shard, BF), pltpu.VMEM(shard, BF),
            pltpu.VMEM((dp, share, wide[0]), BF), pltpu.VMEM((dp, share, wide[1]), BF),
            pltpu.VMEM((share, wide[0]), F32), pltpu.VMEM((share, wide[1]), F32),
            pltpu.VMEM((RANKS, share, width), BF), pltpu.VMEM((RANKS, share, width), BF), pltpu.VMEM((share, width), F32),
            pltpu.VMEM((bits + 1, 2, model), F32), pltpu.VMEM((bits + RANKS, 2, model), F32),
            pltpu.VMEM((rows, model), F32), pltpu.VMEM((rows, model), BF),
            *GroupReduce.box_shapes(dp, 1, share, wide[0], splits[0]), *GroupReduce.box_shapes(dp, 1, share, wide[1], splits[1]),
            *GroupReduce.sem_shapes(dp, 1), *GroupReduce.sem_shapes(dp, 1),
            *LineScatter.sems(2), *LineScatter.sems(1), DMA((bits + RANKS,)), DMA((bits + RANKS,)), DMA((10,)),
        ],
        compiler_params=pltpu.CompilerParams(collective_id=5, has_side_effects=True, vmem_limit_bytes=63 << 20),
        name="input_back",
    )(grad_q, grad_k, grad_v, a1_all.reshape(length, model), grad_one, tokens, grad_hidden, attended_own, gain, gain_two)


def finish_body(output, dx, gains, mixed, out_t, ff,
                output_out, dx_out, gain1_out, gain2_out, q_out, k_out, v_out, wo_out, gate_out, up_out, down_out,
                b0, b1, gs, g1, g2, ms, ot, fs, gate, up, down, i_sem, o_sem):
    width = q_out.shape[1]
    loads = [local(s, t, i_sem.at[i]) for i, (s, t) in enumerate(
        ((ff.at[2], fs.at[2]), (ff.at[0], fs.at[0]), (ff.at[1], fs.at[1]), (mixed, ms), (output, b0), (dx, b1), (out_t, ot), (gains, gs)))]
    for c in loads:
        c.start()
    sent = []

    def put(source, target):
        sent.append(local(source, target, o_sem.at[len(sent)]))
        sent[-1].start()

    loads[1].wait()
    gate[...] = fs[0].astype(F32)
    put(gate, gate_out)
    loads[2].wait()
    up[...] = fs[1].astype(F32)
    put(up, up_out)
    loads[4].wait()
    put(b0, output_out)
    loads[5].wait()
    put(b1, dx_out)
    loads[3].wait()
    for i, target in enumerate((q_out, k_out, v_out)):
        put(ms.at[:, pl.ds(i * width, width)], target)
    loads[0].wait()
    down[...] = fs[2].astype(F32)
    put(down, down_out)
    loads[6].wait()
    put(ot, wo_out)
    loads[7].wait()
    g1[...] = gs[0]
    put(g1, gain1_out)
    g2[...] = gs[1]
    put(g2, gain2_out)
    for c in sent:
        c.wait()


def finish_kernel(output, dx, gains, mixed, out_t, ff):
    rows, model = output.shape
    share, width = out_t.shape
    columns = ff.shape[2]
    gain, head, wide = ((model,), F32), ((share, width), F32), ((share, columns), F32)
    outs = [((rows, model), BF), ((rows, model), BF), gain, gain, head, head, head, head, wide, wide, wide]
    return pl.pallas_call(
        finish_body,
        in_specs=[ANY] * 6,
        out_specs=[ANY] * 11,
        out_shape=[jax.ShapeDtypeStruct(*o) for o in outs],
        scratch_shapes=[
            pltpu.VMEM((rows, model), BF), pltpu.VMEM((rows, model), BF), pltpu.VMEM((2, model), F32), pltpu.VMEM((model,), F32), pltpu.VMEM((model,), F32),
            pltpu.VMEM((share, 3 * width), F32), pltpu.VMEM((share, width), F32),
            pltpu.VMEM((3, share, columns), BF), pltpu.VMEM((share, columns), F32), pltpu.VMEM((share, columns), F32), pltpu.VMEM((share, columns), F32),
            DMA((8,)), DMA((11,)),
        ],
        compiler_params=pltpu.CompilerParams(vmem_limit_bytes=63 << 20),
        name="finish",
    )(output, dx, gains, mixed, out_t, ff)


def on_device(tokens, segments, granularity, norm1_gain, norm2_gain, w_query, w_key, w_value, w_out, w_gate, w_up, w_down, cotangent):
    length = segments.shape[1]
    cosine, sine = (jnp.asarray(t) for t in rope_numpy(length))
    dp = lax.axis_size("dp")
    a1_all, query_rot, key_rot, value_low, w_out_all, cot_own, probs_low, grad_rows, rows_two, hidden_own, attended_own = forward_kernel(
        dp, tokens, cotangent, segments, w_out, w_query, w_key, w_value, norm1_gain, norm2_gain, cosine, sine
    )
    grads_ff, down_parts, grad_hidden, gain_two = mlp_kernel(
        dp, rows_two, grad_rows, w_gate, w_up, w_down, hidden_own, cot_own, granularity, norm2_gain
    )
    output, grad_q, grad_k, grad_v, own_ff, grad_one = attention_back_kernel(
        dp, grad_hidden, w_out_all, down_parts, grads_ff, query_rot, key_rot, value_low, probs_low, hidden_own, w_query, w_key, w_value, cosine, sine
    )
    grad_tokens, gains, own_qkv, own_out = input_back_kernel(
        dp, grad_q, grad_k, grad_v, a1_all, grad_one, tokens, grad_hidden, attended_own, norm1_gain, gain_two
    )
    outs = finish_kernel(output, grad_tokens, gains, own_qkv, own_out, own_ff)
    return tuple(o.T if i in (7, 10) else o for i, o in enumerate(outs))


def solution(mesh):
    in_specs = (
        P(("dp", "tensor"), None), P("dp", None), P("dp"), P(), P(),
        P(None, "tensor"), P(None, "tensor"), P(None, "tensor"), P("tensor", None),
        P(None, "tensor"), P(None, "tensor"), P("tensor", None), P(("dp", "tensor"), None),
    )
    out_specs = (
        P(("dp", "tensor"), None), P(("dp", "tensor"), None), P(), P(),
        P("dp", "tensor"), P("dp", "tensor"), P("dp", "tensor"), P("tensor", "dp"),
        P("dp", "tensor"), P("dp", "tensor"), P("tensor", "dp"),
    )
    return jax.shard_map(on_device, mesh=mesh, in_specs=in_specs, out_specs=out_specs, check_vma=False)
```

```python
import functools

import jax
import jax.numpy as jnp
import numpy as np
from jax import lax
from jax.experimental import pallas as pl
from jax.experimental.pallas import tpu as pltpu
from jax.sharding import PartitionSpec as P

HD = 128
FF = 6144
EPS = 1e-06
NEG = -1e30
BF = jnp.bfloat16
F32 = jnp.float32
QB = 256


def norm_factor(values):
    return lax.rsqrt(jnp.mean(values * values, axis=-1, keepdims=True) + EPS)


def norm_back(values, factor, row_gain, gradient):
    scaled = gradient * row_gain
    inner_mean = jnp.mean(scaled * values, axis=-1, keepdims=True)
    back_rows = factor * scaled - values * (factor * factor * factor) * inner_mean
    return (back_rows, jnp.sum(gradient * values * factor, axis=0))


def dot(left, right, dims=((1,), (0,))):
    return lax.dot_general(left, right, (dims, ((), ())), preferred_element_type=F32)


MESH = pl.DeviceIdType.MESH
ANY = pl.BlockSpec(memory_space=pl.ANY)
VM = pl.BlockSpec(memory_space=pltpu.VMEM)
DMA = pltpu.SemaphoreType.DMA
RANKS = 4


def across(rank, k):
    if k == 3:
        return 3 - rank
    if k == 1:
        return rank + 1 - 2 * lax.rem(rank, 2)
    if k == 2:
        return rank + 2 - 4 * lax.div(rank, 2)
    return rank


def flip(index, bit):
    step = 2**bit
    return index + step - 2 * step * lax.rem(lax.div(index, step), 2)


def inner_plane(rank):
    return (rank == 1) | (rank == 2)


def greet(peers):
    barrier = pltpu.get_barrier_semaphore()
    for peer in peers:
        pl.semaphore_signal(barrier, inc=1, device_id=peer, device_id_type=MESH)
    pl.semaphore_wait(barrier, len(peers))


def line_peers(rank):
    return [{"tensor": across(rank, k)} for k in (1, 2, 3)]


class LineGather:
    def __init__(self, rank, view, pieces, send_sems, recv_sems):
        self.rank, self.view, self.pieces = rank, view, pieces
        self.send_sems, self.recv_sems = send_sems, recv_sems
        self.inner = inner_plane(rank)

    @staticmethod
    def sems(pieces):
        return [DMA((4, pieces)), DMA((RANKS, pieces))]

    def copy(self, source, piece, k, slot):
        return pltpu.make_async_remote_copy(
            src_ref=self.view(source, piece), dst_ref=self.view(source, piece),
            send_sem=self.send_sems.at[slot, piece], recv_sem=self.recv_sems.at[source, piece],
            device_id={"tensor": across(self.rank, k)}, device_id_type=MESH,
        )

    def start(self, piece):
        self.copy(self.rank, piece, 2, 0).start()
        self.copy(self.rank, piece, 1, 1).start()
        pl.when(self.inner)(lambda: self.copy(self.rank, piece, 3, 2).start())

    def arrive(self, k, piece):
        source = across(self.rank, k)
        self.copy(source, piece, 1, 3).wait_recv()
        if k == 2:
            pl.when(self.inner)(lambda: self.copy(source, piece, 1, 3).start())

    def finish(self):
        for piece in range(self.pieces):
            self.copy(self.rank, piece, 2, 0).wait_send()
            self.copy(self.rank, piece, 1, 1).wait_send()

        @pl.when(self.inner)
        def _():
            for piece in range(self.pieces):
                self.copy(self.rank, piece, 3, 2).wait_send()
                self.copy(across(self.rank, 2), piece, 1, 3).wait_send()


def local(source, target, sem):
    return pltpu.make_async_copy(source, target, sem)


class LineScatter:
    def __init__(self, rank, parts, inbox, send_sems, recv_sems, pieces):
        self.rank, self.parts, self.inbox, self.pieces = rank, parts, inbox, pieces
        self.send_sems, self.recv_sems = send_sems, recv_sems
        self.inner = inner_plane(rank)
        self.end = (rank == 0) | (rank == 3)
        self.rows = parts.shape[1] // pieces

    @staticmethod
    def sems(pieces):
        return [DMA((4, pieces)), DMA((4, pieces))]

    def where(self, piece):
        return pl.ds(piece * self.rows, self.rows)

    def copy(self, part, slot, k, piece):
        return pltpu.make_async_remote_copy(
            src_ref=self.parts.at[part, self.where(piece)], dst_ref=self.inbox.at[slot, self.where(piece)],
            send_sem=self.send_sems.at[part, piece], recv_sem=self.recv_sems.at[slot, piece],
            device_id={"tensor": across(self.rank, k)}, device_id_type=MESH,
        )

    def send_far(self, pieces=None):
        for piece in pieces or range(self.pieces):
            pl.when(self.inner)(lambda: self.copy(3, 3, 3, piece).start())
            pl.when(self.end)(lambda: self.copy(3, 0, 1, piece).start())

    def send_two_end(self):
        @pl.when(self.end)
        def _():
            for piece in range(self.pieces):
                self.copy(2, 2, 2, piece).start()

    def send_two_inner(self, pieces=None):
        @pl.when(self.inner)
        def _():
            for piece in pieces or range(self.pieces):
                where = self.where(piece)
                self.copy(3, 0, 1, piece).wait_recv()
                self.parts[2, where] = (self.parts[2, where].astype(F32) + self.inbox[0, where].astype(F32)).astype(BF)
                self.copy(2, 2, 2, piece).start()

    def send_near(self, pieces=None):
        for piece in pieces or range(self.pieces):
            self.copy(1, 1, 1, piece).start()

    def total(self, target, then=None):
        for piece in range(self.pieces):
            where = self.where(piece)
            self.copy(1, 1, 1, piece).wait_recv()
            self.copy(2, 2, 2, piece).wait_recv()
            target[where] = (self.parts[0, where].astype(F32) + self.inbox[1, where].astype(F32)) + self.inbox[2, where].astype(F32)

            @pl.when(self.inner)
            def _():
                self.copy(3, 3, 3, piece).wait_recv()
                target[where] += self.inbox[3, where].astype(F32)

            if then is not None:
                then(piece, where)

    def finish(self):
        for piece in range(self.pieces):
            for part in (1, 2, 3):
                self.copy(part, part, part, piece).wait_send()


class GroupReduce:
    def __init__(self, group, dp, send, keep, first, boxes, split, sems):
        self.group, self.dp, self.send, self.keep, self.first, self.boxes = group, dp, send, keep, first, boxes
        self.bits = dp.bit_length() - 1
        self.mates = dp // 2
        columns = first.shape[3]
        self.cols = (pl.ds(0, split), pl.ds(split, columns - split))
        self.sems = sems

    @staticmethod
    def sem_shapes(dp, count):
        mates, bits = dp // 2, dp.bit_length() - 1
        shapes = [DMA((count, mates)), DMA((count, mates))]
        for t in range(1, bits):
            shapes += [DMA((2, count, mates >> t)), DMA((2, count, mates >> t))]
        return shapes

    @staticmethod
    def box_shapes(dp, count, share, columns, split):
        mates, bits = dp // 2, dp.bit_length() - 1
        shapes = [pltpu.VMEM((count, mates, share, columns), BF)]
        for t in range(1, bits):
            shapes += [pltpu.VMEM((count, mates >> t, share, split), BF), pltpu.VMEM((count, mates >> t, share, columns - split), BF)]
        return shapes

    def peers(self):
        return [{"dp": flip(self.group, b)} for b in range(self.bits)]

    def bit(self, b):
        return lax.rem(lax.div(self.group, 2**b), 2)

    def copy0(self, w, j):
        return pltpu.make_async_remote_copy(
            src_ref=self.send(w, 2 * j + 1 - self.bit(0)), dst_ref=self.first.at[w, j],
            send_sem=self.sems[0].at[w, j], recv_sem=self.sems[1].at[w, j],
            device_id={"dp": flip(self.group, 0)}, device_id_type=MESH)

    def place(self, t, half, j, mine):
        n = self.bits
        if half == 0:
            low = sum((self.bit(i) * 2 ** (i - 1) for i in range(1, t)), 0)
            bit = self.bit(t)
            return (2 * j + (bit if mine else 1 - bit)) * 2 ** (t - 1) + low
        high = sum((self.bit(n - i) * 2 ** (n - 1 - i) for i in range(1, t)), 0)
        bit = self.bit(n - t)
        return high + (bit if mine else 1 - bit) * 2 ** (n - 1 - t) + j

    def copy(self, t, half, w, j):
        return pltpu.make_async_remote_copy(
            src_ref=self.keep(w, self.place(t, half, j, False)).at[:, self.cols[half]], dst_ref=self.boxes[2 * (t - 1) + half].at[w, j],
            send_sem=self.sems[2 * t].at[half, w, j], recv_sem=self.sems[2 * t + 1].at[half, w, j],
            device_id={"dp": flip(self.group, t if half == 0 else self.bits - t)}, device_id_type=MESH)

    def start0(self, w):
        for j in range(self.mates):
            self.copy0(w, j).start()

    def start(self, t, w):
        for j in range(self.mates >> t):
            for half in range(2):
                self.copy(t, half, w, j).start()

    def add0(self, w):
        def body(j, carry):
            self.copy0(w, j).wait_recv()
            mine = self.keep(w, j)
            mine[...] = (mine[...].astype(F32) + self.first[w, j].astype(F32)).astype(BF)
            return carry

        lax.fori_loop(0, self.mates, body, 0)
        self.start(1, w)

    def add(self, t, w, target=None):
        for half in range(2):
            def body(j, carry):
                self.copy(t, half, w, j).wait_recv()
                mine = self.keep(w, self.place(t, half, j, True)).at[:, self.cols[half]]
                value = mine[...].astype(F32) + self.boxes[2 * (t - 1) + half][w, j].astype(F32)
                if target is None:
                    mine[...] = value.astype(BF)
                else:
                    target[:, self.cols[half]] = value.astype(target.dtype)
                return carry

            lax.fori_loop(0, self.mates >> t, body, 0)
        if target is None:
            self.start(t + 1, w)

    def finish(self, count):
        def body(w, carry):
            for j in range(self.mates):
                self.copy0(w, j).wait_send()
            for t in range(1, self.bits):
                for j in range(self.mates >> t):
                    for half in range(2):
                        self.copy(t, half, w, j).wait_send()
            return carry

        lax.fori_loop(0, count, body, 0)


def rope_numpy(length):
    half = HD // 2
    frequency = np.float32(10000.0) ** (-np.arange(half, dtype=np.float32) / np.float32(half))
    angles = np.arange(length, dtype=np.float32)[:, None] * frequency[None, :]
    cosine, sine = np.cos(angles), np.sin(angles)
    return (np.concatenate([cosine, cosine], 1), np.concatenate([-sine, sine], 1))


def column_of(row, target):
    target[...] = jnp.transpose(jnp.broadcast_to(row.astype(F32), (HD, row.shape[1])))


def forward_body(dp, tok, cot, seg, wo, wq, wk, wv, gain, gain2, cosine, sine,
                 a1_out, q_out, k_out, v_out, wo_out, cot_out, p_out, dy_out, a2_out, h_out, ob_out,
                 xs, a1s, qkv, ws, wos, dys, obs, ps, hs, segs,
                 x_ss, x_rs, z_ss, z_rs, d_ss, d_rs, c_ss, y_ss, y_rs, o_ss, o_rs, l_sem, k_sem, b_sem):
    rank, group = lax.axis_index("tensor"), lax.axis_index("dp")
    rows, model = tok.shape
    length, width = q_out.shape
    heads = width // HD
    scale = HD ** (-0.5)
    half_rows = rows // 2
    parts = wo.shape[0]
    mates = parts // 2
    member = lax.rem(group, parts)
    base = group - member
    parity = lax.rem(member, 2)
    pair = lax.div(member, 2)
    partner = flip(group, 0)

    def mate(step):
        return lax.rem(pair + step, mates) * 2 + parity

    first = [local(wo.at[member], wos.at[rank, member], l_sem.at[0]), local(tok, xs.at[rank], l_sem.at[1]), local(cot, dys.at[rank], l_sem.at[2])]
    weights = [local(w, ws.at[i], l_sem.at[3 + i]) for i, w in enumerate((wq, wk, wv))]
    for c in first + weights:
        c.start()
    greet(line_peers(rank) + [{"dp": partner}] + [{"dp": base + mate(s)} for s in range(1, mates)])
    out_gather = LineGather(rank, lambda s, p: wos.at[s, member], 1, z_ss, z_rs)
    gather = LineGather(rank, lambda s, p: xs.at[s, pl.ds(p * half_rows, half_rows)], 2, x_ss, x_rs)

    def near(k, source):
        return pltpu.make_async_remote_copy(
            src_ref=dys.at[source], dst_ref=dys.at[source], send_sem=y_ss.at[k], recv_sem=y_rs.at[k],
            device_id={"tensor": across(rank, k)}, device_id_type=MESH)

    inner = inner_plane(rank)
    attended = LineGather(rank, lambda s, p: obs.at[s, :, pl.ds(pl.multiple_of(p * HD, HD), HD)], heads, o_ss, o_rs)
    first[0].wait()
    out_gather.start(0)
    first[1].wait()
    gather.start(0)
    gather.start(1)
    first[2].wait()
    column_of(seg[...], segs)
    real = segs[pl.ds(pl.multiple_of(rank * rows, rows), rows), :1] >= 0.0
    dys[rank] = jnp.where(real, dys[rank], jnp.zeros((rows, model), BF))
    near(1, rank).start()
    pl.when(inner)(near(3, rank).start)
    keep = [local(dys.at[rank], cot_out, k_sem.at[0])]
    keep[0].start()
    for w in weights:
        w.wait()

    def chunk(source):
        x = xs[source].astype(F32)
        a1s[source] = (x * norm_factor(x) * gain[...].reshape(1, model)).astype(BF)
        where = pl.ds(pl.multiple_of(source * rows, rows), rows)
        for i in range(3):
            product = dot(a1s[source], ws[i])
            for h in range(heads):
                head = product[:, h * HD : (h + 1) * HD]
                if i < 2:
                    head = head * cosine[where, :] + pltpu.roll(head, HD // 2, 1) * sine[where, :]
                qkv[i, where, h * HD : (h + 1) * HD] = head.astype(BF)

    def chunks(i, carry):
        @pl.when(i == 1)
        def _():
            for k in (1, 2, 3):
                out_gather.arrive(k, 0)
            for step in range(1, mates):
                mate_copy(step).start()
            core_copy(0, parity).start()
            for piece in range(2):
                gather.arrive(1, piece)
                gather.arrive(2, piece)

        @pl.when(i == 3)
        def _():
            for step in range(1, mates):
                mate_arrival(step).wait_recv()
                core_copy(step, parity).start()
            for piece in range(2):
                gather.arrive(3, piece)

        chunk(pick(i, [rank, across(rank, 1), across(rank, 2), across(rank, 3)]))
        return carry

    def mate_copy(step):
        return pltpu.make_async_remote_copy(
            src_ref=wos.at[:, member], dst_ref=wos.at[:, member], send_sem=d_ss.at[step], recv_sem=d_rs.at[member],
            device_id={"dp": base + mate(step)}, device_id_type=MESH)

    def mate_arrival(step):
        piece = mate(step)
        return pltpu.make_async_remote_copy(
            src_ref=wos.at[:, piece], dst_ref=wos.at[:, piece], send_sem=d_ss.at[step], recv_sem=d_rs.at[piece],
            device_id={"dp": base + piece}, device_id_type=MESH)

    def core_copy(step, owner):
        piece = lax.rem(pair + step, mates) * 2 + owner
        return pltpu.make_async_remote_copy(
            src_ref=wos.at[:, piece], dst_ref=wos.at[:, piece], send_sem=c_ss.at[step], recv_sem=d_rs.at[piece],
            device_id={"dp": partner}, device_id_type=MESH)

    lax.fori_loop(0, RANKS, chunks, 0)
    keep += [local(a1s, a1_out, k_sem.at[1])] + [local(qkv.at[i], t, k_sem.at[2 + i]) for i, t in enumerate((q_out, k_out, v_out))]
    for c in keep[1:]:
        c.start()

    def head(h, carry):
        cols = pl.ds(pl.multiple_of(h * HD, HD), HD)
        for start in range(0, length, QB):
            extent = start + QB
            scores = dot(qkv[0, start:extent, cols], qkv[1, :extent, cols], ((1,), (1,)))
            row_ids = lax.broadcasted_iota(jnp.int32, (QB, extent), 0) + start
            col_ids = lax.broadcasted_iota(jnp.int32, (QB, extent), 1)
            allowed = (col_ids <= row_ids) & (segs[start:extent, :1] == seg[:, :extent].astype(F32))
            logits = jnp.where(allowed, scores * scale, NEG)
            expo = jnp.exp(logits - jnp.max(logits, axis=-1, keepdims=True))
            probs = (expo * (1.0 / jnp.sum(expo, axis=-1, keepdims=True))).astype(BF)
            ps[h, start:extent, :extent] = probs
            obs[rank, start:extent, cols] = dot(probs, qkv[2, :extent, cols]).astype(BF)
        attended.start(h)
        return carry

    lax.fori_loop(0, heads, head, 0)
    for step in range(mates):
        core_copy(step, 1 - parity).wait_recv()
    more = [local(ps, p_out, k_sem.at[5]), local(wos, wo_out, k_sem.at[6])]
    for c in more:
        c.start()
    keep += more

    def add(source, first=False, last=False):
        def block(b, carry):
            weight = wos[source].reshape(width, model)
            part = dot(obs[source, pl.ds(pl.multiple_of(b * rows, rows), rows), :], weight)
            total = part + (xs[b].astype(F32) if first else hs[b])
            if last:
                @pl.when(b == rank)
                def _():
                    hs[b] = total

            else:
                hs[b] = total
            if last:
                xs[b] = (total * norm_factor(total) * gain2[...].reshape(1, model)).astype(BF)
                local(xs.at[b], a2_out.at[b], b_sem.at[b]).start()
            return carry

        lax.fori_loop(0, RANKS, block, 0)

    add(rank, first=True)
    for piece in range(heads):
        attended.arrive(2, piece)
    for piece in range(heads):
        attended.arrive(1, piece)
    add(across(rank, 2))
    add(across(rank, 1))
    one, three = across(rank, 1), across(rank, 3)
    near(1, one).wait_recv()
    more = [local(dys.at[one], dy_out.at[one], l_sem.at[0])]
    more[0].start()
    inner_copy = local(dys.at[three], dy_out.at[three], l_sem.at[1])

    @pl.when(inner)
    def _():
        near(3, three).wait_recv()
        inner_copy.start()

    for piece in range(heads):
        attended.arrive(3, piece)
    gather.finish()
    add(across(rank, 3), last=True)
    more += [local(hs.at[rank], h_out, l_sem.at[2]),
             local(obs.at[:, pl.ds(pl.multiple_of(rank * rows, rows), rows)], ob_out, l_sem.at[3])]
    for c in more[1:]:
        c.start()
    out_gather.finish()
    for step in range(1, mates):
        mate_copy(step).wait_send()
    for step in range(mates):
        core_copy(step, parity).wait_send()
    attended.finish()
    near(1, rank).wait_send()

    @pl.when(inner)
    def _():
        near(3, rank).wait_send()
        inner_copy.wait()

    for c in keep + more:
        c.wait()
    for b in range(RANKS):
        local(xs.at[b], a2_out.at[b], b_sem.at[b]).wait()


def forward_kernel(dp, tokens, cotangent, segments, w_out, w_query, w_key, w_value, gain, gain2, cosine, sine):
    rows, model = tokens.shape
    width = w_query.shape[1]
    heads = width // HD
    length = RANKS * rows
    parts = min(dp, 8)
    mates = parts // 2
    shape = (RANKS, rows, model)
    shard, wide = jax.ShapeDtypeStruct(shape, BF), jax.ShapeDtypeStruct((length, width), BF)
    outs = pl.pallas_call(
        functools.partial(forward_body, dp),
        in_specs=[ANY, ANY, VM, ANY, ANY, ANY, ANY, VM, VM, VM, VM],
        out_specs=[ANY] * 11,
        out_shape=[shard, wide, wide, wide, jax.ShapeDtypeStruct((RANKS, parts, width // parts, model), BF),
                   jax.ShapeDtypeStruct((rows, model), BF), jax.ShapeDtypeStruct((heads, length, length), BF), shard, shard,
                   jax.ShapeDtypeStruct((rows, model), F32), jax.ShapeDtypeStruct((RANKS, rows, width), BF)],
        scratch_shapes=[
            pltpu.VMEM(shape, BF), pltpu.VMEM(shape, BF), pltpu.VMEM((3, length, width), BF), pltpu.VMEM((3, model, width), BF),
            pltpu.VMEM((RANKS, parts, width // parts, model), BF), pltpu.VMEM(shape, BF), pltpu.VMEM((RANKS, length, width), BF),
            pltpu.VMEM((heads, length, length), BF), pltpu.VMEM(shape, F32), pltpu.VMEM((length, HD), F32),
            *LineGather.sems(2), *LineGather.sems(1), DMA((mates,)), DMA((parts,)), DMA((mates,)),
            DMA((4,)), DMA((4,)), *LineGather.sems(heads), DMA((6,)), DMA((7,)), DMA((RANKS,)),
        ],
        compiler_params=pltpu.CompilerParams(collective_id=1, has_side_effects=True, vmem_limit_bytes=62 << 20),
        name="forward_gather",
    )(tokens, cotangent, segments, w_out.reshape(parts, width // parts, model), w_query, w_key, w_value, gain, gain2, cosine, sine)
    a1_all, query, key, value, w_out_all, cot_own, probs, dy, a2, hidden, attended = outs
    return a1_all, query, key, value, w_out_all.reshape(RANKS, width, model), cot_own, probs, dy, a2, hidden, attended


def pick(step, choices):
    value = choices[-1]
    for i in range(len(choices) - 1):
        value = jnp.where(step == i, choices[i], value)
    return value


FT = 768
WB = 384


def mlp_body(a2, dy, wg, wu, wd, hid, cot, gran, gain,
             g_out, down_out, dh_out, gain_out,
             lefts, acts, ws, parts, inbox, stage, downs, hs, cots, total, gains, r_ss, r_rs, y_ss, y_rs, l_sem, s_sem, d_sem):
    rank = lax.axis_index("tensor")
    rows, model = cot.shape
    width = wg.shape[1]
    per, share = stage.shape[1], stage.shape[2]
    end = (rank == 0) | (rank == 3)

    def part(source):
        return pl.ds(pl.multiple_of(source * rows, rows), rows)

    def dy_load(k, sem):
        return local(dy.at[across(rank, k)], lefts.at[1, part(across(rank, k))], l_sem.at[sem])

    inner = inner_plane(rank)
    half = rows // 2

    def piece_of(source, piece):
        return pl.ds(pl.multiple_of(source * rows + piece * half, half), half)

    def hand(slot, shard, piece, k, kept=True):
        where = piece_of(across(rank, shard), piece)
        source = dy.at[across(rank, shard), pl.ds(piece * half, half)] if kept else lefts.at[1, where]
        return pltpu.make_async_remote_copy(
            src_ref=source, dst_ref=lefts.at[1, where], send_sem=y_ss.at[slot, piece], recv_sem=y_rs.at[slot, piece],
            device_id={"tensor": across(rank, k)}, device_id_type=MESH)

    def mid(piece):
        return hand(0, 1, piece, 3)

    def second(piece):
        return hand(1, 3, piece, 1)

    def third(piece):
        return hand(2, 2, piece, 1, False)

    def arrived(slot, shard, piece):
        where = piece_of(across(rank, shard), piece)
        return pltpu.make_async_remote_copy(
            src_ref=lefts.at[1, where], dst_ref=lefts.at[1, where], send_sem=y_ss.at[slot, piece], recv_sem=y_rs.at[slot, piece],
            device_id={"tensor": across(rank, 1)}, device_id_type=MESH)

    own = local(cot, lefts.at[1, part(rank)], l_sem.at[7])
    own.start()
    loads = [local(wg, ws.at[0], l_sem.at[0]), local(a2, lefts.at[0], l_sem.at[1]), local(wu, ws.at[1], l_sem.at[2]),
             dy_load(1, 3), local(wd, ws.at[2], l_sem.at[4])]
    inner_load = dy_load(3, 8)
    pl.when(inner)(inner_load.start)
    late = [local(hid, hs, l_sem.at[5]), local(cot, cots, l_sem.at[6])]
    for c in loads + late:
        c.start()
    greet(line_peers(rank))

    @pl.when(inner)
    def _():
        mid(0).start()
        second(0).start()
        mid(1).start()
        second(1).start()

    scatter = LineScatter(rank, parts, inbox, r_ss, r_rs, 4)
    planes = [rank] + [across(rank, k) for k in (1, 2, 3)]
    kinds = [jnp.where(end, a, b) for a, b in zip((1, 2, 0, 3), (3, 1, 2, 0))]
    order = [jnp.where(end, planes[a], planes[b]) for a, b in zip((1, 2, 0, 3), (3, 1, 2, 0))]
    limit = FF // 8 * lax.shift_left(1, gran[0] - 1) - rank * width

    def step(i, carry):
        where = pl.ds(pl.multiple_of(pick(i, order) * rows, rows), rows)

        def tile(t, inner_carry):
            cols = pl.ds(pl.multiple_of(t * FT, FT), FT)

            @pl.when((i == 0) & (t == 0))
            def _():
                loads[0].wait()
                loads[1].wait()

            gate = dot(lefts[0, where, :], ws[0, :, cols])

            @pl.when((i == 0) & (t == 0))
            def _():
                loads[2].wait()

            up = dot(lefts[0, where, :], ws[1, :, cols])

            @pl.when((i == 0) & (t == 0))
            def _():
                loads[3].wait()
                pl.when(inner)(inner_load.wait)
                own.wait()
                loads[4].wait()

            @pl.when((i == 1) & (t == 0) & end)
            def _():
                for piece in range(2):
                    arrived(1, 2, piece).wait_recv()

            @pl.when((i == 3) & (t == 0) & end)
            def _():
                for piece in range(2):
                    arrived(2, 3, piece).wait_recv()

            dz = dot(lefts[1, where, :], ws[2, cols, :], ((1,), (1,)))
            unit = lax.broadcasted_iota(jnp.int32, gate.shape, 1) + t * FT
            mask = unit < limit
            sigma = jax.nn.sigmoid(gate)
            active = jnp.where(mask, gate * sigma, 0.0)
            acts[2, where, cols] = (active * up).astype(BF)
            acts[0, where, cols] = jnp.where(mask, dz * up * sigma * (1.0 + gate * (1.0 - sigma)), 0.0).astype(BF)
            acts[1, where, cols] = (dz * active).astype(BF)
            return inner_carry

        lax.fori_loop(0, width // FT, tile, 0)

        def back(t, inner_carry):
            cols = pl.ds(pl.multiple_of(t * FT, FT), FT)
            parts[pick(i, kinds), :, cols] = (
                dot(acts[0, where, :], ws[0, cols, :], ((1,), (1,))) + dot(acts[1, where, :], ws[1, cols, :], ((1,), (1,)))
            ).astype(BF)
            return inner_carry

        lax.fori_loop(0, model // FT, back, 0)

        @pl.when(inner & (i == 0))
        def _():
            scatter.send_far()
            arrived(0, 2, 0).wait_recv()
            third(0).start()

        @pl.when(inner & (i == 1))
        def _():
            arrived(0, 2, 1).wait_recv()
            third(1).start()
            scatter.send_near()

        pl.when(end & (i == 0))(scatter.send_near)
        pl.when(end & (i == 1))(scatter.send_two_end)
        pl.when(end & (i == 3))(scatter.send_far)

        @pl.when((end & (i == 0)) | (inner & (i == 1)))
        def _():
            downs[1] = dot(acts[2, where, :], ws[2]).astype(BF)

        return carry

    lax.fori_loop(0, 4, step, 0)
    blocks = model // WB

    def put(i, slot):
        w, b = lax.div(i, blocks), lax.rem(i, blocks)
        return local(stage.at[slot], g_out.at[w, pl.ds(b * per, per)], s_sem.at[slot])

    def grads(i, carry):
        slot = lax.rem(i, 2)
        w, b = lax.div(i, blocks), lax.rem(i, blocks)
        left = lax.div(w, 2)
        cols = pl.ds(pl.multiple_of(b * WB, WB), WB)
        value = dot(lefts[left, :, cols], acts[w], ((0,), (0,)))
        pl.when(i >= 2)(lambda: put(i - 2, slot).wait())
        low = value.astype(BF)
        for p in range(per):
            stage[slot, p] = low[p * share : (p + 1) * share]
        put(i, slot).start()
        for piece in range(4):
            pl.when(i == 3 * blocks - 7 + 2 * piece)(lambda: scatter.send_two_inner([piece]))
        return carry

    lax.fori_loop(0, 3 * blocks, grads, 0)

    def down(i, carry):
        kind = jnp.where(i == 2, 0, i + 2)
        where = part(pick(i, [planes[2], planes[3], rank]))
        downs[kind] = dot(acts[2, where, :], ws[2]).astype(BF)
        return carry

    lax.fori_loop(0, 3, down, 0)
    keep = local(downs, down_out, l_sem.at[0])
    keep.start()
    for c in late:
        c.wait()

    def dh_copy(piece, where):
        return local(total.at[where], dh_out.at[where], d_sem.at[piece])

    def finish_rows(piece, where):
        values, gradient = hs[where], total[where]
        back_rows, row = norm_back(values, norm_factor(values), gain[...].reshape(1, model), gradient)
        total[where] = cots[where].astype(F32) + back_rows
        row = row.reshape(1, model)
        gains[...] = row if piece == 0 else gains[...] + row
        dh_copy(piece, where).start()

    scatter.total(total, finish_rows)
    last = [local(gains, gain_out, l_sem.at[2])]
    for c in last:
        c.start()
    scatter.finish()

    @pl.when(inner)
    def _():
        for piece in range(2):
            mid(piece).wait_send()
            second(piece).wait_send()
            third(piece).wait_send()

    put(3 * blocks - 2, 0).wait()
    put(3 * blocks - 1, 1).wait()
    for c in last + [keep]:
        c.wait()
    for piece in range(4):
        dh_copy(piece, scatter.where(piece)).wait()


def mlp_kernel(dp, a2, dy, w_gate, w_up, w_down, hidden_own, cot_own, granularity, gain):
    rows, model = cot_own.shape
    width = w_gate.shape[1]
    share = model // dp
    shard = (RANKS, rows, model)
    return pl.pallas_call(
        mlp_body,
        in_specs=[ANY] * 7 + [pl.BlockSpec(memory_space=pltpu.SMEM), VM],
        out_specs=[ANY] * 4,
        out_shape=[jax.ShapeDtypeStruct((3, dp, share, width), BF), jax.ShapeDtypeStruct(shard, BF),
                   jax.ShapeDtypeStruct((rows, model), F32), jax.ShapeDtypeStruct((1, model), F32)],
        scratch_shapes=[
            pltpu.VMEM((2, RANKS * rows, model), BF), pltpu.VMEM((3, RANKS * rows, width), BF), pltpu.VMEM((3, model, width), BF),
            pltpu.VMEM(shard, BF), pltpu.VMEM(shard, BF), pltpu.VMEM((2, WB // share, share, width), BF), pltpu.VMEM(shard, BF),
            pltpu.VMEM((rows, model), F32), pltpu.VMEM((rows, model), BF), pltpu.VMEM((rows, model), F32), pltpu.VMEM((1, model), F32),
            *LineScatter.sems(4), DMA((3, 2)), DMA((3, 2)), DMA((9,)), DMA((2,)), DMA((4,)),
        ],
        compiler_params=pltpu.CompilerParams(collective_id=3, has_side_effects=True, vmem_limit_bytes=63 << 20),
        name="mlp_scatter",
    )(a2.reshape(-1, model), dy, w_gate, w_up, w_down, hidden_own, cot_own, granularity, gain)


def attention_back_body(dp, dh, wo_all, downs, grads, q, k, v, p_all, hid, wq, wk, wv, cosine, sine,
                        out_out, dq_out, dk_out, dv_out, gf_out, da_out,
                        dhs, low, wos, parts, inbox, dobs, dos, qkv, ps, ds, dqkv, hs, outs, kept, finals, ws, shares, *rest):
    rank, group = lax.axis_index("tensor"), lax.axis_index("dp")
    rounds = 2 * (dp.bit_length() - 1)
    first, boxes, rest = rest[0], rest[1 : rounds - 1], rest[rounds - 1 :]
    sems, (r_ss, r_rs, a_ss, a_rs, l_sem, p_sem, f_sem) = rest[:rounds], rest[rounds:]
    rows, model = dh.shape
    length, width = q.shape
    heads, half, scale = width // HD, HD // 2, HD ** (-0.5)
    count = grads.shape[0]
    parity = lax.rem(group, 2)
    loads = [local(downs, parts, l_sem.at[2]), local(dh, dhs, l_sem.at[0]), local(wo_all, wos, l_sem.at[1])]
    owns = [local(grads.at[w, :, parity], kept.at[w], f_sem.at[w]) for w in range(count)]
    late = [local(t, qkv.at[i], l_sem.at[3 + i]) for i, t in enumerate((q, k, v))] + [local(hid, hs, l_sem.at[6])]
    late += [local(t, ws.at[i], l_sem.at[7 + i]) for i, t in enumerate((wq, wk, wv))]
    for c in loads + owns + late:
        c.start()

    def probs(h):
        return local(p_all.at[h], ps.at[lax.rem(h, 2)], p_sem.at[lax.rem(h, 2)])

    probs(0).start()
    probs(1).start()
    reduce = GroupReduce(
        group, dp, lambda w, d: grads.at[w, lax.div(d, 2), lax.rem(d, 2)], lambda w, j: kept.at[w, j], first, boxes, model // 2, sems)
    greet(line_peers(rank) + reduce.peers())
    for w in range(count):
        reduce.start0(w)
    scatter = LineScatter(rank, parts, inbox, r_ss, r_rs, 2)
    loads[0].wait()
    scatter.send_far([0])

    def exchange(k, source):
        where = pl.ds(pl.multiple_of(source * rows, rows), rows)
        return pltpu.make_async_remote_copy(
            src_ref=dobs.at[k - 1], dst_ref=dos.at[where], send_sem=a_ss.at[k], recv_sem=a_rs.at[source],
            device_id={"tensor": across(rank, k)}, device_id_type=MESH)

    loads[1].wait()
    low[...] = dhs[...].astype(BF)
    loads[2].wait()
    for k in (3, 2, 1):
        dobs[k - 1] = dot(low[...], wos[across(rank, k)], ((1,), (1,))).astype(BF)
        exchange(k, rank).start()
    scatter.send_far([1])
    scatter.send_two_end()
    scatter.send_near()
    dos[pl.ds(pl.multiple_of(rank * rows, rows), rows), :] = dot(low[...], wos[rank], ((1,), (1,))).astype(BF)
    for c in owns:
        c.wait()

    def fold(w, carry):
        reduce.add0(w)
        return carry

    lax.fori_loop(0, count, fold, 0)
    for c in late:
        c.wait()
    scatter.send_two_inner([0])
    for k in (3, 2, 1):
        exchange(k, across(rank, k)).wait_recv()

    def head(h, carry):
        cols = pl.ds(pl.multiple_of(h * HD, HD), HD)
        slot = lax.rem(h, 2)
        probs(h).wait()

        def unrope(grad, start):
            where = slice(start, start + QB)
            return (grad * cosine[where, :] - pltpu.roll(grad, half, 1) * sine[where, :]).astype(BF)

        for start in range(0, length, QB):
            extent = start + QB
            where = slice(start, extent)
            grad_p = dot(dos[where, cols], qkv[2, :extent, cols], ((1,), (1,)))
            p = ps[slot, where, :extent].astype(F32)
            weighted = p * grad_p
            delta = jnp.sum(weighted, axis=-1, keepdims=True)
            ds[where, :extent] = ((weighted - p * delta) * scale).astype(BF)
            dqkv[0, where, cols] = unrope(dot(ds[where, :extent], qkv[1, :extent, cols]), start)
        for start in range(0, length, QB):
            where = slice(start, start + QB)
            dqkv[1, where, cols] = unrope(dot(ds[start:, where], qkv[0, start:, cols], ((0,), (0,))), start)
            dqkv[2, where, cols] = dot(ps[slot, start:, where], dos[start:, cols], ((0,), (0,))).astype(BF)
        pl.when(h + 2 < heads)(lambda: probs(h + 2).start())
        pl.when(h == 0)(lambda: scatter.send_two_inner([1]))
        return carry

    lax.fori_loop(0, heads, head, 0)
    done = [local(dqkv.at[i], t, l_sem.at[i]) for i, t in enumerate((dq_out, dk_out, dv_out))]
    for c in done:
        c.start()

    def share_of(k, carry):
        where = pl.ds(pl.multiple_of(pick(k, [rank] + [across(rank, i) for i in (1, 2, 3)]) * rows, rows), rows)
        value = dot(dqkv[0, where, :], ws[0], ((1,), (1,)))
        for s in (1, 2):
            value += dot(dqkv[s, where, :], ws[s], ((1,), (1,)))
        shares[k] = value.astype(BF)
        return carry

    reduce.add(1, 0)
    lax.fori_loop(0, RANKS, share_of, 0)
    done.append(local(shares, da_out, l_sem.at[4]))
    done[-1].start()
    reduce.add(1, 1)
    reduce.add(1, 2)
    for t in range(2, reduce.bits - 1):
        for w in range(count):
            reduce.add(t, w)

    def put(w):
        return local(finals.at[w], gf_out.at[w], f_sem.at[w])

    for w in range(count):
        reduce.add(reduce.bits - 1, w, finals.at[w])
        put(w).start()

    def out_rows(piece, where):
        outs[where] = (hs[where] + dhs[where]).astype(BF)

    scatter.total(dhs, out_rows)
    last = local(outs, out_out, l_sem.at[3])
    last.start()
    scatter.finish()
    for k in (1, 2, 3):
        exchange(k, rank).wait_send()
    reduce.finish(count)
    for w in range(count):
        put(w).wait()
    for c in done + [last]:
        c.wait()


def attention_back_kernel(dp, grad_hidden, w_out_all, down_parts, grads_ff, query, key, value, probs_low, hidden_own, w_query, w_key, w_value, cosine, sine):
    rows, model = grad_hidden.shape
    length, width = query.shape
    count, _, share, columns = grads_ff.shape
    mates = dp // 2
    shard = (RANKS, rows, model)
    heads = jax.ShapeDtypeStruct((length, width), BF)
    return pl.pallas_call(
        functools.partial(attention_back_body, dp),
        in_specs=[ANY] * 12 + [VM, VM],
        out_specs=[ANY] * 6,
        out_shape=[jax.ShapeDtypeStruct((rows, model), BF), heads, heads, heads, jax.ShapeDtypeStruct((count, share, columns), BF),
                   jax.ShapeDtypeStruct(shard, BF)],
        scratch_shapes=[
            pltpu.VMEM((rows, model), F32), pltpu.VMEM((rows, model), BF), pltpu.VMEM((RANKS, width, model), BF),
            pltpu.VMEM(shard, BF), pltpu.VMEM(shard, BF), pltpu.VMEM((3, rows, width), BF), pltpu.VMEM((length, width), BF),
            pltpu.VMEM((3, length, width), BF), pltpu.VMEM((2, length, length), BF), pltpu.VMEM((length, length), BF),
            pltpu.VMEM((3, length, width), BF), pltpu.VMEM((rows, model), F32), pltpu.VMEM((rows, model), BF),
            pltpu.VMEM((count, mates, share, columns), BF), pltpu.VMEM((count, share, columns), BF),
            pltpu.VMEM((3, model, width), BF), pltpu.VMEM(shard, BF),
            *GroupReduce.box_shapes(dp, count, share, columns, columns // 2), *GroupReduce.sem_shapes(dp, count),
            *LineScatter.sems(2), DMA((4,)), DMA((RANKS,)), DMA((10,)), DMA((2,)), DMA((count,)),
        ],
        compiler_params=pltpu.CompilerParams(collective_id=4, has_side_effects=True, vmem_limit_bytes=63 << 20),
        name="attention_back",
    )(grad_hidden, w_out_all, down_parts, grads_ff.reshape(count, mates, 2, share, columns),
      query, key, value, probs_low, hidden_own, w_query, w_key, w_value, cosine, sine)


def input_back_body(dp, dq, dk, dv, a1, da, tok, dh, ob, gain, gain2,
                    dx_out, gains_out, gqkv_out, gout_out,
                    dqkv, a1s, xs, dhs, low, obs, parts, inbox, g1, g2, f1, f2, f2_low, box2, f3, gbuf, gbox, total, dxs, *rest):
    rank, group = lax.axis_index("tensor"), lax.axis_index("dp")
    bits = dp.bit_length() - 1
    boxes = [rest[: 2 * bits - 1], rest[2 * bits - 1 : 4 * bits - 2]]
    rest = rest[4 * bits - 2 :]
    sems = [rest[: 2 * bits], rest[2 * bits : 4 * bits]]
    r_ss, r_rs, z_ss, z_rs, g_ss, g_rs, l_sem = rest[4 * bits :]
    rows, model = tok.shape
    width = dq.shape[1]
    share = g1.shape[1]
    per = WB // share
    parity = lax.rem(group, 2)
    loads = [local(da, parts, l_sem.at[3])]
    late = [local(a1, a1s, l_sem.at[8]), local(dh, dhs, l_sem.at[6]), local(ob, obs, l_sem.at[7]), local(tok, xs, l_sem.at[9])]
    late += [local(t, dqkv.at[i], l_sem.at[i]) for i, t in enumerate((dq, dk, dv))]
    for c in loads + late:
        c.start()
    scatter = LineScatter(rank, parts, inbox, r_ss, r_rs, 2)
    mixed = GroupReduce(group, dp, lambda w, d: g1.at[d], lambda w, j: g1.at[2 * j + parity], boxes[0][0], boxes[0][1:], f1.shape[1] // 256 * 128, sems[0])
    output = GroupReduce(group, dp, lambda w, d: g2.at[d], lambda w, j: g2.at[2 * j + parity], boxes[1][0], boxes[1][1:], f2.shape[1] // 256 * 128, sems[1])
    greet(line_peers(rank) + mixed.peers())
    for c in loads:
        c.wait()
    scatter.send_far()
    scatter.send_two_end()
    scatter.send_near()
    late[0].wait()

    def gain_rows(k, carry):
        where = pl.ds(pl.multiple_of(pick(k, [rank] + [across(rank, i) for i in (1, 2, 3)]) * rows, rows), rows)
        row = jnp.sum(parts[k].astype(F32) * a1s[where, :].astype(F32), axis=0, keepdims=True)
        gbuf[0, 0:1, :] = jnp.where(k == 0, row, gbuf[0, 0:1, :] + row)
        return carry

    gbuf[0, 0:1, :] = jnp.zeros((1, model), F32)
    lax.fori_loop(0, RANKS, gain_rows, 0)
    gbuf[0, 0:1, :] = gbuf[0, 0:1, :] / gain[...].reshape(1, model)
    gbuf[0, 1:2, :] = gain2[...]

    def swap(t):
        return pltpu.make_async_remote_copy(
            src_ref=gbuf.at[t], dst_ref=gbox.at[t], send_sem=g_ss.at[t], recv_sem=g_rs.at[t], device_id={"dp": flip(group, t)}, device_id_type=MESH)

    def advance(t):
        swap(t).wait_recv()
        gbuf[t + 1] = gbuf[t] + gbox[t]
        if t + 1 < bits:
            swap(t + 1).start()

    def share_gains(k, source):
        return pltpu.make_async_remote_copy(
            src_ref=gbuf.at[bits], dst_ref=gbox.at[bits + source], send_sem=g_ss.at[bits + k], recv_sem=g_rs.at[bits + source],
            device_id={"tensor": across(rank, k)}, device_id_type=MESH)

    swap(0).start()
    for c in late[1:]:
        c.wait()
    low[...] = dhs[...].astype(BF)

    def out_block(b, carry):
        cols = pl.ds(pl.multiple_of(b * WB, WB), WB)
        for r in range(RANKS):
            value = dot(low[:, cols], obs[r], ((0,), (0,))).astype(BF)
            for p in range(per):
                g2[b * per + p, :, r * width : (r + 1) * width] = value[p * share : (p + 1) * share]
        return carry

    lax.fori_loop(0, model // WB, out_block, 0)
    advance(0)
    output.start0(0)

    def mixed_block(b, carry):
        cols = pl.ds(pl.multiple_of(b * WB, WB), WB)
        for s in range(3):
            value = dot(a1s[:, cols], dqkv[s], ((0,), (0,))).astype(BF)
            for p in range(per):
                g1[b * per + p, :, s * width : (s + 1) * width] = value[p * share : (p + 1) * share]
        return carry

    lax.fori_loop(0, model // WB, mixed_block, 0)
    for t in range(1, bits):
        advance(t)
    for k in (1, 2, 3):
        share_gains(k, rank).start()
    gbox[bits + rank] = gbuf[bits]
    mixed.start0(0)
    output.add0(0)
    mixed.add0(0)
    scatter.send_two_inner()
    for t in range(1, bits - 1):
        output.add(t, 0)
        mixed.add(t, 0)
    output.add(bits - 1, 0, f2)
    ends = LineScatter(rank, f2_low, box2, z_ss, z_rs, 1)
    for k in range(4):
        column = pl.ds(pl.multiple_of(across(rank, k) * width, HD), width)
        f2_low[k] = f2[:, column].astype(BF)
    ends.send_far()
    ends.send_two_end()
    ends.send_near()
    mixed.add(bits - 1, 0, f1)
    done = [local(f1, gqkv_out, l_sem.at[0])]
    done[0].start()
    scatter.total(total)
    values, gradient = xs[...].astype(F32), total[...]
    back_rows, _ = norm_back(values, norm_factor(values), gain[...].reshape(1, model), gradient)
    dxs[...] = (dhs[...] + back_rows).astype(BF)
    done.append(local(dxs, dx_out, l_sem.at[1]))
    done[1].start()
    for k in (1, 2, 3):
        share_gains(k, across(rank, k)).wait_recv()
    for t in range(bits):
        swap(t).wait_send()
    gbuf[0] = ((gbox[bits] + gbox[bits + 1]) + gbox[bits + 2]) + gbox[bits + 3]
    done.append(local(gbuf.at[0], gains_out, l_sem.at[2]))
    done[2].start()
    ends.send_two_inner()
    ends.total(f3)
    done.append(local(f3, gout_out, l_sem.at[3]))
    done[3].start()
    scatter.finish()
    ends.finish()
    mixed.finish(1)
    output.finish(1)
    for k in (1, 2, 3):
        share_gains(k, rank).wait_send()
    for c in done:
        c.wait()


def input_back_kernel(dp, grad_q, grad_k, grad_v, a1_all, grad_one, tokens, grad_hidden, attended_own, gain, gain_two):
    rows, model = tokens.shape
    length, width = grad_q.shape
    share = model // dp
    bits = dp.bit_length() - 1
    shard = (RANKS, rows, model)
    wide = (3 * width, RANKS * width)
    splits = [w // 256 * 128 for w in wide]
    return pl.pallas_call(
        functools.partial(input_back_body, dp),
        in_specs=[ANY] * 8 + [VM, VM],
        out_specs=[ANY] * 4,
        out_shape=[jax.ShapeDtypeStruct((rows, model), BF), jax.ShapeDtypeStruct((2, model), F32),
                   jax.ShapeDtypeStruct((share, wide[0]), F32), jax.ShapeDtypeStruct((share, width), F32)],
        scratch_shapes=[
            pltpu.VMEM((3, length, width), BF), pltpu.VMEM((length, model), BF),
            pltpu.VMEM((rows, model), BF), pltpu.VMEM((rows, model), F32), pltpu.VMEM((rows, model), BF), pltpu.VMEM((RANKS, rows, width), BF),
            pltpu.VMEM(shard, BF), pltpu.VMEM(shard, BF),
            pltpu.VMEM((dp, share, wide[0]), BF), pltpu.VMEM((dp, share, wide[1]), BF),
            pltpu.VMEM((share, wide[0]), F32), pltpu.VMEM((share, wide[1]), F32),
            pltpu.VMEM((RANKS, share, width), BF), pltpu.VMEM((RANKS, share, width), BF), pltpu.VMEM((share, width), F32),
            pltpu.VMEM((bits + 1, 2, model), F32), pltpu.VMEM((bits + RANKS, 2, model), F32),
            pltpu.VMEM((rows, model), F32), pltpu.VMEM((rows, model), BF),
            *GroupReduce.box_shapes(dp, 1, share, wide[0], splits[0]), *GroupReduce.box_shapes(dp, 1, share, wide[1], splits[1]),
            *GroupReduce.sem_shapes(dp, 1), *GroupReduce.sem_shapes(dp, 1),
            *LineScatter.sems(2), *LineScatter.sems(1), DMA((bits + RANKS,)), DMA((bits + RANKS,)), DMA((10,)),
        ],
        compiler_params=pltpu.CompilerParams(collective_id=5, has_side_effects=True, vmem_limit_bytes=63 << 20),
        name="input_back",
    )(grad_q, grad_k, grad_v, a1_all.reshape(length, model), grad_one, tokens, grad_hidden, attended_own, gain, gain_two)


def finish_body(output, dx, gains, mixed, out_t, ff,
                output_out, dx_out, gain1_out, gain2_out, q_out, k_out, v_out, wo_out, gate_out, up_out, down_out,
                b0, b1, gs, g1, g2, ms, ot, fs, gate, up, down, i_sem, o_sem):
    width = q_out.shape[1]
    loads = [local(s, t, i_sem.at[i]) for i, (s, t) in enumerate(
        ((ff.at[2], fs.at[2]), (ff.at[0], fs.at[0]), (ff.at[1], fs.at[1]), (mixed, ms), (output, b0), (dx, b1), (out_t, ot), (gains, gs)))]
    for c in loads:
        c.start()
    sent = []

    def put(source, target):
        sent.append(local(source, target, o_sem.at[len(sent)]))
        sent[-1].start()

    loads[1].wait()
    gate[...] = fs[0].astype(F32)
    put(gate, gate_out)
    loads[2].wait()
    up[...] = fs[1].astype(F32)
    put(up, up_out)
    loads[4].wait()
    put(b0, output_out)
    loads[5].wait()
    put(b1, dx_out)
    loads[3].wait()
    for i, target in enumerate((q_out, k_out, v_out)):
        put(ms.at[:, pl.ds(i * width, width)], target)
    loads[0].wait()
    down[...] = fs[2].astype(F32)
    put(down, down_out)
    loads[6].wait()
    put(ot, wo_out)
    loads[7].wait()
    g1[...] = gs[0]
    put(g1, gain1_out)
    g2[...] = gs[1]
    put(g2, gain2_out)
    for c in sent:
        c.wait()


def finish_kernel(output, dx, gains, mixed, out_t, ff):
    rows, model = output.shape
    share, width = out_t.shape
    columns = ff.shape[2]
    gain, head, wide = ((model,), F32), ((share, width), F32), ((share, columns), F32)
    outs = [((rows, model), BF), ((rows, model), BF), gain, gain, head, head, head, head, wide, wide, wide]
    return pl.pallas_call(
        finish_body,
        in_specs=[ANY] * 6,
        out_specs=[ANY] * 11,
        out_shape=[jax.ShapeDtypeStruct(*o) for o in outs],
        scratch_shapes=[
            pltpu.VMEM((rows, model), BF), pltpu.VMEM((rows, model), BF), pltpu.VMEM((2, model), F32), pltpu.VMEM((model,), F32), pltpu.VMEM((model,), F32),
            pltpu.VMEM((share, 3 * width), F32), pltpu.VMEM((share, width), F32),
            pltpu.VMEM((3, share, columns), BF), pltpu.VMEM((share, columns), F32), pltpu.VMEM((share, columns), F32), pltpu.VMEM((share, columns), F32),
            DMA((8,)), DMA((11,)),
        ],
        compiler_params=pltpu.CompilerParams(vmem_limit_bytes=63 << 20),
        name="finish",
    )(output, dx, gains, mixed, out_t, ff)


def on_device(tokens, segments, granularity, norm1_gain, norm2_gain, w_query, w_key, w_value, w_out, w_gate, w_up, w_down, cotangent):
    length = segments.shape[1]
    cosine, sine = (jnp.asarray(t) for t in rope_numpy(length))
    dp = lax.axis_size("dp")
    a1_all, query_rot, key_rot, value_low, w_out_all, cot_own, probs_low, grad_rows, rows_two, hidden_own, attended_own = forward_kernel(
        dp, tokens, cotangent, segments, w_out, w_query, w_key, w_value, norm1_gain, norm2_gain, cosine, sine
    )
    grads_ff, down_parts, grad_hidden, gain_two = mlp_kernel(
        dp, rows_two, grad_rows, w_gate, w_up, w_down, hidden_own, cot_own, granularity, norm2_gain
    )
    output, grad_q, grad_k, grad_v, own_ff, grad_one = attention_back_kernel(
        dp, grad_hidden, w_out_all, down_parts, grads_ff, query_rot, key_rot, value_low, probs_low, hidden_own, w_query, w_key, w_value, cosine, sine
    )
    grad_tokens, gains, own_qkv, own_out = input_back_kernel(
        dp, grad_q, grad_k, grad_v, a1_all, grad_one, tokens, grad_hidden, attended_own, norm1_gain, gain_two
    )
    outs = finish_kernel(output, grad_tokens, gains, own_qkv, own_out, own_ff)
    return tuple(o.T if i in (7, 10) else o for i, o in enumerate(outs))


def solution(mesh):
    in_specs = (
        P(("dp", "tensor"), None), P("dp", None), P("dp"), P(), P(),
        P(None, "tensor"), P(None, "tensor"), P(None, "tensor"), P("tensor", None),
        P(None, "tensor"), P(None, "tensor"), P("tensor", None), P(("dp", "tensor"), None),
    )
    out_specs = (
        P(("dp", "tensor"), None), P(("dp", "tensor"), None), P(), P(),
        P("dp", "tensor"), P("dp", "tensor"), P("dp", "tensor"), P("tensor", "dp"),
        P("dp", "tensor"), P("dp", "tensor"), P("tensor", "dp"),
    )
    return jax.shard_map(on_device, mesh=mesh, in_specs=in_specs, out_specs=out_specs, check_vma=False)
```
